128 devices in a mesh: gx: 8 (over x, core), gy: 4 (over y), gz: 4 (over z).
Axes of the slice: x: 4, y: 4, z: 4, core: 2. Of those that a mesh axis runs over, the one named last changes fastest.
Arguments:
- start_block: float32 [16, 32, 64, 512], P(None, 'gx', 'gy', 'gz')
- basis: bfloat16 [256, 32, 64, 512], P(None, 'gx', 'gy', 'gz')
- trans_x: float32 [32, 64, 512], P('gx', 'gy', 'gz'), may hold values from 0.05 to 1
- trans_y: float32 [32, 64, 512], P('gx', 'gy', 'gz'), may hold values from 0.05 to 1
- trans_z: float32 [32, 64, 512], P('gx', 'gy', 'gz'), may hold values from 0.05 to 1
- pore_volume: float32 [32, 64, 512], P('gx', 'gy', 'gz'), may hold values from 0.5 to 2
- shift_table: float32 [16], replicated, may hold values from 0.5 to 4
- shift_index: int32 [1], replicated, may hold values from 0 to 15
- fault_send: int32 [128, 128, 32], P(('gx', 'gy', 'gz')), may hold values from 0 to 8191
- fault_recv: int32 [128, 128, 32], P(('gx', 'gy', 'gz')), may hold values from 0 to 8191
- fault_trans: float32 [128, 128, 32], P(('gx', 'gy', 'gz')), may hold values from 0.05 to 0.5
- well_cells: int32 [64], replicated, may hold values from 0 to 1048575
Outputs:
- new_block: float32 [16, 32, 64, 512], P(None, 'gx', 'gy', 'gz')
- first_coeffs: float32 [256, 16], replicated
- coeffs: float32 [256, 16], replicated
- well_resp: float32 [64, 16], replicated
The draws below stay inside these ranges and needn't reach their ends.
Inputs may be any that keep to these rules, and one draw needn't show every extreme that they name: fault_send[d, p, s] is a local cell number on device d; the value of that cell feeds a connection into device p. fault_recv[d, p, s] is a local cell number on device d. `well_cells`: flat cell index, last dimension fastest.
All inputs are finite; a program needn't handle non-finite values.
Results may differ from the reference program's by a relative error of at most 0.0065.
Values sent between devices are 32-bit elements; how exact they have to be, the bound alone decides.
A program may use at most 128 MiB of HBM per device.

```python
import math
import jax
import jax.numpy as jnp
from jax import lax

CX = 4
CY = 16
CZ = 128
SLOTS = 32
COLS = 16
BASIS = 256
WELLS = 64
TERMS = 8
SHIFTS = 16
NX = 32
NY = 64
NZ = 512
N_GX = 8
N_GY = 4
N_GZ = 4
DEVICES = 128


def mode_field(index):
    freq_x = (index % 4).astype(jnp.float32)
    freq_y = (index // 4 % 4).astype(jnp.float32)
    freq_z = (index // 16).astype(jnp.float32)
    pos_x = lax.broadcasted_iota(jnp.int32, (1, NX, 1, 1), 1).astype(jnp.float32)
    pos_y = lax.broadcasted_iota(jnp.int32, (1, 1, NY, 1), 2).astype(jnp.float32)
    pos_z = lax.broadcasted_iota(jnp.int32, (1, 1, 1, NZ), 3).astype(jnp.float32)
    root_two = math.sqrt(2.0)
    along_x = jnp.cos(math.pi * (pos_x + 0.5) * freq_x / NX) * jnp.where(freq_x > 0.0, root_two, 1.0)
    along_y = jnp.cos(math.pi * (pos_y + 0.5) * freq_y / NY) * jnp.where(freq_y > 0.0, root_two, 1.0)
    along_z = jnp.cos(math.pi * (pos_z + 0.5) * freq_z / NZ) * jnp.where(freq_z > 0.0, root_two, 1.0)
    return along_x * along_y * along_z


def draw_basis(key, part):
    column_index = lax.broadcasted_iota(jnp.int32, (BASIS, 1, 1, 1), 0)
    values = jax.random.normal(key, (BASIS, NX, NY, NZ), jnp.float32)
    gains = jax.random.uniform(jax.random.fold_in(key, 11), (BASIS, 1, 1, 1), jnp.float32, 0.8, 1.2)
    mixed = 0.6 * values + 0.8 * mode_field(column_index)
    return (mixed * gains * (1.0 / math.sqrt(NX * NY * NZ))).astype(jnp.bfloat16)


def draw_start_block(key, part):
    column_scale = jnp.exp(jax.random.uniform(jax.random.fold_in(key, 21), (COLS, 1, 1, 1), jnp.float32, 0.0, math.log(10.0)))
    pos_x = lax.broadcasted_iota(jnp.int32, (1, NX, 1, 1), 1).astype(jnp.float32)
    ramp = 1.0 + 2.0 * pos_x / max(NX - 1, 1)
    values = jax.random.normal(key, (COLS, NX, NY, NZ), jnp.float32)
    lead_index = lax.broadcasted_iota(jnp.int32, (COLS, 1, 1, 1), 0)
    repeats = BASIS // COLS
    smooth = jnp.zeros((COLS, NX, NY, NZ), jnp.float32)
    for turn in range(repeats):
        weights = jax.random.normal(jax.random.fold_in(key, 41 + turn), (COLS, 1, 1, 1), jnp.float32)
        smooth = smooth + weights * mode_field(lead_index + COLS * turn)
    smooth = smooth * (1.0 / math.sqrt(repeats))
    return column_scale * (values * ramp + smooth)


def plant(drawn, own_key, least, largest):
    shape = drawn.shape
    spot = [jax.random.randint(jax.random.fold_in(own_key, axis), (), 0, shape[axis]) for axis in range(len(shape))]
    drawn = drawn.at[tuple(spot)].set(least)
    longest = shape.index(max(shape))
    spot[longest] = (spot[longest] + 1) % shape[longest]
    return drawn.at[tuple(spot)].set(largest)


def steps_of(rng, extent, pieces, low, largest):
    def one(position, blocks):
        draws = jax.random.uniform(jax.random.fold_in(jax.random.fold_in(rng, 6), position), (blocks,), jnp.float32, low / len(pieces), largest / len(pieces))
        return jnp.repeat(jnp.exp(draws), extent[position] // blocks).reshape((-1,) + (1,) * (len(extent) - position - 1))

    loudness = one(*pieces[0])
    for cut in pieces[1:]:
        loudness = loudness * one(*cut)
    return loudness


def setup_inputs(seed: int = 0) -> dict:
    arg_keys = jax.random.split(jax.random.key(seed), 13)
    return {
        "start_block": draw_start_block(jax.random.fold_in(arg_keys[12], 71), 0),
        "basis": draw_basis(jax.random.fold_in(arg_keys[12], 71), 0),
        "trans_x": jnp.clip(jnp.exp(math.log(1.0) - 2.9957323 * jax.random.uniform(arg_keys[2], (NX, NY, NZ), jnp.float32) ** steps_of(arg_keys[2], (NX, NY, NZ), ((0, 8), (1, 4), (2, 4)), -0.2, 0.2)), 0.05, 1.0),
        "trans_y": jnp.clip(jnp.exp(math.log(1.0) - 2.9957323 * jax.random.uniform(arg_keys[3], (NX, NY, NZ), jnp.float32) ** steps_of(arg_keys[3], (NX, NY, NZ), ((0, 8), (1, 4), (2, 4)), -0.2, 0.2)), 0.05, 1.0),
        "trans_z": jnp.clip(jnp.exp(math.log(1.0) - 2.9957323 * jax.random.uniform(arg_keys[4], (NX, NY, NZ), jnp.float32) ** steps_of(arg_keys[4], (NX, NY, NZ), ((0, 8), (1, 4), (2, 4)), -0.2, 0.2)), 0.05, 1.0),
        "pore_volume": jnp.clip(jnp.exp(math.log(2.0) - 1.3862944 * jax.random.uniform(arg_keys[5], (NX, NY, NZ), jnp.float32) ** steps_of(arg_keys[5], (NX, NY, NZ), ((0, 8), (1, 4), (2, 4)), -0.2, 0.2)), 0.5, 2.0),
        "shift_table": jnp.clip(jnp.exp(jax.random.uniform(arg_keys[6], (SHIFTS,), jnp.float32, math.log(0.5), math.log(4.0))), 0.5, 4.0),
        "shift_index": jax.random.randint(arg_keys[7], (1,), 0, SHIFTS).astype(jnp.int32),
        "fault_send": plant(jax.random.randint(arg_keys[8], (DEVICES, DEVICES, SLOTS), 0, CX * CY * CZ), jax.random.fold_in(arg_keys[8], 1), 0, (CX * CY * CZ) - 1).astype(jnp.int32),
        "fault_recv": plant(jax.random.randint(arg_keys[9], (DEVICES, DEVICES, SLOTS), 0, CX * CY * CZ), jax.random.fold_in(arg_keys[9], 1), 0, (CX * CY * CZ) - 1).astype(jnp.int32),
        "fault_trans": jnp.clip(jnp.exp(math.log(0.5) - 2.3025851 * jax.random.uniform(arg_keys[10], (DEVICES, DEVICES, SLOTS), jnp.float32) ** steps_of(arg_keys[10], (DEVICES, DEVICES, SLOTS), ((0, 128),), -0.2, 0.2)), 0.05, 0.5),
        "well_cells": plant(jax.random.randint(arg_keys[11], (WELLS,), 0, NX * NY * NZ), jax.random.fold_in(arg_keys[11], 1), 0, (NX * NY * NZ) - 1).astype(jnp.int32),
    }


def to_blocks(field, lead):
    shaped = field.reshape(lead, N_GX, CX, N_GY, CY, N_GZ, CZ)
    shaped = shaped.transpose(1, 3, 5, 0, 2, 4, 6)
    return shaped.reshape(N_GX * N_GY * N_GZ, lead, CX * CY * CZ)

def from_blocks(blocked, lead):
    shaped = blocked.reshape(N_GX, N_GY, N_GZ, lead, CX, CY, CZ)
    shaped = shaped.transpose(3, 0, 4, 1, 5, 2, 6)
    return shaped.reshape(lead, NX, NY, NZ)

def land_values(weights, targets, values):
    total = jnp.zeros((COLS, CX * CY * CZ), jnp.float32)
    return total.at[:, targets.reshape(-1)].add((weights[None] * values).reshape(COLS, -1))

def land_weights(weights, targets):
    total = jnp.zeros((1, CX * CY * CZ), jnp.float32)
    return total.at[0, targets.reshape(-1)].add(weights.reshape(-1))

def pick_cells(block_values, sources):
    return block_values[:, sources]

def reference(start_block, basis, trans_x, trans_y, trans_z, pore_volume, shift_table, shift_index, fault_send, fault_recv, fault_trans, well_cells):
    pos_x = lax.broadcasted_iota(jnp.int32, (NX, NY, NZ), 0)
    pos_y = lax.broadcasted_iota(jnp.int32, (NX, NY, NZ), 1)
    pos_z = lax.broadcasted_iota(jnp.int32, (NX, NY, NZ), 2)
    upper_x = jnp.where(pos_x < NX - 1, trans_x, 0.0)
    upper_y = jnp.where(pos_y < NY - 1, trans_y, 0.0)
    upper_z = jnp.where(pos_z < NZ - 1, trans_z, 0.0)
    lower_x = jnp.pad(upper_x, ((1, 0), (0, 0), (0, 0)))[:-1]
    lower_y = jnp.pad(upper_y, ((0, 0), (1, 0), (0, 0)))[:, :-1]
    lower_z = jnp.pad(upper_z, ((0, 0), (0, 0), (1, 0)))[:, :, :-1]
    shift = jnp.sum(jnp.where(jnp.arange(SHIFTS, dtype=jnp.int32) == shift_index[0], shift_table, 0.0))
    fault_diag = from_blocks(jax.vmap(land_weights)(fault_trans, fault_recv), 1)[0]
    diagonal = upper_x + lower_x + upper_y + lower_y + upper_z + lower_z + shift * pore_volume + fault_diag

    def operate(field):
        padded = jnp.pad(field, ((0, 0), (1, 1), (1, 1), (1, 1)))
        beside = upper_x * padded[:, 2:, 1:-1, 1:-1] + lower_x * padded[:, :-2, 1:-1, 1:-1]
        beside = beside + upper_y * padded[:, 1:-1, 2:, 1:-1] + lower_y * padded[:, 1:-1, :-2, 1:-1]
        beside = beside + upper_z * padded[:, 1:-1, 1:-1, 2:] + lower_z * padded[:, 1:-1, 1:-1, :-2]
        blocked = to_blocks(field, COLS)
        sent = jax.vmap(pick_cells)(blocked, fault_send)
        arrived = jnp.transpose(sent, (2, 1, 0, 3))
        remote = from_blocks(jax.vmap(land_values)(fault_trans, fault_recv, arrived), COLS)
        return diagonal * field - beside - remote
    sigma = 1.0 / 0.9
    weight_now = 1.0 / sigma
    solution = jnp.zeros_like(start_block)
    residual = start_block
    direction = residual / diagonal
    for number in range(TERMS):
        solution = solution + direction
        if number < TERMS - 1:
            residual = residual - operate(direction)
            weight_new = 1.0 / (2.0 * sigma - weight_now)
            direction = weight_new * weight_now * direction + 2.0 * weight_new / 0.9 * (residual / diagonal)
            weight_now = weight_new
    cells = NX * NY * NZ
    flat_basis = basis.reshape(BASIS, cells)
    flat_x = solution.reshape(COLS, cells)
    first_coeffs = jnp.dot(flat_basis.astype(jnp.float32), flat_x.astype(jnp.bfloat16).T.astype(jnp.float32), preferred_element_type=jnp.float32)
    first_rest = flat_x - jnp.dot(first_coeffs.astype(jnp.bfloat16).T.astype(jnp.float32), flat_basis.astype(jnp.float32), preferred_element_type=jnp.float32)
    second_coeffs = jnp.dot(flat_basis.astype(jnp.float32), first_rest.astype(jnp.bfloat16).T.astype(jnp.float32), preferred_element_type=jnp.float32)
    rest = first_rest - jnp.dot(second_coeffs.astype(jnp.bfloat16).T.astype(jnp.float32), flat_basis.astype(jnp.float32), preferred_element_type=jnp.float32)
    gram = jnp.dot(rest, rest.T, precision=lax.Precision.HIGHEST)
    lower = jnp.linalg.cholesky(gram)
    scale = math.sqrt(cells)
    new_flat = lax.linalg.triangular_solve(lower, rest, left_side=True, lower=True) * scale
    well_resp = new_flat[:, well_cells].T
    return (new_flat.reshape(COLS, NX, NY, NZ), first_coeffs, first_coeffs + second_coeffs, well_resp)
```

```python
import functools
import math

import jax
import jax.numpy as jnp
from jax import lax
from jax.experimental import pallas as pl
from jax.experimental.pallas import tpu as pltpu
from jax.sharding import PartitionSpec as P

TERMS = 8
MESH = pl.DeviceIdType.MESH
F32 = jnp.float32
BF16 = jnp.bfloat16
SIGMA = 1.0 / 0.9


def weights():
    now = 1.0 / SIGMA
    table = []
    for _ in range(TERMS - 1):
        new = 1.0 / (2.0 * SIGMA - now)
        table.append((new * now, 2.0 * new / 0.9))
        now = new
    return table


def zigzag(i, half):
    return half + ((i + 1) // 2) * (1 - 2 * (i % 2))


def offsets(slot):
    return (zigzag(slot // 16, 4), zigzag(slot // 4 % 4, 2), zigzag(slot % 4, 2))


def peer(slot, place, sign):
    (ox, oy, oz), (ax, ay, az) = offsets(slot), place
    return ((ax + sign * ox + 8) % 8, (ay + sign * oy + 4) % 4, (az + sign * oz + 4) % 4)


def number(coords):
    return coords[0] * 16 + coords[1] * 4 + coords[2]


def lanes(shape):
    return lax.broadcasted_iota(jnp.int32, shape, len(shape) - 1)


def half_swap(first, second):
    low = lanes(first.shape) < 64
    return (
        jnp.where(low, first, pltpu.roll(second, 64, 1)),
        jnp.where(low, pltpu.roll(first, 64, 1), second),
    )


def quarter_swap(value):
    upper = lax.broadcasted_iota(jnp.int32, value.shape, 0) // 4
    odd = lanes(value.shape) // 32 % 2
    moved = jnp.where(upper == 0, pltpu.roll(value, 96, 1), pltpu.roll(value, 32, 1))
    return jnp.where(upper == odd, value, pltpu.roll(moved, 4, 0))


def solve_kernel(
    start_ref, tx_ref, ty_ref, tz_ref, pv_ref, table_ref, index_ref, fs_ref, fr_ref, ft_ref,
    out_ref,
    dpad, dbf, res, acc, amat, ohs, ohr, his, hir, wr, send, recv, zsend, zrecv, coef, edge,
    rows, tsend, trecv,
    ssem, rsem, hssem, hrsem, tssem, trsem,
):
    place = (lax.axis_index("gx"), lax.axis_index("gy"), lax.axis_index("gz"))
    ax, ay, az = place
    up_x, down_x = ((ax + 1) % 8, ay, az), ((ax + 7) % 8, ay, az)
    up_y, down_y = (ax, (ay + 1) % 4, az), (ax, (ay + 3) % 4, az)
    up_z, down_z = (ax, ay, (az + 1) % 4), (ax, ay, (az + 3) % 4)
    barrier = pltpu.get_barrier_semaphore()

    def greet(slot, carry):
        pl.semaphore_signal(barrier, inc=1, device_id=peer(slot, place, 1), device_id_type=MESH)
        return carry

    lax.fori_loop(0, 127, greet, 0)

    def copy(src, dst, ss, rs, where):
        return pltpu.make_async_remote_copy(
            src_ref=src, dst_ref=dst, send_sem=ss, recv_sem=rs, device_id=where, device_id_type=MESH
        )

    def reorder(slot, carry):
        to = number(peer(slot, place, 1))
        source = number(peer(slot, place, -1))
        rows[0, pl.ds(slot, 1), 0:32] = fs_ref[pl.ds(to, 1), :]
        rows[1, pl.ds(slot, 1), 0:32] = fr_ref[pl.ds(source, 1), :]
        return carry

    lax.fori_loop(0, 128, reorder, 0)

    def reorder_weights(slot, carry):
        source = number(peer(slot, place, -1))
        wr[0, pl.ds(slot, 1), 0:32] = ft_ref[pl.ds(source, 1), :]
        return carry

    lax.fori_loop(0, 128, reorder_weights, 0)

    def flat(ref, which, half):
        lane = lanes((16, 128))
        pieces = [ref[which, pl.ds(half * 4 + q, 16, stride=8), :] for q in range(4)]
        total = pieces[0]
        for q in range(1, 4):
            total = jnp.where(lane // 32 == q, pltpu.roll(pieces[q], 32 * q, 1), total)
        return total

    column = lax.broadcasted_iota(jnp.int32, (256, 128), 0)
    for half in range(2):
        send_cells = flat(rows, 0, half)
        recv_cells = flat(rows, 1, half)
        recv_weight = flat(wr, 0, half)
        part = slice(half * 128, half * 128 + 128)
        for j in range(16):
            cell = send_cells[j : j + 1]
            his[j, :, part] = jnp.broadcast_to(cell // 256, (8, 128))
            ohs[j, :, part] = jnp.where(column == cell % 256, 1.0, 0.0).astype(BF16)
            cell = recv_cells[j : j + 1]
            hir[j, :, part] = jnp.broadcast_to((cell // 256).astype(F32), (16, 128)).astype(BF16)
            ohr[j, :, part] = jnp.where(column == cell % 256, 1.0, 0.0).astype(BF16)
            edge[j, :, part] = jnp.broadcast_to(recv_weight[j : j + 1], (8, 128))
    lane = lanes((1, 128))
    line = lane % 64
    first = (line % 2) * 128
    near, far = jnp.where(lane < 64, 127, 0), jnp.where(lane < 64, 0, 127)
    his[16, :, 0:128] = jnp.broadcast_to(line // 2, (8, 128))
    hir[16, :, 0:128] = jnp.broadcast_to((line // 2).astype(F32), (16, 128)).astype(BF16)
    ohs[16, :, 0:128] = jnp.where(column == first + near, 1.0, 0.0).astype(BF16)
    ohr[16, :, 0:128] = jnp.where(column == first + far, 1.0, 0.0).astype(BF16)

    for x in range(4):
        tsend[x : x + 1] = ty_ref[x * 16 + 15 : x * 16 + 16]
    tsend[4:8] = jnp.zeros((4, 128), F32)
    pl.semaphore_wait(barrier, 127)
    faces = (
        copy(tx_ref.at[pl.ds(48, 16)], trecv.at[pl.ds(0, 16)], tssem.at[0], trsem.at[0], up_x),
        copy(tsend, trecv.at[pl.ds(16, 8)], tssem.at[1], trsem.at[1], up_y),
        copy(tz_ref, trecv.at[pl.ds(24, 64)], tssem.at[2], trsem.at[2], up_z),
    )
    for face in faces:
        face.start()
    high, low = [], []
    total = jnp.zeros((64, 256), F32)
    pair = lax.broadcasted_iota(jnp.int32, (32, 256), 0)
    for j in range(16):
        weight = jnp.broadcast_to(edge[j, 0:1, :], (32, 256))
        hit = pair == jnp.broadcast_to(hir[j, 0:1, :].astype(F32).astype(jnp.int32), (32, 256))
        weight = jnp.where(hit, weight, 0.0)
        high = weight.astype(BF16)
        low = (weight - high.astype(F32)).astype(BF16)
        both = jnp.concatenate([high, low], axis=0)
        total = total + lax.dot_general(
            both, ohr[j], (((1,), (1,)), ((), ())), preferred_element_type=F32
        )
    fault = total[0:32] + total[32:64]
    acc[0:32, 0, :] = fault
    for face in faces:
        face.wait()
    shift = table_ref[0]
    for i in range(1, 16):
        shift = jnp.where(index_ref[0] == i, table_ref[i], shift)
    lane = lanes((16, 128))
    row = lax.broadcasted_iota(jnp.int32, (16, 128), 0)
    inside = [jnp.where(p > 0, 1.0, 0.0) for p in place]
    outside = [jnp.where(p < n - 1, 1.0, 0.0) for p, n in zip(place, (8, 4, 4))]
    for x in range(4):
        these = slice(x * 16, x * 16 + 16)
        upper_x = tx_ref[these] * (outside[0] if x == 3 else 1.0)
        if x == 0:
            lower_x = trecv[0:16] * inside[0]
        else:
            lower_x = tx_ref[(x - 1) * 16 : x * 16]
        ty = ty_ref[these]
        upper_y = jnp.where(row == 15, ty * outside[1], ty)
        lower_y = jnp.where(
            row == 0, trecv[16 + x : 17 + x] * inside[1], pltpu.roll(ty, 1, 0)
        )
        tz = tz_ref[these]
        upper_z = jnp.where(lane == 127, tz * outside[2], tz)
        lower_z = jnp.where(
            lane == 0,
            pltpu.roll(trecv[24 + x * 16 : 40 + x * 16], 1, 1) * inside[2],
            pltpu.roll(tz, 1, 1),
        )
        coef[0, these] = upper_x
        coef[1, these] = lower_x
        coef[2, these] = upper_y
        coef[3, these] = lower_y
        coef[4, these] = upper_z
        coef[5, these] = lower_z
        coef[6, these] = (
            upper_x + lower_x + upper_y + lower_y + upper_z + lower_z + shift * pv_ref[these]
        )
    for p in range(32):
        for parity in range(2):
            r = 2 * p + parity
            diagonal = coef[6, r : r + 1] + acc[p, 0:1, parity * 128 : parity * 128 + 128]
            coef[6, r : r + 1] = diagonal
            coef[7, r : r + 1] = 1.0 / diagonal
    both = jnp.concatenate([coef[5], coef[4]], axis=0).T
    lane = lanes((1, 128))
    edge[16, :, 0:128] = jnp.broadcast_to(
        jnp.where(lane < 64, both[0:1], both[127:128]), (8, 128)
    )
    lane = lanes((64, 128))
    coef[4] = jnp.where(lane == 127, 0.0, coef[4])
    coef[5] = jnp.where(lane == 0, 0.0, coef[5])

    def begin(r, carry):
        start = start_ref[pl.ds(r, 16, stride=64), :]
        res[r] = start
        d = start * jnp.broadcast_to(coef[7, pl.ds(r, 1)], (16, 128))
        dpad[0, 1 + r // 16, 1 + r % 16] = d
        out_ref[pl.ds(r, 16, stride=64), :] = d
        return carry

    lax.fori_loop(0, 64, begin, 0)

    def gather(j, width):
        product = jnp.dot(
            dbf[...].reshape(512, 256), ohs[j, :, 0:width], preferred_element_type=F32
        )
        tiles = []
        for h in range(width // 128):
            part = slice(h * 128, h * 128 + 128)
            hi = his[j, :, part]
            first = jnp.zeros((8, 128), F32)
            second = jnp.zeros((8, 128), F32)
            for p in range(32):
                hit = hi == p
                first = jnp.where(hit, product[p * 16 : p * 16 + 8, part], first)
                second = jnp.where(hit, product[p * 16 + 8 : p * 16 + 16, part], second)
            tiles.append((first, second))
        return tiles

    def scatter(j, tiles):
        width = 128 * len(tiles)
        for h, (first, second) in enumerate(tiles):
            part = slice(h * 128, h * 128 + 128)
            weight = edge[j, :, part]
            value = jnp.concatenate([first * weight, second * weight], axis=0).astype(BF16)
            hi = hir[j, :, part]
            for p in range(32):
                amat[p * 16 : p * 16 + 16, part] = jnp.where(
                    hi == float(p), value, jnp.zeros_like(value)
                )
        return lax.dot_general(
            amat[:, 0:width], ohr[j, :, 0:width], (((1,), (1,)), ((), ())),
            preferred_element_type=F32,
        ).reshape(32, 16, 256)

    def iterate(t, carry):
        now, gain = carry
        par = t % 2
        here = dpad.at[par]

        def halve(p, carry):
            for parity in range(2):
                r = 2 * p + parity
                dbf[p, :, parity * 128 : parity * 128 + 128] = here[
                    1 + r // 16, 1 + r % 16
                ].astype(BF16)
            return carry

        lax.fori_loop(0, 32, halve, 0)
        halos = [
            copy(here.at[4, pl.ds(1, 16)], here.at[0, pl.ds(1, 16)], hssem.at[0], hrsem.at[par, 0], up_x),
            copy(here.at[1, pl.ds(1, 16)], here.at[5, pl.ds(1, 16)], hssem.at[1], hrsem.at[par, 1], down_x),
            copy(here.at[pl.ds(1, 4), 16], here.at[pl.ds(1, 4), 0], hssem.at[2], hrsem.at[par, 2], up_y),
            copy(here.at[pl.ds(1, 4), 1], here.at[pl.ds(1, 4), 17], hssem.at[3], hrsem.at[par, 3], down_y),
        ]
        for halo in halos:
            halo.start()

        def outgoing(j, carry):
            for h, (first, second) in enumerate(gather(j, 256)):
                first, second = half_swap(first, second)
                first, second = quarter_swap(first), quarter_swap(second)
                base = j * 8 + h * 4
                send[base] = first[0:4]
                send[base + 1] = first[4:8]
                send[base + 2] = second[0:4]
                send[base + 3] = second[4:8]

            def ship(i, carry):
                slot = j * 8 + i
                copy(send.at[slot], recv.at[par, slot], ssem, rsem.at[par, j], peer(slot, place, 1)).start()
                return carry

            lax.fori_loop(0, jnp.where(j == 15, 7, 8), ship, 0)
            return carry

        lax.fori_loop(0, 16, outgoing, 0)
        recv[par, 127] = send[127]
        ((first, second),) = gather(16, 128)
        first, second = half_swap(first, second)
        zsend[0] = first
        zsend[1] = second
        halos_z = [
            copy(zsend.at[0], zrecv.at[par, 0], hssem.at[4], hrsem.at[par, 4], up_z),
            copy(zsend.at[1], zrecv.at[par, 1], hssem.at[5], hrsem.at[par, 5], down_z),
        ]
        for halo in halos_z:
            halo.start()
        for halo in halos:
            halo.wait_recv()

        def stencil(r, carry):
            x, y = 1 + r // 16, 1 + r % 16
            d = here[x, y]

            def times(which, value):
                return jnp.broadcast_to(coef[which, pl.ds(r, 1)], (16, 128)) * value

            total = times(0, here[x + 1, y]) + times(1, here[x - 1, y])
            total = total + times(2, here[x, y + 1]) + times(3, here[x, y - 1])
            total = total + times(4, pltpu.roll(d, 127, 1)) + times(5, pltpu.roll(d, 1, 1))
            res[r] = res[r] - (times(6, d) - total)
            return carry

        lax.fori_loop(0, 64, stencil, 0)
        for halo in halos_z:
            halo.wait_recv()
        tiles = half_swap(zrecv[par, 0], zrecv[par, 1])
        acc[...] = scatter(16, [tiles])

        def incoming(j, carry):
            @pl.when(j < 15)
            def _():
                copy(
                    send.at[pl.ds(0, 8)], recv.at[par, pl.ds(0, 8)], ssem, rsem.at[par, j], place
                ).wait_recv()

            @pl.when(j == 15)
            def _():
                copy(
                    send.at[pl.ds(0, 7)], recv.at[par, pl.ds(0, 7)], ssem, rsem.at[par, j], place
                ).wait_recv()

            tiles = []
            for h in range(2):
                base = j * 8 + h * 4
                first = jnp.concatenate([recv[par, base], recv[par, base + 1]], axis=0)
                second = jnp.concatenate([recv[par, base + 2], recv[par, base + 3]], axis=0)
                tiles.append(half_swap(quarter_swap(first), quarter_swap(second)))
            acc[...] += scatter(j, tiles)
            return carry

        lax.fori_loop(0, 16, incoming, 0)

        def update(p, carry):
            for parity in range(2):
                r = 2 * p + parity
                residual = res[r] + acc[p, :, parity * 128 : parity * 128 + 128]
                res[r] = residual
                inverse = jnp.broadcast_to(coef[7, pl.ds(r, 1)], (16, 128))
                x, y = 1 + r // 16, 1 + r % 16
                d = now * here[x, y] + gain * (residual * inverse)
                dpad[1 - par, x, y] = d
                out_ref[pl.ds(r, 16, stride=64), :] += d
            return carry

        lax.fori_loop(0, 32, update, 0)
        for halo in halos + halos_z:
            halo.wait_send()
        copy(send.at[pl.ds(0, 127)], recv.at[par, pl.ds(0, 127)], ssem, rsem.at[par, 0], place).wait_send()
        nxt_now, nxt_gain = carry
        for step in range(TERMS - 2):
            nxt_now = jnp.where(t == step, weights()[step + 1][0], nxt_now)
            nxt_gain = jnp.where(t == step, weights()[step + 1][1], nxt_gain)
        return nxt_now, nxt_gain

    lax.fori_loop(
        0, TERMS - 1, iterate, (jnp.float32(weights()[0][0]), jnp.float32(weights()[0][1]))
    )


def solve(start, tx, ty, tz, pv, table, index, fs, fr, ft):
    vmem = pl.BlockSpec(memory_space=pltpu.VMEM)
    smem = pl.BlockSpec(memory_space=pltpu.SMEM)
    return pl.pallas_call(
        solve_kernel,
        out_shape=jax.ShapeDtypeStruct((1024, 128), F32),
        in_specs=[vmem] * 5 + [smem] * 2 + [vmem] * 3,
        out_specs=vmem,
        scratch_shapes=[
            pltpu.VMEM((2, 6, 18, 16, 128), F32),
            pltpu.VMEM((32, 16, 256), BF16),
            pltpu.VMEM((64, 16, 128), F32),
            pltpu.VMEM((32, 16, 256), F32),
            pltpu.VMEM((512, 256), BF16),
            pltpu.VMEM((17, 256, 256), BF16),
            pltpu.VMEM((17, 256, 256), BF16),
            pltpu.VMEM((17, 8, 256), jnp.int32),
            pltpu.VMEM((17, 16, 256), BF16),
            pltpu.VMEM((1, 128, 128), F32),
            pltpu.VMEM((128, 4, 128), F32),
            pltpu.VMEM((2, 128, 4, 128), F32),
            pltpu.VMEM((2, 8, 128), F32),
            pltpu.VMEM((2, 2, 8, 128), F32),
            pltpu.VMEM((8, 64, 128), F32),
            pltpu.VMEM((17, 8, 256), F32),
            pltpu.VMEM((2, 128, 128), jnp.int32),
            pltpu.VMEM((8, 128), F32),
            pltpu.VMEM((88, 128), F32),
            pltpu.SemaphoreType.DMA,
            pltpu.SemaphoreType.DMA((2, 16)),
            pltpu.SemaphoreType.DMA((6,)),
            pltpu.SemaphoreType.DMA((2, 6)),
            pltpu.SemaphoreType.DMA((3,)),
            pltpu.SemaphoreType.DMA((3,)),
        ],
        compiler_params=pltpu.CompilerParams(
            collective_id=0, has_side_effects=True, vmem_limit_bytes=60 * 1024 * 1024
        ),
    )(start, tx, ty, tz, pv, table, index, fs, fr, ft)


def local(
    start_block, basis, trans_x, trans_y, trans_z, pore_volume, shift_table, shift_index,
    fault_send, fault_recv, fault_trans, well_cells,
):
    columns, size_x, size_y, size_z = start_block.shape
    cells = size_x * size_y * size_z
    count_x = lax.axis_size("gx")
    count_y = lax.axis_size("gy")
    count_z = lax.axis_size("gz")
    index_x = lax.axis_index("gx")
    index_y = lax.axis_index("gy")
    index_z = lax.axis_index("gz")
    full_x = size_x * count_x
    full_y = size_y * count_y
    full_z = size_z * count_z
    solution = solve(
        start_block.reshape(1024, 128),
        trans_x.reshape(64, 128),
        trans_y.reshape(64, 128),
        trans_z.reshape(64, 128),
        pore_volume.reshape(64, 128),
        shift_table,
        shift_index,
        fault_send[0],
        fault_recv[0],
        fault_trans[0],
    )
    plane = full_y * full_z
    well_x = well_cells // plane
    well_y = well_cells // full_z % full_y
    well_z = well_cells % full_z
    owned = (
        (well_x // size_x == index_x)
        & (well_y // size_y == index_y)
        & (well_z // size_z == index_z)
    )
    local_cell = (well_x % size_x * size_y + well_y % size_y) * size_z + well_z % size_z
    flat_basis = basis.reshape(basis.shape[0], cells)
    flat_x = solution.reshape(columns, cells)
    first_term = jnp.dot(
        flat_basis, flat_x.astype(jnp.bfloat16).T, preferred_element_type=jnp.float32
    )
    first_coeffs = lax.psum(first_term, ("gx", "gy", "gz"))
    first_rest = flat_x - jnp.dot(
        first_coeffs.astype(jnp.bfloat16).T, flat_basis, preferred_element_type=jnp.float32
    )
    second_term = jnp.dot(
        flat_basis, first_rest.astype(jnp.bfloat16).T, preferred_element_type=jnp.float32
    )
    second_coeffs = lax.psum(second_term, ("gx", "gy", "gz"))
    rest = first_rest - jnp.dot(
        second_coeffs.astype(jnp.bfloat16).T, flat_basis, preferred_element_type=jnp.float32
    )
    gram_term = jnp.dot(rest, rest.T, precision=lax.Precision.HIGHEST)
    gram, wells_value = lax.psum(
        (gram_term, jnp.where(owned[None, :], rest[:, local_cell], 0.0)), ("gx", "gy", "gz")
    )
    lower = jnp.linalg.cholesky(gram)
    scale = math.sqrt(full_x * full_y * full_z)
    new_flat = lax.linalg.triangular_solve(lower, rest, left_side=True, lower=True) * scale
    well_resp = (
        lax.linalg.triangular_solve(lower, wells_value, left_side=True, lower=True) * scale
    ).T
    return (
        new_flat.reshape(start_block.shape),
        first_coeffs,
        first_coeffs + second_coeffs,
        well_resp,
    )


def solution(mesh):
    in_specs = (
        P(None, "gx", "gy", "gz"),
        P(None, "gx", "gy", "gz"),
        P("gx", "gy", "gz"),
        P("gx", "gy", "gz"),
        P("gx", "gy", "gz"),
        P("gx", "gy", "gz"),
        P(),
        P(),
        P(("gx", "gy", "gz"), None, None),
        P(("gx", "gy", "gz"), None, None),
        P(("gx", "gy", "gz"), None, None),
        P(),
    )
    out_specs = (P(None, "gx", "gy", "gz"), P(), P(), P())
    return jax.shard_map(local, mesh=mesh, in_specs=in_specs, out_specs=out_specs, check_vma=False)
```

```python
import functools
import math

import jax
import jax.numpy as jnp
from jax import lax
from jax.experimental import pallas as pl
from jax.experimental.pallas import tpu as pltpu
from jax.sharding import PartitionSpec as P

TERMS = 8
MESH = pl.DeviceIdType.MESH
F32 = jnp.float32
BF16 = jnp.bfloat16
SIGMA = 1.0 / 0.9


def weights():
    now = 1.0 / SIGMA
    table = []
    for _ in range(TERMS - 1):
        new = 1.0 / (2.0 * SIGMA - now)
        table.append((new * now, 2.0 * new / 0.9))
        now = new
    return table


def far_first():
    along = {8: (0.0, 0.5, 1.0, 1.5, 2.0, 1.5, 1.0, 0.5), 4: (0.0, 1.0, 2.0, 1.0)}
    every = [(x, y, z) for x in range(8) for y in range(4) for z in range(4)]
    return sorted(every, key=lambda o: -(along[8][o[0]] + along[4][o[1]] + along[4][o[2]]))


SLOTS = far_first()


def lanes(shape):
    return lax.broadcasted_iota(jnp.int32, shape, len(shape) - 1)


def half_swap(first, second):
    low = lanes(first.shape) < 64
    return (
        jnp.where(low, first, pltpu.roll(second, 64, 1)),
        jnp.where(low, pltpu.roll(first, 64, 1), second),
    )


def quarter_swap(value):
    upper = lax.broadcasted_iota(jnp.int32, value.shape, 0) // 4
    odd = lanes(value.shape) // 32 % 2
    moved = jnp.where(upper == 0, pltpu.roll(value, 96, 1), pltpu.roll(value, 32, 1))
    return jnp.where(upper == odd, value, pltpu.roll(moved, 4, 0))


def split(value):
    high = value.astype(BF16)
    return high, (value - high.astype(F32)).astype(BF16)


def dot_nt(a, b, **kw):
    return lax.dot_general(a, b, (((1,), (1,)), ((), ())), preferred_element_type=F32, **kw)


def solve_kernel(
    start_ref, basis_ref, tx_ref, ty_ref, tz_ref, pv_ref, table_ref, index_ref, fs_ref, fr_ref, ft_ref, wells_ref,
    out_ref, first_ref, coeffs_ref, resp_ref,
    dpad, dbf, res, xacc, acc, ohs, ohr, his, hir, wr, send, recv, zsend, zrecv, coef, edge,
    rows, tsend, trecv, bas, bt, rest, gmat, gsend, grecv, gall, gsum, csend, crecv, call, csum,
    qsend, qrecv, wsend, wrecv, wall, wsum, ohw, hiw, cmat,
    ssem, rsem, hssem, hrsem, tssem, trsem, bsem, gs1, gr1, gs2, gr2, cs1, cr1, cs2, cr2,
    qs, qr, ws1, wr1, ws2, wr2,
):
    ax, ay, az = lax.axis_index("gx"), lax.axis_index("gy"), lax.axis_index("gz")
    place = (ax, ay, az)
    me = ax * 16 + ay * 4 + az
    xs = [(ax + i) % 8 for i in range(8)]
    ys = [(ay + i) % 4 for i in range(4)]
    zs = [(az + i) % 4 for i in range(4)]

    def peer(offset):
        return (xs[offset[0] % 8], ys[offset[1] % 4], zs[offset[2] % 4])

    def opposite(offset):
        return tuple(-o for o in offset)

    def number(offset):
        x, y, z = peer(offset)
        return x * 16 + y * 4 + z

    up_x, down_x = peer((1, 0, 0)), peer((7, 0, 0))
    up_y, down_y = peer((0, 1, 0)), peer((0, 3, 0))
    up_z, down_z = peer((0, 0, 1)), peer((0, 0, 3))

    def copy(src, dst, ss, rs, where):
        return pltpu.make_async_remote_copy(
            src_ref=src, dst_ref=dst, send_sem=ss, recv_sem=rs, device_id=where, device_id_type=MESH
        )

    barrier = pltpu.get_barrier_semaphore()
    for offset in SLOTS[:127]:
        pl.semaphore_signal(barrier, inc=1, device_id=peer(offset), device_id_type=MESH)
    fetch = pltpu.make_async_copy(basis_ref, bas, bsem)
    fetch.start()

    for slot, offset in enumerate(SLOTS):
        to = number(offset)
        source = number(opposite(offset))
        rows[0, slot : slot + 1, 0:32] = fs_ref[pl.ds(to, 1), :]
        rows[1, slot : slot + 1, 0:32] = fr_ref[pl.ds(source, 1), :]
        wr[0, slot : slot + 1, 0:32] = ft_ref[pl.ds(source, 1), :]

    def flat(ref, which, half):
        lane = lanes((16, 128))
        pieces = [ref[which, pl.ds(half * 4 + q, 16, stride=8), :] for q in range(4)]
        total = pieces[0]
        for q in range(1, 4):
            total = jnp.where(lane // 32 == q, pltpu.roll(pieces[q], 32 * q, 1), total)
        return total

    column = lax.broadcasted_iota(jnp.int32, (256, 128), 0)
    for half in range(2):
        send_cells = flat(rows, 0, half)
        recv_cells = flat(rows, 1, half)
        recv_weight = flat(wr, 0, half)
        part = slice(half * 128, half * 128 + 128)
        for j in range(16):
            cell = send_cells[j : j + 1]
            his[j, :, part] = jnp.broadcast_to(cell // 256, (8, 128))
            ohs[j, :, part] = jnp.where(column == cell % 256, 1.0, 0.0).astype(BF16)
            cell = recv_cells[j : j + 1]
            place_in = slice((j % 4) * 256 + half * 128, (j % 4) * 256 + half * 128 + 128)
            hir[j // 4, :, place_in] = jnp.broadcast_to((cell // 256).astype(F32), (16, 128)).astype(BF16)
            ohr[j // 4, :, place_in] = jnp.where(column == cell % 256, 1.0, 0.0).astype(BF16)
            edge[j // 4, :, place_in] = jnp.broadcast_to(recv_weight[j : j + 1], (8, 128))
    lane = lanes((1, 128))
    line = lane % 64
    first = (line % 2) * 128
    near, far = jnp.where(lane < 64, 127, 0), jnp.where(lane < 64, 0, 127)
    his[16, :, 0:128] = jnp.broadcast_to(line // 2, (8, 128))
    hir[4, :, 0:128] = jnp.broadcast_to((line // 2).astype(F32), (16, 128)).astype(BF16)
    ohs[16, :, 0:128] = jnp.where(column == first + near, 1.0, 0.0).astype(BF16)
    ohr[4, :, 0:128] = jnp.where(column == first + far, 1.0, 0.0).astype(BF16)
    well = wells_ref[...]
    well_x, well_y, well_z = well // 32768, well // 512 % 64, well % 512
    owned = (well_x // 4 == ax) & (well_y // 16 == ay) & (well_z // 128 == az)
    cell = (well_x % 4 * 16 + well_y % 16) * 128 + well_z % 128
    hiw[...] = jnp.broadcast_to(jnp.where(owned, cell // 256, -1), (8, 128))
    ohw[...] = jnp.where(column == cell % 256, 1.0, 0.0).astype(BF16)

    def begin(i, carry):
        for u in range(4):
            p = 4 * i + u
            for parity in range(2):
                res[p, :, parity * 128 : parity * 128 + 128] = start_ref[
                    pl.ds(2 * p + parity, 16, stride=64), :
                ]
        return carry

    lax.fori_loop(0, 8, begin, 0)
    pair = lax.broadcasted_iota(jnp.int32, (32, 1024), 0)
    total = jnp.zeros((64, 256), F32)
    for j in range(4):
        weight = jnp.broadcast_to(edge[j, 0:1, :], (32, 1024))
        hit = pair == jnp.broadcast_to(hir[j, 0:1, :].astype(F32).astype(jnp.int32), (32, 1024))
        high, low = split(jnp.where(hit, weight, 0.0))
        total = total + dot_nt(jnp.concatenate([high, low], axis=0), ohr[j])
    fault = total[0:32] + total[32:64]
    acc[0:32, 0, :] = fault

    for x in range(4):
        tsend[x : x + 1] = ty_ref[x * 16 + 15 : x * 16 + 16]
    tsend[4:8] = jnp.zeros((4, 128), F32)
    pl.semaphore_wait(barrier, 127)
    faces = (
        copy(tx_ref.at[pl.ds(48, 16)], trecv.at[pl.ds(0, 16)], tssem.at[0], trsem.at[0], up_x),
        copy(tsend, trecv.at[pl.ds(16, 8)], tssem.at[1], trsem.at[1], up_y),
        copy(tz_ref, trecv.at[pl.ds(24, 64)], tssem.at[2], trsem.at[2], up_z),
    )
    for face in faces:
        face.start()
    shift = table_ref[0]
    for i in range(1, 16):
        shift = jnp.where(index_ref[0] == i, table_ref[i], shift)
    for face in faces:
        face.wait()
    lane = lanes((16, 128))
    row = lax.broadcasted_iota(jnp.int32, (16, 128), 0)
    inside = [jnp.where(p > 0, 1.0, 0.0) for p in place]
    outside = [jnp.where(p < n - 1, 1.0, 0.0) for p, n in zip(place, (8, 4, 4))]
    for x in range(4):
        these = slice(x * 16, x * 16 + 16)
        upper_x = tx_ref[these] * (outside[0] if x == 3 else 1.0)
        if x == 0:
            lower_x = trecv[0:16] * inside[0]
        else:
            lower_x = tx_ref[(x - 1) * 16 : x * 16]
        ty = ty_ref[these]
        upper_y = jnp.where(row == 15, ty * outside[1], ty)
        lower_y = jnp.where(
            row == 0, trecv[16 + x : 17 + x] * inside[1], pltpu.roll(ty, 1, 0)
        )
        tz = tz_ref[these]
        upper_z = jnp.where(lane == 127, tz * outside[2], tz)
        lower_z = jnp.where(
            lane == 0,
            pltpu.roll(trecv[24 + x * 16 : 40 + x * 16], 1, 1) * inside[2],
            pltpu.roll(tz, 1, 1),
        )
        coef[0, these] = upper_x
        coef[1, these] = lower_x
        coef[2, these] = upper_y
        coef[3, these] = lower_y
        coef[4, these] = upper_z
        coef[5, these] = lower_z
        coef[6, these] = (
            upper_x + lower_x + upper_y + lower_y + upper_z + lower_z + shift * pv_ref[these]
        )
    for p in range(32):
        for parity in range(2):
            r = 2 * p + parity
            coef[6, r : r + 1] += acc[p, 0:1, parity * 128 : parity * 128 + 128]
    coef[7] = 1.0 / coef[6]
    both = jnp.concatenate([coef[5], coef[4]], axis=0).T
    lane = lanes((1, 128))
    edge[4, :, 0:128] = jnp.broadcast_to(
        jnp.where(lane < 64, both[0:1], both[127:128]), (8, 128)
    )
    lane = lanes((64, 128))
    coef[4] = jnp.where(lane == 127, 0.0, coef[4])
    coef[5] = jnp.where(lane == 0, 0.0, coef[5])

    def initial(i, carry):
        for u in range(4):
            p = 4 * i + u
            for parity in range(2):
                part = slice(parity * 128, parity * 128 + 128)
                inverse = jnp.broadcast_to(coef[7, pl.ds(2 * p + parity, 1)], (16, 128))
                d = res[p, :, part] * inverse
                dpad[0, 1 + i // 2, 1 + (i % 2) * 8 + 2 * u + parity] = d
                dbf[p, :, part] = d.astype(BF16)
                xacc[p, :, part] = d
        return carry

    lax.fori_loop(0, 8, initial, 0)

    def pick(source, one_hot, hi_of, width):
        product = jnp.dot(source, one_hot, preferred_element_type=F32)
        tiles = []
        for h in range(width // 128):
            part = slice(h * 128, h * 128 + 128)
            hi = hi_of(part)
            first = jnp.zeros((8, 128), F32)
            second = jnp.zeros((8, 128), F32)
            for p in range(32):
                hit = hi == p
                first = jnp.where(hit, product[p * 16 : p * 16 + 8, part], first)
                second = jnp.where(hit, product[p * 16 + 8 : p * 16 + 16, part], second)
            tiles.append((first, second))
        return tiles

    def gather(j, width):
        return pick(
            dbf[...].reshape(512, 256), ohs[j, :, 0:width], lambda part: his[j, :, part], width
        )

    def scatter(j, tiles):
        width = 128 * len(tiles)
        blocks = []
        for h, (first, second) in enumerate(tiles):
            part = slice(h * 128, h * 128 + 128)
            weight = edge[j, :, part]
            value = jnp.concatenate([first * weight, second * weight], axis=0).astype(BF16)
            hi = hir[j, :, part]
            zero = jnp.zeros_like(value)
            blocks.append(
                jnp.concatenate([jnp.where(hi == float(p), value, zero) for p in range(32)], axis=0)
            )
        placed = blocks[0] if len(blocks) == 1 else jnp.concatenate(blocks, axis=1)
        return dot_nt(placed, ohr[j, :, 0:width]).reshape(32, 16, 256)

    exchange = copy(gsend.at[pl.ds(0, 127)], grecv.at[pl.ds(0, 127)], gs1, gr1, place)
    spread = copy(gsend.at[pl.ds(0, 127)], gall.at[pl.ds(0, 127)], gs2, gr2, place)

    def permute(t):
        a = lax.broadcasted_iota(jnp.int32, (256, 256), 0)
        b = lax.broadcasted_iota(jnp.int32, (256, 256), 1)
        order = jnp.where(b == a % 16 * 16 + a // 16, 1.0, 0.0).astype(BF16)

        def block(i, carry):
            k = t * 4 + i
            for q in range(2):
                sides = []
                for side in range(2):
                    base = k * 1024 + (2 * q + side) * 16
                    sides.append(
                        jnp.concatenate(
                            [bas[pl.ds(pl.multiple_of(base + 64 * kk, 16), 16), :] for kk in range(16)],
                            axis=0,
                        )
                    )
                turned = jnp.dot(
                    order, jnp.concatenate(sides, axis=1), preferred_element_type=F32
                ).astype(BF16)
                for side in range(2):
                    for xx in range(16):
                        r = (2 * q + side) * 16 + xx
                        bt[r // 2, pl.ds(pl.multiple_of(k * 16, 16), 16), r % 2 * 128 : r % 2 * 128 + 128] = (
                            turned[xx * 16 : xx * 16 + 16, side * 128 : side * 128 + 128]
                        )
            return carry

        lax.fori_loop(0, 4, block, 0)

    def iterate(t, carry):
        now, gain = carry
        par = t % 2
        here = dpad.at[par]
        halos = [
            copy(here.at[4, pl.ds(1, 16)], here.at[0, pl.ds(1, 16)], hssem.at[0], hrsem.at[par, 0], up_x),
            copy(here.at[1, pl.ds(1, 16)], here.at[5, pl.ds(1, 16)], hssem.at[1], hrsem.at[par, 1], down_x),
            copy(here.at[pl.ds(1, 4), 16], here.at[pl.ds(1, 4), 0], hssem.at[2], hrsem.at[par, 2], up_y),
            copy(here.at[pl.ds(1, 4), 1], here.at[pl.ds(1, 4), 17], hssem.at[3], hrsem.at[par, 3], down_y),
        ]
        for halo in halos:
            halo.start()
        for j in range(16):
            for h, (first, second) in enumerate(gather(j, 256)):
                first, second = half_swap(first, second)
                first, second = quarter_swap(first), quarter_swap(second)
                base = j * 8 + h * 4
                send[base] = first[0:4]
                send[base + 1] = first[4:8]
                send[base + 2] = second[0:4]
                send[base + 3] = second[4:8]
            for slot in range(j * 8, min(j * 8 + 8, 127)):
                copy(send.at[slot], recv.at[par, slot], ssem, rsem.at[par, slot // 32], peer(SLOTS[slot])).start()
        recv[par, 127] = send[127]
        ((first, second),) = gather(16, 128)
        first, second = half_swap(first, second)
        zsend[0] = first
        zsend[1] = second
        halos_z = [
            copy(zsend.at[0], zrecv.at[par, 0], hssem.at[4], hrsem.at[par, 4], up_z),
            copy(zsend.at[1], zrecv.at[par, 1], hssem.at[5], hrsem.at[par, 5], down_z),
        ]
        for halo in halos_z:
            halo.start()

        @pl.when(t == 0)
        def _():
            fetch.wait()

        @pl.when(t < 4)
        def _():
            permute(t)

        @pl.when(t == 4)
        def _():
            gmat[...] = jnp.zeros_like(gmat)

            def add(i, carry):
                total = gmat[...]
                for u in range(4):
                    total = total + dot_nt(bt[4 * i + u], bt[4 * i + u])
                gmat[...] = total
                return carry

            lax.fori_loop(0, 8, add, 0)

        @pl.when(t == 5)
        def _():
            for c in range(128):
                gsend[c] = gmat[c % 64 * 4 : c % 64 * 4 + 4, c // 64 * 128 : c // 64 * 128 + 128]
            for offset in SLOTS[:127]:
                copy(gsend.at[number(offset)], grecv.at[me], gs1, gr1, peer(offset)).start()
            grecv[me] = gsend[me]

        @pl.when(t == 6)
        def _():
            exchange.wait_recv()
            gsum[...] = jnp.sum(grecv[...], axis=0)
            for offset in SLOTS[:127]:
                copy(gsum, gall.at[me], gs2, gr2, peer(offset)).start()
            gall[me] = gsum[...]

        for halo in halos:
            halo.wait_recv()

        def stencil(i, carry):
            x = 1 + i // 4
            for u in range(4):
                r = 4 * i + u
                y = 1 + (i % 4) * 4 + u
                p, part = 2 * i + u // 2, slice(u % 2 * 128, u % 2 * 128 + 128)
                d = here[x, y]

                def times(which, value):
                    return jnp.broadcast_to(coef[which, pl.ds(r, 1)], (16, 128)) * value

                total = times(0, here[x + 1, y]) + times(1, here[x - 1, y])
                total = total + times(2, here[x, y + 1]) + times(3, here[x, y - 1])
                total = total + times(4, pltpu.roll(d, 127, 1)) + times(5, pltpu.roll(d, 1, 1))
                res[p, :, part] = res[p, :, part] - (times(6, d) - total)
            return carry

        lax.fori_loop(0, 16, stencil, 0)
        for halo in halos_z:
            halo.wait_recv()
        acc[...] = scatter(4, [half_swap(zrecv[par, 0], zrecv[par, 1])])

        def incoming(j, carry):
            @pl.when(j < 3)
            def _():
                copy(
                    send.at[pl.ds(0, 32)], recv.at[par, pl.ds(0, 32)], ssem, rsem.at[par, j], place
                ).wait_recv()

            @pl.when(j == 3)
            def _():
                copy(
                    send.at[pl.ds(0, 31)], recv.at[par, pl.ds(0, 31)], ssem, rsem.at[par, j], place
                ).wait_recv()

            tiles = []
            for h in range(8):
                base = j * 32 + h * 4
                first = jnp.concatenate([recv[par, base], recv[par, base + 1]], axis=0)
                second = jnp.concatenate([recv[par, base + 2], recv[par, base + 3]], axis=0)
                tiles.append(half_swap(quarter_swap(first), quarter_swap(second)))
            acc[...] += scatter(j, tiles)
            return carry

        lax.fori_loop(0, 4, incoming, 0)

        def update(i, carry):
            for u in range(4):
                p = 4 * i + u
                for parity in range(2):
                    part = slice(parity * 128, parity * 128 + 128)
                    residual = res[p, :, part] + acc[p, :, part]
                    res[p, :, part] = residual
                    inverse = jnp.broadcast_to(coef[7, pl.ds(2 * p + parity, 1)], (16, 128))
                    x, y = 1 + i // 2, 1 + (i % 2) * 8 + 2 * u + parity
                    d = now * here[x, y] + gain * (residual * inverse)
                    dpad[1 - par, x, y] = d
                    dbf[p, :, part] = d.astype(BF16)
                    xacc[p, :, part] += d
            return carry

        lax.fori_loop(0, 8, update, 0)
        for halo in halos + halos_z:
            halo.wait_send()
        copy(send.at[pl.ds(0, 127)], recv.at[par, pl.ds(0, 127)], ssem, rsem.at[par, 0], place).wait_send()
        nxt_now, nxt_gain = carry
        for step in range(TERMS - 2):
            nxt_now = jnp.where(t == step, weights()[step + 1][0], nxt_now)
            nxt_gain = jnp.where(t == step, weights()[step + 1][1], nxt_gain)
        return nxt_now, nxt_gain

    lax.fori_loop(
        0, TERMS - 1, iterate, (jnp.float32(weights()[0][0]), jnp.float32(weights()[0][1]))
    )

    def project(i, total):
        for u in range(4):
            p = 4 * i + u
            high, low = split(xacc[p])
            total = total + dot_nt(jnp.concatenate([high, low], axis=0), bt[p])
        return total

    total = lax.fori_loop(0, 8, project, jnp.zeros((32, 256), F32))
    for c in range(32):
        csend[c] = total[c % 16 * 2 : c % 16 * 2 + 2, c // 16 * 128 : c // 16 * 128 + 128]
    mine = ax * 4 + ay
    for offset in [o for o in SLOTS if o[2] == 0]:
        x, y = xs[offset[0]], ys[offset[1]]
        to = copy(csend.at[x * 4 + y], crecv.at[me], cs1, cr1, (x, y, y))
        if offset[:2] != (0, 0):
            to.start()
        else:

            @pl.when(az != ay)
            def _(to=to):
                to.start()

    @pl.when(az == ay)
    def _():
        crecv[me] = csend[mine]
        copy(crecv.at[pl.ds(0, 127)], crecv.at[pl.ds(0, 127)], cs1, cr1, place).wait_recv()
        csum[...] = jnp.sum(crecv[...], axis=0)
        for offset in SLOTS[:127]:
            copy(csum, call.at[mine], cs2, cr2, peer(offset)).start()
        call[mine] = csum[...]
        copy(call.at[pl.ds(0, 31)], call.at[pl.ds(0, 31)], cs2, cr2, place).wait_recv()

    @pl.when(az != ay)
    def _():
        copy(call, call, cs2, cr2, place).wait_recv()

    for c in range(32):
        cmat[c % 16 * 2 : c % 16 * 2 + 2, c // 16 * 128 : c // 16 * 128 + 128] = call[c]
    spread.wait_recv()
    for c in range(128):
        gmat[c % 64 * 4 : c % 64 * 4 + 4, c // 64 * 128 : c // 64 * 128 + 128] = gall[c]
    leading = cmat[0:16]
    first = leading.astype(BF16)
    second_sum = leading + cmat[16:32] - jnp.dot(
        first.astype(F32), gmat[...], precision=lax.Precision.HIGHEST, preferred_element_type=F32
    )
    both = jnp.concatenate([first, second_sum.astype(BF16)], axis=0)
    pad = jnp.zeros((112, 256), F32)
    first_ref[...] = jnp.concatenate([leading, pad], axis=0).T[:, 0:16]
    coeffs_ref[...] = jnp.concatenate([leading + second_sum, pad], axis=0).T[:, 0:16]

    def subtract(i, total):
        for u in range(4):
            p = 4 * i + u
            taken = jnp.dot(both, bt[p], preferred_element_type=F32)
            left = xacc[p] - taken[0:16] - taken[16:32]
            high, low = split(left)
            parts = jnp.concatenate([high, low], axis=0)
            rest[p] = parts
            total = total + dot_nt(parts, parts)
        return total

    total = lax.fori_loop(0, 8, subtract, jnp.zeros((32, 32), F32))
    gram = total[0:16, 0:16] + total[0:16, 16:32] + total[16:32, 0:16]
    lane = lanes((8, 128))
    wide = jnp.concatenate([gram, jnp.zeros((16, 112), F32)], axis=1)
    row = lax.broadcasted_iota(jnp.int32, (8, 128), 0)
    for half in range(2):
        value = wide[half * 8 : half * 8 + 8]
        line = jnp.zeros((1, 128), F32)
        for i in range(8):
            line = line + pltpu.roll(value[i : i + 1], 16 * i, 1)
        qsend[half : half + 1] = line
    for offset in SLOTS[:127]:
        copy(qsend, qrecv.at[me], qs, qr, peer(offset)).start()
    qrecv[me] = qsend[...]

    ((first_w, second_w),) = pick(
        rest[:, 0:16].reshape(512, 256), ohw[...], lambda part: hiw[...], 128
    )
    ((low_first, low_second),) = pick(
        rest[:, 16:32].reshape(512, 256), ohw[...], lambda part: hiw[...], 128
    )
    packed, _ = half_swap(first_w + low_first, second_w + low_second)
    for c in range(4):
        wsend[c] = packed[2 * c : 2 * c + 2]
    for c in range(4):

        @pl.when(~((ax == 2 * c) & (ay == c) & (az == c)))
        def _(c=c):
            copy(wsend.at[c], wrecv.at[me], ws1, wr1, (2 * c, c, c)).start()

    owner = (ax == 2 * ay) & (az == ay)

    @pl.when(owner)
    def _():
        wrecv[me] = wsend[ay]
        copy(wrecv.at[pl.ds(0, 127)], wrecv.at[pl.ds(0, 127)], ws1, wr1, place).wait_recv()
        wsum[...] = jnp.sum(wrecv[...], axis=0)
        for offset in SLOTS[:127]:
            copy(wsum, wall.at[ay], ws2, wr2, peer(offset)).start()
        wall[ay] = wsum[...]

    copy(qrecv.at[pl.ds(0, 127)], qrecv.at[pl.ds(0, 127)], qs, qr, place).wait_recv()
    sums = jnp.sum(qrecv[...], axis=0)
    pieces = []
    for half in range(2):
        for i in range(8):
            pieces.append(pltpu.roll(sums[half : half + 1], (128 - 16 * i) % 128, 1))
    gram = jnp.concatenate(pieces, axis=0)
    lane = lanes((16, 128))
    row = lax.broadcasted_iota(jnp.int32, (16, 128), 0)
    table = jnp.where(lane < 16, gram, jnp.where(lane == row + 16, 1.0, 0.0))
    for j in range(15):
        column = jnp.broadcast_to(table[:, j : j + 1], (16, 128))
        factor = jnp.where(row > j, column / column[j : j + 1], 0.0)
        table = table - factor * table[j : j + 1]
    pivot = jnp.sum(jnp.where(lane == row, table, 0.0), axis=1, keepdims=True)
    scale = 1024.0 / jnp.sqrt(pivot)
    inverse = table[:, 16:32] * scale
    high, low = split(inverse)
    factors = jnp.concatenate([high, low, high], axis=1)

    def finish(i, carry):
        for u in range(2):
            p = 2 * i + u
            parts = rest[p]
            block = jnp.dot(
                factors, jnp.concatenate([parts[0:16], parts[0:16], parts[16:32]], axis=0),
                preferred_element_type=F32,
            )
            for parity in range(2):
                out_ref[pl.ds(2 * p + parity, 16, stride=64), :] = block[
                    :, parity * 128 : parity * 128 + 128
                ]
        return carry

    lax.fori_loop(0, 16, finish, 0)

    @pl.when(owner)
    def _():
        copy(wall.at[pl.ds(0, 3)], wall.at[pl.ds(0, 3)], ws2, wr2, place).wait_recv()

    @pl.when(jnp.logical_not(owner))
    def _():
        copy(wall, wall, ws2, wr2, place).wait_recv()

    packed = jnp.concatenate([wall[c] for c in range(4)], axis=0)
    at_wells = jnp.where(lanes((16, 128)) < 64, jnp.concatenate([packed, pltpu.roll(packed, 64, 1)], axis=0), 0.0)
    answer = jnp.dot(inverse, at_wells, precision=lax.Precision.HIGHEST, preferred_element_type=F32)
    resp_ref[...] = jnp.concatenate([answer, jnp.zeros((112, 128), F32)], axis=0).T[0:64, 0:16]
    exchange.wait_send()
    copy(gall.at[pl.ds(0, 127)], gall.at[pl.ds(0, 127)], gs2, gr2, place).wait_send()
    copy(qrecv.at[pl.ds(0, 127)], qrecv.at[pl.ds(0, 127)], qs, qr, place).wait_send()

    @pl.when(az == ay)
    def _():
        copy(call.at[pl.ds(0, 31)], call.at[pl.ds(0, 31)], cs1, cr1, place).wait_send()
        copy(crecv.at[pl.ds(0, 127)], crecv.at[pl.ds(0, 127)], cs2, cr2, place).wait_send()

    @pl.when(az != ay)
    def _():
        copy(call, call, cs1, cr1, place).wait_send()

    @pl.when(owner)
    def _():
        copy(wall.at[pl.ds(0, 3)], wall.at[pl.ds(0, 3)], ws1, wr1, place).wait_send()
        copy(wrecv.at[pl.ds(0, 127)], wrecv.at[pl.ds(0, 127)], ws2, wr2, place).wait_send()

    @pl.when(jnp.logical_not(owner))
    def _():
        copy(wall, wall, ws1, wr1, place).wait_send()


def solve(*args):
    vmem = pl.BlockSpec(memory_space=pltpu.VMEM)
    smem = pl.BlockSpec(memory_space=pltpu.SMEM)
    dma = pltpu.SemaphoreType.DMA
    return pl.pallas_call(
        solve_kernel,
        out_shape=(
            jax.ShapeDtypeStruct((1024, 128), F32),
            jax.ShapeDtypeStruct((256, 16), F32),
            jax.ShapeDtypeStruct((256, 16), F32),
            jax.ShapeDtypeStruct((64, 16), F32),
        ),
        in_specs=[vmem, pl.BlockSpec(memory_space=pl.ANY)] + [vmem] * 4 + [smem] * 2 + [vmem] * 4,
        out_specs=(vmem,) * 4,
        scratch_shapes=[
            pltpu.VMEM((2, 6, 18, 16, 128), F32),
            pltpu.VMEM((32, 16, 256), BF16),
            pltpu.VMEM((32, 16, 256), F32),
            pltpu.VMEM((32, 16, 256), F32),
            pltpu.VMEM((32, 16, 256), F32),
            pltpu.VMEM((17, 256, 256), BF16),
            pltpu.VMEM((5, 256, 1024), BF16),
            pltpu.VMEM((17, 8, 256), jnp.int32),
            pltpu.VMEM((5, 16, 1024), BF16),
            pltpu.VMEM((1, 128, 128), F32),
            pltpu.VMEM((128, 4, 128), F32),
            pltpu.VMEM((2, 128, 4, 128), F32),
            pltpu.VMEM((2, 8, 128), F32),
            pltpu.VMEM((2, 2, 8, 128), F32),
            pltpu.VMEM((8, 64, 128), F32),
            pltpu.VMEM((5, 8, 1024), F32),
            pltpu.VMEM((2, 128, 128), jnp.int32),
            pltpu.VMEM((8, 128), F32),
            pltpu.VMEM((88, 128), F32),
            pltpu.VMEM((16384, 128), BF16),
            pltpu.VMEM((32, 256, 256), BF16),
            pltpu.VMEM((32, 32, 256), BF16),
            pltpu.VMEM((256, 256), F32),
            pltpu.VMEM((128, 4, 128), F32),
            pltpu.VMEM((128, 4, 128), F32),
            pltpu.VMEM((128, 4, 128), F32),
            pltpu.VMEM((4, 128), F32),
            pltpu.VMEM((32, 2, 128), F32),
            pltpu.VMEM((128, 2, 128), F32),
            pltpu.VMEM((32, 2, 128), F32),
            pltpu.VMEM((2, 128), F32),
            pltpu.VMEM((2, 128), F32),
            pltpu.VMEM((128, 2, 128), F32),
            pltpu.VMEM((4, 2, 128), F32),
            pltpu.VMEM((128, 2, 128), F32),
            pltpu.VMEM((4, 2, 128), F32),
            pltpu.VMEM((2, 128), F32),
            pltpu.VMEM((256, 128), BF16),
            pltpu.VMEM((8, 128), jnp.int32),
            pltpu.VMEM((32, 256), F32),
            dma,
            dma((2, 4)),
            dma((6,)),
            dma((2, 6)),
            dma((3,)),
            dma((3,)),
        ]
        + [dma] * 15,
        compiler_params=pltpu.CompilerParams(
            collective_id=0, has_side_effects=True, vmem_limit_bytes=60 * 1024 * 1024
        ),
    )(*args)


def local(
    start_block, basis, trans_x, trans_y, trans_z, pore_volume, shift_table, shift_index,
    fault_send, fault_recv, fault_trans, well_cells,
):
    wells = jnp.concatenate([well_cells, well_cells]).reshape(1, 128)
    new_block, first_coeffs, coeffs, well_resp = solve(
        start_block.reshape(1024, 128),
        basis.reshape(16384, 128),
        trans_x.reshape(64, 128),
        trans_y.reshape(64, 128),
        trans_z.reshape(64, 128),
        pore_volume.reshape(64, 128),
        shift_table,
        shift_index,
        fault_send[0],
        fault_recv[0],
        fault_trans[0],
        wells,
    )
    return new_block.reshape(start_block.shape), first_coeffs, coeffs, well_resp


def solution(mesh):
    in_specs = (
        P(None, "gx", "gy", "gz"),
        P(None, "gx", "gy", "gz"),
        P("gx", "gy", "gz"),
        P("gx", "gy", "gz"),
        P("gx", "gy", "gz"),
        P("gx", "gy", "gz"),
        P(),
        P(),
        P(("gx", "gy", "gz"), None, None),
        P(("gx", "gy", "gz"), None, None),
        P(("gx", "gy", "gz"), None, None),
        P(),
    )
    out_specs = (P(None, "gx", "gy", "gz"), P(), P(), P())
    return jax.shard_map(local, mesh=mesh, in_specs=in_specs, out_specs=out_specs, check_vma=False)
```

```python
import functools
import math

import jax
import jax.numpy as jnp
import numpy as np
from jax import lax
from jax.experimental import pallas as pl
from jax.experimental.pallas import tpu as pltpu
from jax.sharding import PartitionSpec as P

TERMS = 8
MESH = pl.DeviceIdType.MESH
F32 = jnp.float32
BF16 = jnp.bfloat16
SIGMA = 1.0 / 0.9


def weights():
    now = 1.0 / SIGMA
    table = []
    for _ in range(TERMS - 1):
        new = 1.0 / (2.0 * SIGMA - now)
        table.append((new * now, 2.0 * new / 0.9))
        now = new
    return table


def far_first():
    along = {8: (0.0, 0.5, 1.0, 1.5, 2.0, 1.5, 1.0, 0.5), 4: (0.0, 1.0, 2.0, 1.0)}
    every = [(x, y, z) for x in range(8) for y in range(4) for z in range(4)]
    return sorted(every, key=lambda o: -(along[8][o[0]] + along[4][o[1]] + along[4][o[2]]))


SLOTS = far_first()


def lanes(shape):
    return lax.broadcasted_iota(jnp.int32, shape, len(shape) - 1)


def half_swap(first, second):
    low = lanes(first.shape) < 64
    return (
        jnp.where(low, first, pltpu.roll(second, 64, 1)),
        jnp.where(low, pltpu.roll(first, 64, 1), second),
    )


def quarter_swap(value):
    upper = lax.broadcasted_iota(jnp.int32, value.shape, 0) // 4
    odd = lanes(value.shape) // 32 % 2
    moved = jnp.where(upper == 0, pltpu.roll(value, 96, 1), pltpu.roll(value, 32, 1))
    return jnp.where(upper == odd, value, pltpu.roll(moved, 4, 0))


def split(value):
    high = value.astype(BF16)
    return high, (value - high.astype(F32)).astype(BF16)


def dot_nt(a, b, **kw):
    return lax.dot_general(a, b, (((1,), (1,)), ((), ())), preferred_element_type=F32, **kw)


def solve_kernel(
    start_ref, basis_ref, tx_ref, ty_ref, tz_ref, pv_ref, table_ref, index_ref, fs_ref, fr_ref, ft_ref, wells_ref, offs_ref,
    rest, factors_ref, first_ref, coeffs_ref, resp_ref,
    dpad, dbf, res, xacc, acc, ohs, ohr, his, hir, mk, mkz, send, recv, zsend, zrecv, coef, edge,
    rows, tsend, trecv, bas, bt, gmat, gsend, grecv, gall, gsum, csend, crecv, call, csum,
    qsend, qrecv, wsend, wrecv, wall, wsum, ohw, hiw, cmat,
    ssem, rsem, hssem, hrsem, tssem, trsem, bsem, gs1, gr1, gs2, gr2, cs1, cr1, cs2, cr2,
    qs, qr, ws1, wr1, ws2, wr2,
):
    ax, ay, az = lax.axis_index("gx"), lax.axis_index("gy"), lax.axis_index("gz")
    place = (ax, ay, az)
    me = ax * 16 + ay * 4 + az
    xs = [(ax + i) % 8 for i in range(8)]
    ys = [(ay + i) % 4 for i in range(4)]
    zs = [(az + i) % 4 for i in range(4)]

    def peer(offset):
        return (xs[offset[0] % 8], ys[offset[1] % 4], zs[offset[2] % 4])

    def number(offset):
        x, y, z = peer(offset)
        return x * 16 + y * 4 + z

    up_x, down_x = peer((1, 0, 0)), peer((7, 0, 0))
    up_y, down_y = peer((0, 1, 0)), peer((0, 3, 0))
    up_z, down_z = peer((0, 0, 1)), peer((0, 0, 3))

    def copy(src, dst, ss, rs, where):
        return pltpu.make_async_remote_copy(
            src_ref=src, dst_ref=dst, send_sem=ss, recv_sem=rs, device_id=where, device_id_type=MESH
        )

    barrier = pltpu.get_barrier_semaphore()
    for offset in SLOTS[:127]:
        pl.semaphore_signal(barrier, inc=1, device_id=peer(offset), device_id_type=MESH)
    fetch = pltpu.make_async_copy(basis_ref, bas, bsem)
    fetch.start()

    offs = offs_ref[...]
    spot = lax.broadcasted_iota(jnp.int32, (128, 128), 0)

    def order_of(sign):
        x, y, z = (offs[i : i + 1] * sign for i in range(3))
        target = (x + ax + 8) % 8 * 16 + (y + ay + 4) % 4 * 4 + (z + az + 4) % 4
        return jnp.where(spot == target, 1.0, 0.0).astype(BF16)

    def spread_rows(which, value):
        rows[which] = jnp.concatenate([value] * 4, axis=0).T

    def halves(ref, order, which):
        cells = ref[...]
        parts = jnp.concatenate([cells // 256, cells % 256], axis=0).astype(F32).astype(BF16)
        moved = jnp.dot(parts, order, preferred_element_type=F32)
        spread_rows(which, moved[0:32])
        spread_rows(which + 1, moved[32:64])

    halves(fs_ref, order_of(1), 0)
    source_order = order_of(-1)
    halves(fr_ref, source_order, 2)
    high, low = split(ft_ref[...])
    lowest = (ft_ref[...] - high.astype(F32) - low.astype(F32)).astype(BF16)
    moved = jnp.dot(
        jnp.concatenate([high, low, lowest], axis=0), source_order, preferred_element_type=F32
    )
    spread_rows(4, moved[0:32] + moved[32:64] + moved[64:96])

    def flat(which, half):
        lane = lanes((16, 128))
        pieces = [rows[which, pl.ds(half * 4 + q, 16, stride=8), :] for q in range(4)]
        total = pieces[0]
        for q in range(1, 4):
            total = jnp.where(lane // 32 == q, pieces[q], total)
        return total

    def mask(hi, p):
        one = jnp.where(hi == float(p), 1.0, 0.0)
        return jnp.concatenate([one, one], axis=0).astype(BF16)

    column = lax.broadcasted_iota(jnp.int32, (256, 128), 0).astype(F32)

    def one_hot(low):
        return jnp.where(column == low, 1.0, 0.0).astype(BF16)

    for half in range(2):
        send_hi, send_lo, recv_hi, recv_lo, recv_weight = (flat(i, half) for i in range(5))
        part = slice(half * 128, half * 128 + 128)
        for j in range(16):
            this = slice(j, j + 1)
            his[j, :, part] = jnp.broadcast_to(send_hi[this], (8, 128))
            ohs[j, :, part] = one_hot(send_lo[this])
            place_in = slice((j % 4) * 256 + half * 128, (j % 4) * 256 + half * 128 + 128)
            hi = jnp.broadcast_to(recv_hi[this], (8, 128))
            hir[j // 4, :, place_in] = hi
            for p in range(32):
                mk[j // 4, p, :, place_in] = mask(hi, p)
            ohr[j // 4, :, place_in] = one_hot(recv_lo[this])
            edge[j // 4, :, place_in] = jnp.broadcast_to(recv_weight[this], (8, 128))
    lane = lanes((1, 128))
    line = lane % 64
    first = (line % 2) * 128
    near, far = jnp.where(lane < 64, 127, 0), jnp.where(lane < 64, 0, 127)
    hi = jnp.broadcast_to((line // 2).astype(F32), (8, 128))
    his[16, :, 0:128] = hi
    for p in range(32):
        mkz[p] = mask(hi, p)
    ohs[16, :, 0:128] = one_hot((first + near).astype(F32))
    ohr[4, :, 0:128] = one_hot((first + far).astype(F32))
    well = wells_ref[...]
    well_x, well_y, well_z = well // 32768, well // 512 % 64, well % 512
    owned = (well_x // 4 == ax) & (well_y // 16 == ay) & (well_z // 128 == az)
    cell = (well_x % 4 * 16 + well_y % 16) * 128 + well_z % 128
    hiw[...] = jnp.broadcast_to(jnp.where(owned, cell // 256, -1).astype(F32), (8, 128))
    ohw[...] = one_hot((cell % 256).astype(F32))

    def begin(i, carry):
        for u in range(4):
            p = 4 * i + u
            for parity in range(2):
                res[p, :, parity * 128 : parity * 128 + 128] = start_ref[
                    pl.ds(2 * p + parity, 16, stride=64), :
                ]
        return carry

    lax.fori_loop(0, 8, begin, 0)
    pair = lax.broadcasted_iota(jnp.int32, (32, 1024), 0).astype(F32)
    total = jnp.zeros((64, 256), F32)
    for j in range(4):
        weight = jnp.broadcast_to(edge[j, 0:1, :], (32, 1024))
        hit = pair == jnp.broadcast_to(hir[j, 0:1, :], (32, 1024))
        high, low = split(jnp.where(hit, weight, 0.0))
        total = total + dot_nt(jnp.concatenate([high, low], axis=0), ohr[j])
    fault = total[0:32] + total[32:64]
    acc[0:32, 0, :] = fault

    for x in range(4):
        tsend[x : x + 1] = ty_ref[x * 16 + 15 : x * 16 + 16]
    tsend[4:8] = jnp.zeros((4, 128), F32)
    pl.semaphore_wait(barrier, 127)
    faces = (
        copy(tx_ref.at[pl.ds(48, 16)], trecv.at[pl.ds(0, 16)], tssem.at[0], trsem.at[0], up_x),
        copy(tsend, trecv.at[pl.ds(16, 8)], tssem.at[1], trsem.at[1], up_y),
        copy(tz_ref, trecv.at[pl.ds(24, 64)], tssem.at[2], trsem.at[2], up_z),
    )
    for face in faces:
        face.start()
    shift = table_ref[0]
    for i in range(1, 16):
        shift = jnp.where(index_ref[0] == i, table_ref[i], shift)
    for face in faces:
        face.wait()
    lane = lanes((16, 128))
    row = lax.broadcasted_iota(jnp.int32, (16, 128), 0)
    inside = [jnp.where(p > 0, 1.0, 0.0) for p in place]
    outside = [jnp.where(p < n - 1, 1.0, 0.0) for p, n in zip(place, (8, 4, 4))]
    for x in range(4):
        these = slice(x * 16, x * 16 + 16)
        upper_x = tx_ref[these] * (outside[0] if x == 3 else 1.0)
        if x == 0:
            lower_x = trecv[0:16] * inside[0]
        else:
            lower_x = tx_ref[(x - 1) * 16 : x * 16]
        ty = ty_ref[these]
        upper_y = jnp.where(row == 15, ty * outside[1], ty)
        lower_y = jnp.where(
            row == 0, trecv[16 + x : 17 + x] * inside[1], pltpu.roll(ty, 1, 0)
        )
        tz = tz_ref[these]
        upper_z = jnp.where(lane == 127, tz * outside[2], tz)
        lower_z = jnp.where(
            lane == 0,
            pltpu.roll(trecv[24 + x * 16 : 40 + x * 16], 1, 1) * inside[2],
            pltpu.roll(tz, 1, 1),
        )
        coef[0, these] = upper_x
        coef[1, these] = lower_x
        coef[2, these] = upper_y
        coef[3, these] = lower_y
        coef[4, these] = upper_z
        coef[5, these] = lower_z
        coef[6, these] = (
            upper_x + lower_x + upper_y + lower_y + upper_z + lower_z + shift * pv_ref[these]
        )
    for p in range(32):
        for parity in range(2):
            r = 2 * p + parity
            coef[6, r : r + 1] += acc[p, 0:1, parity * 128 : parity * 128 + 128]
    coef[7] = 1.0 / coef[6]
    both = jnp.concatenate([coef[5], coef[4]], axis=0).T
    lane = lanes((1, 128))
    edge[4, :, 0:128] = jnp.broadcast_to(
        jnp.where(lane < 64, both[0:1], both[127:128]), (8, 128)
    )
    lane = lanes((64, 128))
    coef[4] = jnp.where(lane == 127, 0.0, coef[4])
    coef[5] = jnp.where(lane == 0, 0.0, coef[5])

    def initial(i, carry):
        for u in range(4):
            p = 4 * i + u
            for parity in range(2):
                part = slice(parity * 128, parity * 128 + 128)
                inverse = jnp.broadcast_to(coef[7, pl.ds(2 * p + parity, 1)], (16, 128))
                d = res[p, :, part] * inverse
                dpad[0, 1 + i // 2, 1 + (i % 2) * 8 + 2 * u + parity] = d
                dbf[p, :, part] = d.astype(BF16)
                xacc[p, :, part] = d
        return carry

    lax.fori_loop(0, 8, initial, 0)

    def pick(source, one_hot, hi_of, width):
        product = jnp.dot(source, one_hot, preferred_element_type=F32)
        tiles = []
        for h in range(width // 128):
            part = slice(h * 128, h * 128 + 128)
            hi = hi_of(part)
            first = jnp.zeros((8, 128), F32)
            second = jnp.zeros((8, 128), F32)
            for p in range(32):
                hit = hi == float(p)
                first = jnp.where(hit, product[p * 16 : p * 16 + 8, part], first)
                second = jnp.where(hit, product[p * 16 + 8 : p * 16 + 16, part], second)
            tiles.append((first, second))
        return tiles

    def gather(j, width):
        return pick(
            dbf[...].reshape(512, 256), ohs[j, :, 0:width], lambda part: his[j, :, part], width
        )

    def scatter(j, tiles):
        values = []
        for h, (first, second) in enumerate(tiles):
            weight = edge[j, :, h * 128 : h * 128 + 128]
            values.append(jnp.concatenate([first * weight, second * weight], axis=0).astype(BF16))
        value = values[0] if len(values) == 1 else jnp.concatenate(values, axis=1)
        masks = mkz if j == 4 else mk.at[j]
        placed = jnp.concatenate([masks[p] * value for p in range(32)], axis=0)
        return dot_nt(placed, ohr[j, :, 0 : 128 * len(tiles)]).reshape(32, 16, 256)

    exchange = copy(gsend.at[pl.ds(0, 127)], grecv.at[pl.ds(0, 127)], gs1, gr1, place)
    spread = copy(gsend.at[pl.ds(0, 127)], gall.at[pl.ds(0, 127)], gs2, gr2, place)

    def permute(t):
        a = lax.broadcasted_iota(jnp.int32, (256, 256), 0)
        b = lax.broadcasted_iota(jnp.int32, (256, 256), 1)
        order = jnp.where(b == a % 16 * 16 + a // 16, 1.0, 0.0).astype(BF16)

        def block(i, carry):
            k = t * 4 + i
            for q in range(2):
                sides = []
                for side in range(2):
                    base = k * 1024 + (2 * q + side) * 16
                    sides.append(
                        jnp.concatenate(
                            [bas[pl.ds(pl.multiple_of(base + 64 * kk, 16), 16), :] for kk in range(16)],
                            axis=0,
                        )
                    )
                turned = jnp.dot(
                    order, jnp.concatenate(sides, axis=1), preferred_element_type=F32
                ).astype(BF16)
                for side in range(2):
                    for xx in range(16):
                        r = (2 * q + side) * 16 + xx
                        bt[r // 2, pl.ds(pl.multiple_of(k * 16, 16), 16), r % 2 * 128 : r % 2 * 128 + 128] = (
                            turned[xx * 16 : xx * 16 + 16, side * 128 : side * 128 + 128]
                        )
            return carry

        lax.fori_loop(0, 4, block, 0)

    def iterate(t, carry):
        now, gain = carry
        par = t % 2
        here = dpad.at[par]
        halos = [
            copy(here.at[4, pl.ds(1, 16)], here.at[0, pl.ds(1, 16)], hssem.at[0], hrsem.at[par, 0], up_x),
            copy(here.at[1, pl.ds(1, 16)], here.at[5, pl.ds(1, 16)], hssem.at[1], hrsem.at[par, 1], down_x),
            copy(here.at[pl.ds(1, 4), 16], here.at[pl.ds(1, 4), 0], hssem.at[2], hrsem.at[par, 2], up_y),
            copy(here.at[pl.ds(1, 4), 1], here.at[pl.ds(1, 4), 17], hssem.at[3], hrsem.at[par, 3], down_y),
        ]
        for halo in halos:
            halo.start()

        def stencil(r):
            x, y = 1 + r // 16, 1 + r % 16
            p, part = r // 2, slice(r % 2 * 128, r % 2 * 128 + 128)
            d = here[x, y]

            def times(which, value):
                return jnp.broadcast_to(coef[which, r : r + 1], (16, 128)) * value

            total = times(4, pltpu.roll(d, 127, 1)) + times(5, pltpu.roll(d, 1, 1))
            for which, inside_too, near in (
                (0, x < 4, (x + 1, y)), (1, x > 1, (x - 1, y)), (2, y < 16, (x, y + 1)), (3, y > 1, (x, y - 1))
            ):
                if inside_too:
                    total = total + times(which, here[near])
            res[p, :, part] = res[p, :, part] - (times(6, d) - total)

        halos_z = [
            copy(zsend.at[0], zrecv.at[par, 0], hssem.at[4], hrsem.at[par, 4], up_z),
            copy(zsend.at[1], zrecv.at[par, 1], hssem.at[5], hrsem.at[par, 5], down_z),
        ]
        for chunk in range(4):
            for j in range(chunk * 4, chunk * 4 + 4):
                for h, (first, second) in enumerate(gather(j, 256)):
                    first, second = half_swap(first, second)
                    first, second = quarter_swap(first), quarter_swap(second)
                    base = j * 8 + h * 4
                    send[base] = first[0:4]
                    send[base + 1] = first[4:8]
                    send[base + 2] = second[0:4]
                    send[base + 3] = second[4:8]
            if chunk == 2:
                ((first, second),) = gather(16, 128)
                first, second = half_swap(first, second)
                zsend[0] = first
                zsend[1] = second
                for halo in halos_z:
                    halo.start()
            for slot in range(chunk * 32, min(chunk * 32 + 32, 127)):
                copy(send.at[slot], recv.at[par, slot], ssem, rsem.at[par, chunk], peer(SLOTS[slot])).start()
        recv[par, 127] = send[127]
        for r in range(64):
            stencil(r)
        @pl.when(t == 0)
        def _():
            fetch.wait()

        @pl.when(t < 4)
        def _():
            permute(t)

        @pl.when(t == 4)
        def _():
            gmat[...] = jnp.zeros_like(gmat)

            def add(i, carry):
                total = gmat[...]
                for u in range(4):
                    total = total + dot_nt(bt[4 * i + u], bt[4 * i + u])
                gmat[...] = total
                return carry

            lax.fori_loop(0, 8, add, 0)

        @pl.when(t == 5)
        def _():
            for c in range(128):
                gsend[c] = gmat[c % 64 * 4 : c % 64 * 4 + 4, c // 64 * 128 : c // 64 * 128 + 128]
            for offset in SLOTS[:127]:
                copy(gsend.at[number(offset)], grecv.at[me], gs1, gr1, peer(offset)).start()
            grecv[me] = gsend[me]

        @pl.when(t == 6)
        def _():
            exchange.wait_recv()
            gsum[...] = jnp.sum(grecv[...], axis=0)
            for offset in SLOTS[:127]:
                copy(gsum, gall.at[me], gs2, gr2, peer(offset)).start()
            gall[me] = gsum[...]

        for halo in halos:
            halo.wait_recv()

        for y in range(16):
            for x, which, beyond in ((0, 1, 0), (3, 0, 5)):
                r = x * 16 + y
                p, part = r // 2, slice(r % 2 * 128, r % 2 * 128 + 128)
                res[p, :, part] += jnp.broadcast_to(coef[which, r : r + 1], (16, 128)) * here[beyond, 1 + y]
        for x in range(4):
            for y, which, beyond in ((0, 3, 0), (15, 2, 17)):
                r = x * 16 + y
                p, part = r // 2, slice(r % 2 * 128, r % 2 * 128 + 128)
                res[p, :, part] += jnp.broadcast_to(coef[which, r : r + 1], (16, 128)) * here[1 + x, beyond]
        for halo in halos_z:
            halo.wait_recv()
        for j in range(4):
            count = 32 if j < 3 else 31
            copy(
                send.at[pl.ds(0, count)], recv.at[par, pl.ds(0, count)], ssem, rsem.at[par, j], place
            ).wait_recv()
            tiles = []
            for h in range(8):
                base = j * 32 + h * 4
                first = jnp.concatenate([recv[par, base], recv[par, base + 1]], axis=0)
                second = jnp.concatenate([recv[par, base + 2], recv[par, base + 3]], axis=0)
                tiles.append(half_swap(quarter_swap(first), quarter_swap(second)))
            if j == 0:
                acc[...] = scatter(4, [half_swap(zrecv[par, 0], zrecv[par, 1])]) + scatter(j, tiles)
            else:
                acc[...] += scatter(j, tiles)

        def update(i, carry):
            for u in range(4):
                p = 4 * i + u
                for parity in range(2):
                    part = slice(parity * 128, parity * 128 + 128)
                    residual = res[p, :, part] + acc[p, :, part]
                    res[p, :, part] = residual
                    inverse = jnp.broadcast_to(coef[7, pl.ds(2 * p + parity, 1)], (16, 128))
                    x, y = 1 + i // 2, 1 + (i % 2) * 8 + 2 * u + parity
                    d = now * here[x, y] + gain * (residual * inverse)
                    dpad[1 - par, x, y] = d
                    dbf[p, :, part] = d.astype(BF16)
                    xacc[p, :, part] += d
            return carry

        lax.fori_loop(0, 8, update, 0)
        for halo in halos + halos_z:
            halo.wait_send()
        copy(send.at[pl.ds(0, 127)], recv.at[par, pl.ds(0, 127)], ssem, rsem.at[par, 0], place).wait_send()
        nxt_now, nxt_gain = carry
        for step in range(TERMS - 2):
            nxt_now = jnp.where(t == step, weights()[step + 1][0], nxt_now)
            nxt_gain = jnp.where(t == step, weights()[step + 1][1], nxt_gain)
        return nxt_now, nxt_gain

    lax.fori_loop(
        0, TERMS - 1, iterate, (jnp.float32(weights()[0][0]), jnp.float32(weights()[0][1]))
    )

    def project(i, total):
        for u in range(4):
            p = 4 * i + u
            high, low = split(xacc[p])
            total = total + dot_nt(jnp.concatenate([high, low], axis=0), bt[p])
        return total

    total = lax.fori_loop(0, 8, project, jnp.zeros((32, 256), F32))
    for c in range(32):
        csend[c] = total[c % 16 * 2 : c % 16 * 2 + 2, c // 16 * 128 : c // 16 * 128 + 128]
    mine = ax * 4 + ay
    for offset in [o for o in SLOTS if o[2] == 0]:
        x, y = xs[offset[0]], ys[offset[1]]
        to = copy(csend.at[x * 4 + y], crecv.at[me], cs1, cr1, (x, y, y))
        if offset[:2] != (0, 0):
            to.start()
        else:

            @pl.when(az != ay)
            def _(to=to):
                to.start()

    spread.wait_recv()
    for c in range(128):
        gmat[c % 64 * 4 : c % 64 * 4 + 4, c // 64 * 128 : c // 64 * 128 + 128] = gall[c]

    @pl.when(az == ay)
    def _():
        crecv[me] = csend[mine]
        copy(crecv.at[pl.ds(0, 127)], crecv.at[pl.ds(0, 127)], cs1, cr1, place).wait_recv()
        csum[...] = jnp.sum(crecv[...], axis=0)
        for offset in SLOTS[:127]:
            copy(csum, call.at[mine], cs2, cr2, peer(offset)).start()
        call[mine] = csum[...]
        copy(call.at[pl.ds(0, 31)], call.at[pl.ds(0, 31)], cs2, cr2, place).wait_recv()

    @pl.when(az != ay)
    def _():
        copy(call, call, cs2, cr2, place).wait_recv()

    for c in range(32):
        cmat[c % 16 * 2 : c % 16 * 2 + 2, c // 16 * 128 : c // 16 * 128 + 128] = call[c]
    leading = cmat[0:16]
    first = leading.astype(BF16)
    second_sum = leading + cmat[16:32] - jnp.dot(
        first.astype(F32), gmat[...], precision=lax.Precision.HIGHEST, preferred_element_type=F32
    )
    both = jnp.concatenate([first, second_sum.astype(BF16)], axis=0)
    first_ref[...] = leading
    coeffs_ref[...] = leading + second_sum

    def subtract(i, total):
        for u in range(4):
            p = 4 * i + u
            taken = jnp.dot(both, bt[p], preferred_element_type=F32)
            left = xacc[p] - taken[0:16] - taken[16:32]
            high, low = split(left)
            parts = jnp.concatenate([high, low], axis=0)
            rest[p] = parts
            total = total + dot_nt(parts, parts)
        return total

    total = lax.fori_loop(0, 8, subtract, jnp.zeros((32, 32), F32))
    gram = total[0:16, 0:16] + total[0:16, 16:32] + total[16:32, 0:16]
    lane = lanes((8, 128))
    wide = jnp.concatenate([gram, jnp.zeros((16, 112), F32)], axis=1)
    row = lax.broadcasted_iota(jnp.int32, (8, 128), 0)
    for half in range(2):
        value = wide[half * 8 : half * 8 + 8]
        line = jnp.zeros((1, 128), F32)
        for i in range(8):
            line = line + pltpu.roll(value[i : i + 1], 16 * i, 1)
        qsend[half : half + 1] = line
    for offset in SLOTS[:127]:
        copy(qsend, qrecv.at[me], qs, qr, peer(offset)).start()
    qrecv[me] = qsend[...]

    ((first_w, second_w),) = pick(
        rest[:, 0:16].reshape(512, 256), ohw[...], lambda part: hiw[...], 128
    )
    ((low_first, low_second),) = pick(
        rest[:, 16:32].reshape(512, 256), ohw[...], lambda part: hiw[...], 128
    )
    packed, _ = half_swap(first_w + low_first, second_w + low_second)
    for c in range(4):
        wsend[c] = packed[2 * c : 2 * c + 2]
    for c in range(4):

        @pl.when(~((ax == 2 * c) & (ay == c) & (az == c)))
        def _(c=c):
            copy(wsend.at[c], wrecv.at[me], ws1, wr1, (2 * c, c, c)).start()

    owner = (ax == 2 * ay) & (az == ay)

    @pl.when(owner)
    def _():
        wrecv[me] = wsend[ay]
        copy(wrecv.at[pl.ds(0, 127)], wrecv.at[pl.ds(0, 127)], ws1, wr1, place).wait_recv()
        wsum[...] = jnp.sum(wrecv[...], axis=0)
        for offset in SLOTS[:127]:
            copy(wsum, wall.at[ay], ws2, wr2, peer(offset)).start()
        wall[ay] = wsum[...]

    copy(qrecv.at[pl.ds(0, 127)], qrecv.at[pl.ds(0, 127)], qs, qr, place).wait_recv()
    sums = jnp.sum(qrecv[...], axis=0)
    pieces = []
    for half in range(2):
        for i in range(8):
            pieces.append(pltpu.roll(sums[half : half + 1], (128 - 16 * i) % 128, 1))
    gram = jnp.concatenate(pieces, axis=0)
    lane = lanes((16, 128))
    row = lax.broadcasted_iota(jnp.int32, (16, 128), 0)
    table = jnp.where(lane < 16, gram, jnp.where(lane == row + 16, 1.0, 0.0))
    for j in range(15):
        column = jnp.broadcast_to(table[:, j : j + 1], (16, 128))
        factor = jnp.where(row > j, column / column[j : j + 1], 0.0)
        table = table - factor * table[j : j + 1]
    pivot = jnp.sum(jnp.where(lane == row, table, 0.0), axis=1, keepdims=True)
    scale = 1024.0 / jnp.sqrt(pivot)
    inverse = table[:, 16:32] * scale
    high, low = split(inverse)
    factors_ref[...] = jnp.concatenate([high, low, high], axis=1)

    @pl.when(owner)
    def _():
        copy(wall.at[pl.ds(0, 3)], wall.at[pl.ds(0, 3)], ws2, wr2, place).wait_recv()

    @pl.when(jnp.logical_not(owner))
    def _():
        copy(wall, wall, ws2, wr2, place).wait_recv()

    packed = jnp.concatenate([wall[c] for c in range(4)], axis=0)
    at_wells = jnp.where(lanes((16, 128)) < 64, jnp.concatenate([packed, pltpu.roll(packed, 64, 1)], axis=0), 0.0)
    answer = jnp.dot(inverse, at_wells, precision=lax.Precision.HIGHEST, preferred_element_type=F32)
    resp_ref[...] = answer[:, 0:64]
    exchange.wait_send()
    copy(gall.at[pl.ds(0, 127)], gall.at[pl.ds(0, 127)], gs2, gr2, place).wait_send()
    copy(qrecv.at[pl.ds(0, 127)], qrecv.at[pl.ds(0, 127)], qs, qr, place).wait_send()

    @pl.when(az == ay)
    def _():
        copy(call.at[pl.ds(0, 31)], call.at[pl.ds(0, 31)], cs1, cr1, place).wait_send()
        copy(crecv.at[pl.ds(0, 127)], crecv.at[pl.ds(0, 127)], cs2, cr2, place).wait_send()

    @pl.when(az != ay)
    def _():
        copy(call, call, cs1, cr1, place).wait_send()

    @pl.when(owner)
    def _():
        copy(wall.at[pl.ds(0, 3)], wall.at[pl.ds(0, 3)], ws1, wr1, place).wait_send()
        copy(wrecv.at[pl.ds(0, 127)], wrecv.at[pl.ds(0, 127)], ws2, wr2, place).wait_send()

    @pl.when(jnp.logical_not(owner))
    def _():
        copy(wall, wall, ws1, wr1, place).wait_send()


def solve(*args):
    vmem = pl.BlockSpec(memory_space=pltpu.VMEM)
    smem = pl.BlockSpec(memory_space=pltpu.SMEM)
    dma = pltpu.SemaphoreType.DMA
    return pl.pallas_call(
        solve_kernel,
        out_shape=(
            jax.ShapeDtypeStruct((32, 32, 256), BF16),
            jax.ShapeDtypeStruct((16, 48), BF16),
            jax.ShapeDtypeStruct((16, 256), F32),
            jax.ShapeDtypeStruct((16, 256), F32),
            jax.ShapeDtypeStruct((16, 64), F32),
        ),
        in_specs=[vmem, pl.BlockSpec(memory_space=pl.ANY)] + [vmem] * 4 + [smem] * 2 + [vmem] * 5,
        out_specs=(vmem,) * 5,
        scratch_shapes=[
            pltpu.VMEM((2, 6, 18, 16, 128), F32),
            pltpu.VMEM((32, 16, 256), BF16),
            pltpu.VMEM((32, 16, 256), F32),
            pltpu.VMEM((32, 16, 256), F32),
            pltpu.VMEM((32, 16, 256), F32),
            pltpu.VMEM((17, 256, 256), BF16),
            pltpu.VMEM((5, 256, 1024), BF16),
            pltpu.VMEM((17, 8, 256), F32),
            pltpu.VMEM((4, 8, 1024), F32),
            pltpu.VMEM((4, 32, 16, 1024), BF16),
            pltpu.VMEM((32, 16, 128), BF16),
            pltpu.VMEM((128, 4, 128), F32),
            pltpu.VMEM((2, 128, 4, 128), F32),
            pltpu.VMEM((2, 8, 128), F32),
            pltpu.VMEM((2, 2, 8, 128), F32),
            pltpu.VMEM((8, 64, 128), F32),
            pltpu.VMEM((5, 8, 1024), F32),
            pltpu.VMEM((5, 128, 128), F32),
            pltpu.VMEM((8, 128), F32),
            pltpu.VMEM((88, 128), F32),
            pltpu.VMEM((16384, 128), BF16),
            pltpu.VMEM((32, 256, 256), BF16),
            pltpu.VMEM((256, 256), F32),
            pltpu.VMEM((128, 4, 128), F32),
            pltpu.VMEM((128, 4, 128), F32),
            pltpu.VMEM((128, 4, 128), F32),
            pltpu.VMEM((4, 128), F32),
            pltpu.VMEM((32, 2, 128), F32),
            pltpu.VMEM((128, 2, 128), F32),
            pltpu.VMEM((32, 2, 128), F32),
            pltpu.VMEM((2, 128), F32),
            pltpu.VMEM((2, 128), F32),
            pltpu.VMEM((128, 2, 128), F32),
            pltpu.VMEM((4, 2, 128), F32),
            pltpu.VMEM((128, 2, 128), F32),
            pltpu.VMEM((4, 2, 128), F32),
            pltpu.VMEM((2, 128), F32),
            pltpu.VMEM((256, 128), BF16),
            pltpu.VMEM((8, 128), F32),
            pltpu.VMEM((32, 256), F32),
            dma,
            dma((2, 4)),
            dma((6,)),
            dma((2, 6)),
            dma((3,)),
            dma((3,)),
        ]
        + [dma] * 15,
        compiler_params=pltpu.CompilerParams(
            collective_id=0, has_side_effects=True, vmem_limit_bytes=60 * 1024 * 1024
        ),
    )(*args)


def finish_kernel(
    rest_ref, factors_ref, first_in, coeffs_in, resp_in, out_ref, first_ref, coeffs_ref, resp_ref
):
    first_ref[...] = first_in[...]
    coeffs_ref[...] = coeffs_in[...]
    resp_ref[...] = resp_in[...]
    factors = factors_ref[...]

    def finish(i, carry):
        for u in range(4):
            p = 4 * i + u
            parts = rest_ref[p]
            block = jnp.dot(
                factors, jnp.concatenate([parts[0:16], parts[0:16], parts[16:32]], axis=0),
                preferred_element_type=F32,
            )
            for parity in range(2):
                out_ref[pl.ds(2 * p + parity, 16, stride=64), :] = block[
                    :, parity * 128 : parity * 128 + 128
                ]
        return carry

    lax.fori_loop(0, 8, finish, 0)


def finish(*args):
    vmem = pl.BlockSpec(memory_space=pltpu.VMEM)
    return pl.pallas_call(
        finish_kernel,
        out_shape=(
            jax.ShapeDtypeStruct((1024, 128), F32),
            jax.ShapeDtypeStruct((16, 256), F32),
            jax.ShapeDtypeStruct((16, 256), F32),
            jax.ShapeDtypeStruct((16, 64), F32),
        ),
        in_specs=[vmem] * 5,
        out_specs=(vmem,) * 4,
    )(*args)


def local(
    start_block, basis, trans_x, trans_y, trans_z, pore_volume, shift_table, shift_index,
    fault_send, fault_recv, fault_trans, well_cells,
):
    wells = jnp.concatenate([well_cells, well_cells]).reshape(1, 128)
    offsets = np.zeros((8, 128), np.int32)
    offsets[0:3] = np.array(SLOTS, np.int32).T
    parts = solve(
        start_block.reshape(1024, 128),
        basis.reshape(16384, 128),
        trans_x.reshape(64, 128),
        trans_y.reshape(64, 128),
        trans_z.reshape(64, 128),
        pore_volume.reshape(64, 128),
        shift_table,
        shift_index,
        fault_send[0].T,
        fault_recv[0].T,
        fault_trans[0].T,
        wells,
        jnp.asarray(offsets),
    )
    new_block, first_coeffs, coeffs, well_resp = finish(*parts)
    return new_block.reshape(start_block.shape), first_coeffs.T, coeffs.T, well_resp.T


def solution(mesh):
    in_specs = (
        P(None, "gx", "gy", "gz"),
        P(None, "gx", "gy", "gz"),
        P("gx", "gy", "gz"),
        P("gx", "gy", "gz"),
        P("gx", "gy", "gz"),
        P("gx", "gy", "gz"),
        P(),
        P(),
        P(("gx", "gy", "gz"), None, None),
        P(("gx", "gy", "gz"), None, None),
        P(("gx", "gy", "gz"), None, None),
        P(),
    )
    out_specs = (P(None, "gx", "gy", "gz"), P(), P(), P())
    return jax.shard_map(local, mesh=mesh, in_specs=in_specs, out_specs=out_specs, check_vma=False)
```

```python
import functools
import math

import jax
import jax.numpy as jnp
import numpy as np
from jax import lax
from jax.experimental import pallas as pl
from jax.experimental.pallas import tpu as pltpu
from jax.sharding import PartitionSpec as P

TERMS = 8
MESH = pl.DeviceIdType.MESH
F32 = jnp.float32
BF16 = jnp.bfloat16
SIGMA = 1.0 / 0.9


def weights():
    now = 1.0 / SIGMA
    table = []
    for _ in range(TERMS - 1):
        new = 1.0 / (2.0 * SIGMA - now)
        table.append((new * now, 2.0 * new / 0.9))
        now = new
    return table


def far_first():
    along = {8: (0.0, 0.5, 1.0, 1.5, 2.0, 1.5, 1.0, 0.5), 4: (0.0, 1.0, 2.0, 1.0)}
    every = [(x, y, z) for x in range(8) for y in range(4) for z in range(4)]
    return sorted(every, key=lambda o: -(along[8][o[0]] + along[4][o[1]] + along[4][o[2]]))


SLOTS = far_first()


def lanes(shape):
    return lax.broadcasted_iota(jnp.int32, shape, len(shape) - 1)


def half_swap(first, second):
    low = lanes(first.shape) < 64
    return (
        jnp.where(low, first, pltpu.roll(second, 64, 1)),
        jnp.where(low, pltpu.roll(first, 64, 1), second),
    )


def quarter_swap(value):
    upper = lax.broadcasted_iota(jnp.int32, value.shape, 0) // 4
    odd = lanes(value.shape) // 32 % 2
    moved = jnp.where(upper == 0, pltpu.roll(value, 96, 1), pltpu.roll(value, 32, 1))
    return jnp.where(upper == odd, value, pltpu.roll(moved, 4, 0))


def split(value):
    high = value.astype(BF16)
    return high, (value - high.astype(F32)).astype(BF16)


def dot_nt(a, b, **kw):
    return lax.dot_general(a, b, (((1,), (1,)), ((), ())), preferred_element_type=F32, **kw)


def solve_kernel(
    start_ref, basis_ref, tx_ref, ty_ref, tz_ref, pv_ref, table_ref, index_ref, fs_ref, fr_ref, ft_ref, wells_ref, offs_ref,
    rest, factors_ref, first_ref, coeffs_ref, resp_ref,
    dpad, dbf, res, xacc, acc, ohs, ohr, his, hir, mk, send, recv, zsend, zrecv, coef, edge,
    rows, tsend, trecv, bas, bt, gmat, gfull, gsend, grecv, gall, gsum, csend, crecv, call, csum,
    qsend, qrecv, wsend, wrecv, wall, wsum, ohw, hiw, cmat,
    ssem, rsem, hssem, hrsem, tssem, trsem, bsem, gs1, gr1, gs2, gr2, cs1, cr1, cs2, cr2,
    qs, qr, ws1, wr1, ws2, wr2,
):
    ax, ay, az = lax.axis_index("gx"), lax.axis_index("gy"), lax.axis_index("gz")
    place = (ax, ay, az)
    me = ax * 16 + ay * 4 + az
    xs = [(ax + i) % 8 for i in range(8)]
    ys = [(ay + i) % 4 for i in range(4)]
    zs = [(az + i) % 4 for i in range(4)]

    def peer(offset):
        return (xs[offset[0] % 8], ys[offset[1] % 4], zs[offset[2] % 4])

    def number(offset):
        x, y, z = peer(offset)
        return x * 16 + y * 4 + z

    up_x, down_x = peer((1, 0, 0)), peer((7, 0, 0))
    up_y, down_y = peer((0, 1, 0)), peer((0, 3, 0))
    up_z, down_z = peer((0, 0, 1)), peer((0, 0, 3))

    def copy(src, dst, ss, rs, where):
        return pltpu.make_async_remote_copy(
            src_ref=src, dst_ref=dst, send_sem=ss, recv_sem=rs, device_id=where, device_id_type=MESH
        )

    barrier = pltpu.get_barrier_semaphore()
    for offset in SLOTS[:127]:
        pl.semaphore_signal(barrier, inc=1, device_id=peer(offset), device_id_type=MESH)
    fetch = pltpu.make_async_copy(basis_ref, bas, bsem)
    fetch.start()

    offs = offs_ref[...]
    spot = lax.broadcasted_iota(jnp.int32, (128, 128), 0)

    def order_of(sign):
        x, y, z = (offs[i : i + 1] * sign for i in range(3))
        target = (x + ax + 8) % 8 * 16 + (y + ay + 4) % 4 * 4 + (z + az + 4) % 4
        return jnp.where(spot == target, 1.0, 0.0).astype(BF16)

    def spread_rows(which, value):
        rows[which] = jnp.concatenate([value] * 4, axis=0).T

    def halves(ref, order, which):
        cells = ref[...]
        parts = jnp.concatenate([cells // 256, cells % 256], axis=0).astype(F32).astype(BF16)
        moved = jnp.dot(parts, order, preferred_element_type=F32)
        spread_rows(which, moved[0:32])
        spread_rows(which + 1, moved[32:64])

    halves(fs_ref, order_of(1), 0)
    source_order = order_of(-1)
    halves(fr_ref, source_order, 2)
    high, low = split(ft_ref[...])
    lowest = (ft_ref[...] - high.astype(F32) - low.astype(F32)).astype(BF16)
    moved = jnp.dot(
        jnp.concatenate([high, low, lowest], axis=0), source_order, preferred_element_type=F32
    )
    spread_rows(4, moved[0:32] + moved[32:64] + moved[64:96])

    def flat(which, half):
        lane = lanes((16, 128))
        pieces = [rows[which, pl.ds(half * 4 + q, 16, stride=8), :] for q in range(4)]
        total = pieces[0]
        for q in range(1, 4):
            total = jnp.where(lane // 32 == q, pieces[q], total)
        return total

    def mask(hi, p):
        one = jnp.where(hi == float(p), 1.0, 0.0)
        return jnp.concatenate([one, one], axis=0).astype(BF16)

    column = lax.broadcasted_iota(jnp.int32, (256, 128), 0).astype(F32)

    def one_hot(low):
        return jnp.where(column == low, 1.0, 0.0).astype(BF16)

    for half in range(2):
        send_hi, send_lo, recv_hi, recv_lo, recv_weight = (flat(i, half) for i in range(5))
        part = slice(half * 128, half * 128 + 128)
        for j in range(16):
            this = slice(j, j + 1)
            quad = jnp.floor(send_hi[this] * 0.5)
            his[j, :, part] = jnp.broadcast_to(quad, (8, 128))
            low = send_lo[this] + (send_hi[this] - 2.0 * quad) * 256.0
            ohs[j, half, 0:256] = one_hot(low)
            ohs[j, half, 256:512] = one_hot(low - 256.0)
            place_in = slice((j % 4) * 256 + half * 128, (j % 4) * 256 + half * 128 + 128)
            hi = jnp.broadcast_to(recv_hi[this], (8, 128))
            hir[j // 4, :, place_in] = hi
            for p in range(32):
                mk[2 * j + half, p] = mask(hi, p)
            ohr[2 * j + half] = one_hot(recv_lo[this])
            edge[j // 4, :, place_in] = jnp.broadcast_to(recv_weight[this], (8, 128))
    lane = lanes((1, 128))
    line = lane % 64
    first = (line % 2) * 128
    near, far = jnp.where(lane < 64, 127, 0), jnp.where(lane < 64, 0, 127)
    hi = jnp.broadcast_to((line // 2).astype(F32), (8, 128))
    for p in range(32):
        mk[32, p] = mask(hi, p)
    ohr[32] = one_hot((first + far).astype(F32))
    his[16, :, 0:128] = jnp.broadcast_to((line // 4).astype(F32), (8, 128))
    low = ((line % 4) * 128 + near).astype(F32)
    ohs[16, 0, 0:256] = one_hot(low)
    ohs[16, 0, 256:512] = one_hot(low - 256.0)
    well = wells_ref[...]
    well_x, well_y, well_z = well // 32768, well // 512 % 64, well % 512
    owned = (well_x // 4 == ax) & (well_y // 16 == ay) & (well_z // 128 == az)
    cell = (well_x % 4 * 16 + well_y % 16) * 128 + well_z % 128
    hiw[...] = jnp.broadcast_to(jnp.where(owned, cell // 256, -1).astype(F32), (8, 128))
    ohw[...] = one_hot((cell % 256).astype(F32))

    def begin(i, carry):
        for u in range(4):
            p = 4 * i + u
            for parity in range(2):
                res[p, :, parity * 128 : parity * 128 + 128] = start_ref[
                    pl.ds(2 * p + parity, 16, stride=64), :
                ]
        return carry

    lax.fori_loop(0, 8, begin, 0)
    pair = lax.broadcasted_iota(jnp.int32, (32, 1024), 0).astype(F32)
    total = jnp.zeros((64, 256), F32)
    for j in range(4):
        weight = jnp.broadcast_to(edge[j, 0:1, :], (32, 1024))
        hit = pair == jnp.broadcast_to(hir[j, 0:1, :], (32, 1024))
        high, low = split(jnp.where(hit, weight, 0.0))
        total = total + dot_nt(
            jnp.concatenate([high, low], axis=0),
            jnp.concatenate([ohr[8 * j + h] for h in range(8)], axis=1),
        )
    fault = total[0:32] + total[32:64]
    acc[0:32, 0, :] = fault

    for x in range(4):
        tsend[x : x + 1] = ty_ref[x * 16 + 15 : x * 16 + 16]
    tsend[4:8] = jnp.zeros((4, 128), F32)
    pl.semaphore_wait(barrier, 127)
    faces = (
        copy(tx_ref.at[pl.ds(48, 16)], trecv.at[pl.ds(0, 16)], tssem.at[0], trsem.at[0], up_x),
        copy(tsend, trecv.at[pl.ds(16, 8)], tssem.at[1], trsem.at[1], up_y),
        copy(tz_ref, trecv.at[pl.ds(24, 64)], tssem.at[2], trsem.at[2], up_z),
    )
    for face in faces:
        face.start()
    shift = table_ref[0]
    for i in range(1, 16):
        shift = jnp.where(index_ref[0] == i, table_ref[i], shift)
    for face in faces:
        face.wait()
    lane = lanes((16, 128))
    row = lax.broadcasted_iota(jnp.int32, (16, 128), 0)
    inside = [jnp.where(p > 0, 1.0, 0.0) for p in place]
    outside = [jnp.where(p < n - 1, 1.0, 0.0) for p, n in zip(place, (8, 4, 4))]
    for x in range(4):
        these = slice(x * 16, x * 16 + 16)
        upper_x = tx_ref[these] * (outside[0] if x == 3 else 1.0)
        if x == 0:
            lower_x = trecv[0:16] * inside[0]
        else:
            lower_x = tx_ref[(x - 1) * 16 : x * 16]
        ty = ty_ref[these]
        upper_y = jnp.where(row == 15, ty * outside[1], ty)
        lower_y = jnp.where(
            row == 0, trecv[16 + x : 17 + x] * inside[1], pltpu.roll(ty, 1, 0)
        )
        tz = tz_ref[these]
        upper_z = jnp.where(lane == 127, tz * outside[2], tz)
        lower_z = jnp.where(
            lane == 0,
            pltpu.roll(trecv[24 + x * 16 : 40 + x * 16], 1, 1) * inside[2],
            pltpu.roll(tz, 1, 1),
        )
        coef[0, these] = upper_x
        coef[1, these] = lower_x
        coef[2, these] = upper_y
        coef[3, these] = lower_y
        coef[4, these] = upper_z
        coef[5, these] = lower_z
        coef[6, these] = (
            upper_x + lower_x + upper_y + lower_y + upper_z + lower_z + shift * pv_ref[these]
        )
    for p in range(32):
        for parity in range(2):
            r = 2 * p + parity
            coef[6, r : r + 1] += acc[p, 0:1, parity * 128 : parity * 128 + 128]
    coef[7] = 1.0 / coef[6]
    both = jnp.concatenate([coef[5], coef[4]], axis=0).T
    lane = lanes((1, 128))
    edge[4, :, 0:128] = jnp.broadcast_to(
        jnp.where(lane < 64, both[0:1], both[127:128]), (8, 128)
    )
    lane = lanes((64, 128))
    coef[4] = jnp.where(lane == 127, 0.0, coef[4])
    coef[5] = jnp.where(lane == 0, 0.0, coef[5])

    def initial(i, carry):
        for u in range(4):
            p = 4 * i + u
            for parity in range(2):
                part = slice(parity * 128, parity * 128 + 128)
                inverse = jnp.broadcast_to(coef[7, pl.ds(2 * p + parity, 1)], (16, 128))
                d = res[p, :, part] * inverse
                dpad[0, 1 + i // 2, 1 + (i % 2) * 8 + 2 * u + parity] = d
                dbf[u % 2 * 2 + parity, pl.ds(pl.multiple_of((2 * i + u // 2) * 16, 16), 16)] = d.astype(BF16)
                xacc[p, :, part] = jnp.zeros_like(d)
        return carry

    lax.fori_loop(0, 8, initial, 0)

    def pick(source, one_hot, hi_of, width, count):
        product = jnp.dot(source, one_hot, preferred_element_type=F32)
        tiles = []
        for h in range(width // 128):
            part = slice(h * 128, h * 128 + 128)
            hi = hi_of(part)
            first = jnp.zeros((8, 128), F32)
            second = jnp.zeros((8, 128), F32)
            for p in range(count):
                hit = hi == float(p)
                first = jnp.where(hit, product[p * 16 : p * 16 + 8, part], first)
                second = jnp.where(hit, product[p * 16 + 8 : p * 16 + 16, part], second)
            tiles.append((first, second))
        return tiles

    def gather(j, width):
        picks = [ohs[j, h] for h in range(width // 128)]
        return pick(
            jnp.concatenate([dbf[q] for q in range(4)], axis=1),
            picks[0] if len(picks) == 1 else jnp.concatenate(picks, axis=1),
            lambda part: his[j, :, part], width, 16,
        )

    def scatter(j, tiles):
        values = []
        for h, (first, second) in enumerate(tiles):
            weight = edge[j, :, h * 128 : h * 128 + 128]
            values.append(jnp.concatenate([first * weight, second * weight], axis=0).astype(BF16))
        picks = [ohr[8 * j + h] for h in range(len(values))]
        picks = picks[0] if len(picks) == 1 else jnp.concatenate(picks, axis=1)
        sums = []
        for side in range(2):
            placed = [
                jnp.concatenate([mk[8 * j + h, side * 16 + p] * value for p in range(16)], axis=0)
                for h, value in enumerate(values)
            ]
            placed = placed[0] if len(placed) == 1 else jnp.concatenate(placed, axis=1)
            sums.append(dot_nt(placed, picks).reshape(16, 16, 256))
        return sums

    exchange = copy(gsend.at[pl.ds(0, 127)], grecv.at[pl.ds(0, 127)], gs1, gr1, place)
    spread = copy(gsend.at[pl.ds(0, 127)], gall.at[pl.ds(0, 127)], gs2, gr2, place)

    def permute(t):
        a = lax.broadcasted_iota(jnp.int32, (256, 256), 0)
        b = lax.broadcasted_iota(jnp.int32, (256, 256), 1)
        order = jnp.where(b == a % 16 * 16 + a // 16, 1.0, 0.0).astype(BF16)

        def block(i, carry):
            k = t * 6 + i
            for q in range(2):
                sides = []
                for side in range(2):
                    base = k * 1024 + (2 * q + side) * 16
                    sides.append(
                        jnp.concatenate(
                            [bas[pl.ds(pl.multiple_of(base + 64 * kk, 16), 16), :] for kk in range(16)],
                            axis=0,
                        )
                    )
                turned = jnp.dot(
                    order, jnp.concatenate(sides, axis=1), preferred_element_type=F32
                ).astype(BF16)
                for side in range(2):
                    for xx in range(16):
                        r = (2 * q + side) * 16 + xx
                        bt[r // 2, pl.ds(pl.multiple_of(k * 16, 16), 16), r % 2 * 128 : r % 2 * 128 + 128] = (
                            turned[xx * 16 : xx * 16 + 16, side * 128 : side * 128 + 128]
                        )
            return carry

        lax.fori_loop(0, jnp.where(t < 2, 6, 4), block, 0)

    def iterate(t, carry):
        now, gain = carry
        par = t % 2
        here = dpad.at[par]
        halos = [
            copy(here.at[4, pl.ds(1, 16)], here.at[0, pl.ds(1, 16)], hssem.at[0], hrsem.at[par, 0], up_x),
            copy(here.at[1, pl.ds(1, 16)], here.at[5, pl.ds(1, 16)], hssem.at[1], hrsem.at[par, 1], down_x),
            copy(here.at[pl.ds(1, 4), 16], here.at[pl.ds(1, 4), 0], hssem.at[2], hrsem.at[par, 2], up_y),
            copy(here.at[pl.ds(1, 4), 1], here.at[pl.ds(1, 4), 17], hssem.at[3], hrsem.at[par, 3], down_y),
        ]
        for halo in halos:
            halo.start()

        def stencil(r):
            x, y = 1 + r // 16, 1 + r % 16
            p, part = r // 2, slice(r % 2 * 128, r % 2 * 128 + 128)
            d = here[x, y]
            xacc[p, :, part] += d

            def times(which, value):
                return jnp.broadcast_to(coef[which, r : r + 1], (16, 128)) * value

            total = times(4, pltpu.roll(d, 127, 1)) + times(5, pltpu.roll(d, 1, 1))
            for which, inside_too, near in (
                (0, x < 4, (x + 1, y)), (1, x > 1, (x - 1, y)), (2, y < 16, (x, y + 1)), (3, y > 1, (x, y - 1))
            ):
                if inside_too:
                    total = total + times(which, here[near])
            res[p, :, part] = res[p, :, part] - (times(6, d) - total)

        halos_z = [
            copy(zsend.at[0], zrecv.at[par, 0], hssem.at[4], hrsem.at[par, 4], up_z),
            copy(zsend.at[1], zrecv.at[par, 1], hssem.at[5], hrsem.at[par, 5], down_z),
        ]
        for group in (range(0, 2), range(2, 8), range(8, 16)):
            for j in group:
                for h, (first, second) in enumerate(gather(j, 256)):
                    first, second = half_swap(first, second)
                    first, second = quarter_swap(first), quarter_swap(second)
                    base = j * 8 + h * 4
                    send[base] = first[0:4]
                    send[base + 1] = first[4:8]
                    send[base + 2] = second[0:4]
                    send[base + 3] = second[4:8]
            if group[0] == 8:
                ((first, second),) = gather(16, 128)
                first, second = half_swap(first, second)
                zsend[0] = first
                zsend[1] = second
                for halo in halos_z:
                    halo.start()
            for slot in range(group[0] * 8, min(group[-1] * 8 + 8, 127)):
                copy(
                    send.at[slot], recv.at[par, slot], ssem, rsem.at[par, slot // 32], peer(SLOTS[slot])
                ).start()
        recv[par, 127] = send[127]
        for r in range(64):
            stencil(r)
        @pl.when(t == 0)
        def _():
            fetch.wait()

        @pl.when(t < 3)
        def _():
            permute(t)

        @pl.when(t == 3)
        def _():
            gfull[...] = jnp.zeros_like(gfull)

            def add(i, carry):
                total = gfull[...]
                for u in range(4):
                    total = total + dot_nt(bt[4 * i + u], bt[4 * i + u])
                gfull[...] = total
                return carry

            lax.fori_loop(0, 8, add, 0)
            gmat[0] = gfull[0:128, 0:128]
            gmat[1] = gfull[0:128, 128:256]
            gmat[2] = gfull[128:256, 128:256]

        @pl.when(t == 4)
        def _():
            gfull[:, 0:128] = jnp.zeros((256, 128), F32)

            def at_wells(i, carry):
                total = gfull[:, 0:128]
                for u in range(4):
                    p = 4 * i + u
                    hit = hiw[0:1] == lax.convert_element_type(p, F32)
                    found = jnp.dot(bt[p], ohw[...], preferred_element_type=F32)
                    total = total + jnp.where(hit, found, 0.0)
                gfull[:, 0:128] = total
                return carry

            lax.fori_loop(0, 8, at_wells, 0)
            gmat[3] = jnp.where(
                lanes((128, 128)) < 64, gfull[0:128, 0:128], gfull[128:256, 0:128]
            )

        @pl.when(t == 5)
        def _():
            for c in range(128):
                gsend[c] = gmat[c // 32, c % 32 * 4 : c % 32 * 4 + 4]
            for offset in SLOTS[:127]:
                copy(gsend.at[number(offset)], grecv.at[me], gs1, gr1, peer(offset)).start()
            grecv[me] = gsend[me]

        @pl.when(t == 6)
        def _():
            exchange.wait_recv()
            gsum[...] = jnp.sum(grecv[...], axis=0)
            for offset in SLOTS[:127]:
                copy(gsum, gall.at[me], gs2, gr2, peer(offset)).start()
            gall[me] = gsum[...]

        for halo in halos:
            halo.wait_recv()

        for y in range(16):
            for x, which, beyond in ((0, 1, 0), (3, 0, 5)):
                r = x * 16 + y
                p, part = r // 2, slice(r % 2 * 128, r % 2 * 128 + 128)
                res[p, :, part] += jnp.broadcast_to(coef[which, r : r + 1], (16, 128)) * here[beyond, 1 + y]
        for x in range(4):
            for y, which, beyond in ((0, 3, 0), (15, 2, 17)):
                r = x * 16 + y
                p, part = r // 2, slice(r % 2 * 128, r % 2 * 128 + 128)
                res[p, :, part] += jnp.broadcast_to(coef[which, r : r + 1], (16, 128)) * here[1 + x, beyond]
        for halo in halos_z:
            halo.wait_recv()
        for side, value in enumerate(scatter(4, [half_swap(zrecv[par, 0], zrecv[par, 1])])):
            acc[side * 16 : side * 16 + 16] = value
        for j in (3, 2, 1, 0):
            count = 32 if j < 3 else 31
            copy(
                send.at[pl.ds(0, count)], recv.at[par, pl.ds(0, count)], ssem, rsem.at[par, j], place
            ).wait_recv()
            tiles = []
            for h in range(8):
                base = j * 32 + h * 4
                first = jnp.concatenate([recv[par, base], recv[par, base + 1]], axis=0)
                second = jnp.concatenate([recv[par, base + 2], recv[par, base + 3]], axis=0)
                tiles.append(half_swap(quarter_swap(first), quarter_swap(second)))
            sums = scatter(j, tiles)
            if j:
                for side, value in enumerate(sums):
                    acc[side * 16 : side * 16 + 16] += value
        for r in range(64):
            p, part = r // 2, slice(r % 2 * 128, r % 2 * 128 + 128)
            residual = res[p, :, part] + acc[p, :, part] + sums[p // 16][p % 16, :, part]
            res[p, :, part] = residual
            inverse = jnp.broadcast_to(coef[7, r : r + 1], (16, 128))
            x, y = 1 + r // 16, 1 + r % 16
            d = now * here[x, y] + gain * (residual * inverse)
            dpad[1 - par, x, y] = d
            dbf[r % 4, r // 4 * 16 : r // 4 * 16 + 16] = d.astype(BF16)
        for halo in halos + halos_z:
            halo.wait_send()
        copy(send.at[pl.ds(0, 127)], recv.at[par, pl.ds(0, 127)], ssem, rsem.at[par, 0], place).wait_send()
        nxt_now, nxt_gain = carry
        for step in range(TERMS - 2):
            nxt_now = jnp.where(t == step, weights()[step + 1][0], nxt_now)
            nxt_gain = jnp.where(t == step, weights()[step + 1][1], nxt_gain)
        return nxt_now, nxt_gain

    lax.fori_loop(
        0, TERMS - 1, iterate, (jnp.float32(weights()[0][0]), jnp.float32(weights()[0][1]))
    )

    def project(i, total):
        for u in range(8):
            p = 8 * i + u
            d = jnp.concatenate([dpad[1, 1 + i, 1 + 2 * u], dpad[1, 1 + i, 2 + 2 * u]], axis=1)
            x = xacc[p] + d
            xacc[p] = x
            high, low = split(x)
            parts = jnp.concatenate([high, low], axis=0)
            rest[p] = parts
            total = total + dot_nt(parts, bt[p])
        return total

    total = lax.fori_loop(0, 4, project, jnp.zeros((32, 256), F32))
    for c in range(32):
        csend[c] = total[c % 16 * 2 : c % 16 * 2 + 2, c // 16 * 128 : c // 16 * 128 + 128]
    mine = ax * 4 + ay
    for offset in [o for o in SLOTS if o[2] == 0]:
        x, y = xs[offset[0]], ys[offset[1]]
        to = copy(csend.at[x * 4 + y], crecv.at[me], cs1, cr1, (x, y, y))
        if offset[:2] != (0, 0):
            to.start()
        else:

            @pl.when(az != ay)
            def _(to=to):
                to.start()

    ((first_w, second_w),) = pick(
        rest[:, 0:16].reshape(512, 256), ohw[...], lambda part: hiw[...], 128, 32
    )
    ((low_first, low_second),) = pick(
        rest[:, 16:32].reshape(512, 256), ohw[...], lambda part: hiw[...], 128, 32
    )
    packed, _ = half_swap(first_w + low_first, second_w + low_second)
    for c in range(4):
        wsend[c] = packed[2 * c : 2 * c + 2]
    for c in range(4):

        @pl.when(~((ax == 2 * c) & (ay == c) & (az == (c + 1) % 4)))
        def _(c=c):
            copy(wsend.at[c], wrecv.at[me], ws1, wr1, (2 * c, c, (c + 1) % 4)).start()

    owner = (ax == 2 * ay) & (az == (ay + 1) % 4)

    @pl.when(owner)
    def _():
        wrecv[me] = wsend[ay]
        copy(wrecv.at[pl.ds(0, 127)], wrecv.at[pl.ds(0, 127)], ws1, wr1, place).wait_recv()
        wsum[...] = jnp.sum(wrecv[...], axis=0)
        for offset in SLOTS[:127]:
            copy(wsum, wall.at[ay], ws2, wr2, peer(offset)).start()
        wall[ay] = wsum[...]

    spread.wait_recv()
    for c in range(128):
        gmat[c // 32, c % 32 * 4 : c % 32 * 4 + 4] = gall[c]

    @pl.when(az == ay)
    def _():
        crecv[me] = csend[mine]
        copy(crecv.at[pl.ds(0, 127)], crecv.at[pl.ds(0, 127)], cs1, cr1, place).wait_recv()
        csum[...] = jnp.sum(crecv[...], axis=0)
        for offset in SLOTS[:127]:
            copy(csum, call.at[mine], cs2, cr2, peer(offset)).start()
        call[mine] = csum[...]
        copy(call.at[pl.ds(0, 31)], call.at[pl.ds(0, 31)], cs2, cr2, place).wait_recv()

    @pl.when(az != ay)
    def _():
        copy(call, call, cs2, cr2, place).wait_recv()

    for c in range(32):
        cmat[c % 16 * 2 : c % 16 * 2 + 2, c // 16 * 128 : c // 16 * 128 + 128] = call[c]
    leading = cmat[0:16]
    first = leading.astype(BF16)
    exact = dict(precision=lax.Precision.HIGHEST)
    wide = first.astype(F32)
    near, far = wide[:, 0:128], wide[:, 128:256]
    taken = jnp.concatenate(
        [
            jnp.dot(near, gmat[0], preferred_element_type=F32, **exact) + dot_nt(far, gmat[1], **exact),
            jnp.dot(near, gmat[1], preferred_element_type=F32, **exact)
            + jnp.dot(far, gmat[2], preferred_element_type=F32, **exact),
        ],
        axis=1,
    )
    second_sum = leading + cmat[16:32] - taken
    both = jnp.concatenate([first, second_sum.astype(BF16)], axis=0)
    first_ref[...] = leading
    coeffs_ref[...] = leading + second_sum

    def subtract(i, total):
        for u in range(8):
            p = 8 * i + u
            taken = jnp.dot(both, bt[p], preferred_element_type=F32)
            left = xacc[p] - taken[0:16] - taken[16:32]
            high, low = split(left)
            parts = jnp.concatenate([high, low], axis=0)
            rest[p] = parts
            total = total + dot_nt(parts, parts)
        return total

    total = lax.fori_loop(0, 4, subtract, jnp.zeros((32, 32), F32))
    gram = total[0:16, 0:16] + total[0:16, 16:32] + total[16:32, 0:16]
    lane = lanes((8, 128))
    wide = jnp.concatenate([gram, jnp.zeros((16, 112), F32)], axis=1)
    row = lax.broadcasted_iota(jnp.int32, (8, 128), 0)
    for half in range(2):
        value = wide[half * 8 : half * 8 + 8]
        line = jnp.zeros((1, 128), F32)
        for i in range(8):
            line = line + pltpu.roll(value[i : i + 1], 16 * i, 1)
        qsend[half : half + 1] = line
    for offset in SLOTS[:127]:
        copy(qsend, qrecv.at[me], qs, qr, peer(offset)).start()
    qrecv[me] = qsend[...]

    copy(qrecv.at[pl.ds(0, 127)], qrecv.at[pl.ds(0, 127)], qs, qr, place).wait_recv()
    sums = jnp.sum(qrecv[...], axis=0)
    pieces = []
    for half in range(2):
        for i in range(8):
            pieces.append(pltpu.roll(sums[half : half + 1], (128 - 16 * i) % 128, 1))
    gram = jnp.concatenate(pieces, axis=0)
    lane = lanes((16, 128))
    row = lax.broadcasted_iota(jnp.int32, (16, 128), 0)
    table = jnp.where(lane < 16, gram, jnp.where(lane == row + 16, 1.0, 0.0))
    for j in range(15):
        column = jnp.broadcast_to(table[:, j : j + 1], (16, 128))
        factor = jnp.where(row > j, column / column[j : j + 1], 0.0)
        table = table - factor * table[j : j + 1]
    pivot = jnp.sum(jnp.where(lane == row, table, 0.0), axis=1, keepdims=True)
    scale = 1024.0 / jnp.sqrt(pivot)
    inverse = table[:, 16:32] * scale
    high, low = split(inverse)
    factors_ref[...] = jnp.concatenate([high, low, high], axis=1)

    @pl.when(owner)
    def _():
        copy(wall.at[pl.ds(0, 3)], wall.at[pl.ds(0, 3)], ws2, wr2, place).wait_recv()

    @pl.when(jnp.logical_not(owner))
    def _():
        copy(wall, wall, ws2, wr2, place).wait_recv()

    packed = jnp.concatenate([wall[c] for c in range(4)], axis=0)
    at_wells = jnp.where(lanes((16, 128)) < 64, jnp.concatenate([packed, pltpu.roll(packed, 64, 1)], axis=0), 0.0)
    at_basis = gmat[3].astype(BF16)
    taken = jnp.dot(both[:, 0:128], at_basis, preferred_element_type=F32) + pltpu.roll(
        jnp.dot(both[:, 128:256], at_basis, preferred_element_type=F32), 64, 1
    )
    at_wells = jnp.where(lanes((16, 128)) < 64, at_wells - taken[0:16] - taken[16:32], 0.0)
    answer = jnp.dot(inverse, at_wells, precision=lax.Precision.HIGHEST, preferred_element_type=F32)
    resp_ref[...] = answer[:, 0:64]
    exchange.wait_send()
    copy(gall.at[pl.ds(0, 127)], gall.at[pl.ds(0, 127)], gs2, gr2, place).wait_send()
    copy(qrecv.at[pl.ds(0, 127)], qrecv.at[pl.ds(0, 127)], qs, qr, place).wait_send()

    @pl.when(az == ay)
    def _():
        copy(call.at[pl.ds(0, 31)], call.at[pl.ds(0, 31)], cs1, cr1, place).wait_send()
        copy(crecv.at[pl.ds(0, 127)], crecv.at[pl.ds(0, 127)], cs2, cr2, place).wait_send()

    @pl.when(az != ay)
    def _():
        copy(call, call, cs1, cr1, place).wait_send()

    @pl.when(owner)
    def _():
        copy(wall.at[pl.ds(0, 3)], wall.at[pl.ds(0, 3)], ws1, wr1, place).wait_send()
        copy(wrecv.at[pl.ds(0, 127)], wrecv.at[pl.ds(0, 127)], ws2, wr2, place).wait_send()

    @pl.when(jnp.logical_not(owner))
    def _():
        copy(wall, wall, ws1, wr1, place).wait_send()


def solve(*args):
    vmem = pl.BlockSpec(memory_space=pltpu.VMEM)
    smem = pl.BlockSpec(memory_space=pltpu.SMEM)
    dma = pltpu.SemaphoreType.DMA
    return pl.pallas_call(
        solve_kernel,
        out_shape=(
            jax.ShapeDtypeStruct((32, 32, 256), BF16),
            jax.ShapeDtypeStruct((16, 48), BF16),
            jax.ShapeDtypeStruct((16, 256), F32),
            jax.ShapeDtypeStruct((16, 256), F32),
            jax.ShapeDtypeStruct((16, 64), F32),
        ),
        in_specs=[vmem, pl.BlockSpec(memory_space=pl.ANY)] + [vmem] * 4 + [smem] * 2 + [vmem] * 5,
        out_specs=(vmem,) * 5,
        scratch_shapes=[
            pltpu.VMEM((2, 6, 18, 16, 128), F32),
            pltpu.VMEM((4, 256, 128), BF16),
            pltpu.VMEM((32, 16, 256), F32),
            pltpu.VMEM((32, 16, 256), F32),
            pltpu.VMEM((32, 16, 256), F32),
            pltpu.VMEM((17, 2, 512, 128), BF16),
            pltpu.VMEM((33, 256, 128), BF16),
            pltpu.VMEM((17, 8, 256), F32),
            pltpu.VMEM((4, 8, 1024), F32),
            pltpu.VMEM((33, 32, 16, 128), BF16),
            pltpu.VMEM((128, 4, 128), F32),
            pltpu.VMEM((2, 128, 4, 128), F32),
            pltpu.VMEM((2, 8, 128), F32),
            pltpu.VMEM((2, 2, 8, 128), F32),
            pltpu.VMEM((8, 64, 128), F32),
            pltpu.VMEM((5, 8, 1024), F32),
            pltpu.VMEM((5, 128, 128), F32),
            pltpu.VMEM((8, 128), F32),
            pltpu.VMEM((88, 128), F32),
            pltpu.VMEM((16384, 128), BF16),
            pltpu.VMEM((32, 256, 256), BF16),
            pltpu.VMEM((4, 128, 128), F32),
            pltpu.VMEM((256, 256), F32),
            pltpu.VMEM((128, 4, 128), F32),
            pltpu.VMEM((128, 4, 128), F32),
            pltpu.VMEM((128, 4, 128), F32),
            pltpu.VMEM((4, 128), F32),
            pltpu.VMEM((32, 2, 128), F32),
            pltpu.VMEM((128, 2, 128), F32),
            pltpu.VMEM((32, 2, 128), F32),
            pltpu.VMEM((2, 128), F32),
            pltpu.VMEM((2, 128), F32),
            pltpu.VMEM((128, 2, 128), F32),
            pltpu.VMEM((4, 2, 128), F32),
            pltpu.VMEM((128, 2, 128), F32),
            pltpu.VMEM((4, 2, 128), F32),
            pltpu.VMEM((2, 128), F32),
            pltpu.VMEM((256, 128), BF16),
            pltpu.VMEM((8, 128), F32),
            pltpu.VMEM((32, 256), F32),
            dma,
            dma((2, 4)),
            dma((6,)),
            dma((2, 6)),
            dma((3,)),
            dma((3,)),
        ]
        + [dma] * 15,
        compiler_params=pltpu.CompilerParams(
            collective_id=0, has_side_effects=True, vmem_limit_bytes=60 * 1024 * 1024
        ),
    )(*args)


def finish_kernel(
    rest_ref, factors_ref, first_in, coeffs_in, resp_in, out_ref, first_ref, coeffs_ref, resp_ref
):
    first_ref[...] = first_in[...]
    coeffs_ref[...] = coeffs_in[...]
    resp_ref[...] = resp_in[...]
    factors = factors_ref[...]

    def finish(i, carry):
        for u in range(4):
            p = 4 * i + u
            parts = rest_ref[p]
            block = jnp.dot(
                factors, jnp.concatenate([parts[0:16], parts[0:16], parts[16:32]], axis=0),
                preferred_element_type=F32,
            )
            for parity in range(2):
                out_ref[pl.ds(2 * p + parity, 16, stride=64), :] = block[
                    :, parity * 128 : parity * 128 + 128
                ]
        return carry

    lax.fori_loop(0, 8, finish, 0)


def finish(*args):
    vmem = pl.BlockSpec(memory_space=pltpu.VMEM)
    return pl.pallas_call(
        finish_kernel,
        out_shape=(
            jax.ShapeDtypeStruct((1024, 128), F32),
            jax.ShapeDtypeStruct((16, 256), F32),
            jax.ShapeDtypeStruct((16, 256), F32),
            jax.ShapeDtypeStruct((16, 64), F32),
        ),
        in_specs=[vmem] * 5,
        out_specs=(vmem,) * 4,
    )(*args)


def local(
    start_block, basis, trans_x, trans_y, trans_z, pore_volume, shift_table, shift_index,
    fault_send, fault_recv, fault_trans, well_cells,
):
    wells = jnp.concatenate([well_cells, well_cells]).reshape(1, 128)
    offsets = np.zeros((8, 128), np.int32)
    offsets[0:3] = np.array(SLOTS, np.int32).T
    parts = solve(
        start_block.reshape(1024, 128),
        basis.reshape(16384, 128),
        trans_x.reshape(64, 128),
        trans_y.reshape(64, 128),
        trans_z.reshape(64, 128),
        pore_volume.reshape(64, 128),
        shift_table,
        shift_index,
        fault_send[0].T,
        fault_recv[0].T,
        fault_trans[0].T,
        wells,
        jnp.asarray(offsets),
    )
    new_block, first_coeffs, coeffs, well_resp = finish(*parts)
    return new_block.reshape(start_block.shape), first_coeffs.T, coeffs.T, well_resp.T


def solution(mesh):
    in_specs = (
        P(None, "gx", "gy", "gz"),
        P(None, "gx", "gy", "gz"),
        P("gx", "gy", "gz"),
        P("gx", "gy", "gz"),
        P("gx", "gy", "gz"),
        P("gx", "gy", "gz"),
        P(),
        P(),
        P(("gx", "gy", "gz"), None, None),
        P(("gx", "gy", "gz"), None, None),
        P(("gx", "gy", "gz"), None, None),
        P(),
    )
    out_specs = (P(None, "gx", "gy", "gz"), P(), P(), P())
    return jax.shard_map(local, mesh=mesh, in_specs=in_specs, out_specs=out_specs, check_vma=False)
```

```python
import functools
import math

import jax
import jax.numpy as jnp
import numpy as np
from jax import lax
from jax.experimental import pallas as pl
from jax.experimental.pallas import tpu as pltpu
from jax.sharding import PartitionSpec as P

TERMS = 8
MESH = pl.DeviceIdType.MESH
F32 = jnp.float32
BF16 = jnp.bfloat16
SIGMA = 1.0 / 0.9


def weights():
    now = 1.0 / SIGMA
    table = []
    for _ in range(TERMS - 1):
        new = 1.0 / (2.0 * SIGMA - now)
        table.append((new * now, 2.0 * new / 0.9))
        now = new
    return table


def far_first():
    along = {8: (0.0, 0.5, 1.0, 1.5, 2.0, 1.5, 1.0, 0.5), 4: (0.0, 1.0, 2.0, 1.0)}
    every = [(x, y, z) for x in range(8) for y in range(4) for z in range(4)]
    return sorted(every, key=lambda o: -(along[8][o[0]] + along[4][o[1]] + along[4][o[2]]))


SLOTS = far_first()


def lanes(shape):
    return lax.broadcasted_iota(jnp.int32, shape, len(shape) - 1)


def half_swap(first, second):
    low = lanes(first.shape) < 64
    return (
        jnp.where(low, first, pltpu.roll(second, 64, 1)),
        jnp.where(low, pltpu.roll(first, 64, 1), second),
    )


def quarter_swap(value):
    upper = lax.broadcasted_iota(jnp.int32, value.shape, 0) // 4
    odd = lanes(value.shape) // 32 % 2
    moved = jnp.where(upper == 0, pltpu.roll(value, 96, 1), pltpu.roll(value, 32, 1))
    return jnp.where(upper == odd, value, pltpu.roll(moved, 4, 0))


def split(value):
    high = value.astype(BF16)
    return high, (value - high.astype(F32)).astype(BF16)


def dot_nt(a, b, **kw):
    return lax.dot_general(a, b, (((1,), (1,)), ((), ())), preferred_element_type=F32, **kw)


def solve_kernel(
    start_ref, basis_ref, tx_ref, ty_ref, tz_ref, pv_ref, table_ref, index_ref, fs_ref, fr_ref, ft_ref, wells_ref, offs_ref,
    rest, factors_ref, first_ref, coeffs_ref, resp_ref,
    dpad, dbf, res, xacc, acc, ohs, ohr, his, hir, hiz, mk, send, recv, zsend, zrecv, coef, edge,
    rows, tsend, trecv, bas, bt, gmat, gfull, gsend, grecv, gall, gsum, csend, crecv, call, csum,
    qsend, qrecv, wsend, wrecv, wall, wsum, ohw, hiw, cmat,
    ssem, rsem, hssem, hrsem, tssem, trsem, bsem, gs1, gr1, gs2, gr2, cs1, cr1, cs2, cr2,
    qs, qr, ws1, wr1, ws2, wr2,
):
    ax, ay, az = lax.axis_index("gx"), lax.axis_index("gy"), lax.axis_index("gz")
    place = (ax, ay, az)
    me = ax * 16 + ay * 4 + az
    xs = [(ax + i) % 8 for i in range(8)]
    ys = [(ay + i) % 4 for i in range(4)]
    zs = [(az + i) % 4 for i in range(4)]

    def peer(offset):
        return (xs[offset[0] % 8], ys[offset[1] % 4], zs[offset[2] % 4])

    def number(offset):
        x, y, z = peer(offset)
        return x * 16 + y * 4 + z

    up_x, down_x = peer((1, 0, 0)), peer((7, 0, 0))
    up_y, down_y = peer((0, 1, 0)), peer((0, 3, 0))
    up_z, down_z = peer((0, 0, 1)), peer((0, 0, 3))

    def copy(src, dst, ss, rs, where):
        return pltpu.make_async_remote_copy(
            src_ref=src, dst_ref=dst, send_sem=ss, recv_sem=rs, device_id=where, device_id_type=MESH
        )

    barrier = pltpu.get_barrier_semaphore()
    for offset in SLOTS[:127]:
        pl.semaphore_signal(barrier, inc=1, device_id=peer(offset), device_id_type=MESH)
    fetch = pltpu.make_async_copy(basis_ref, bas, bsem)
    fetch.start()

    offs = offs_ref[...]
    spot = lax.broadcasted_iota(jnp.int32, (128, 128), 0)

    def order_of(sign):
        x, y, z = (offs[i : i + 1] * sign for i in range(3))
        target = (x + ax + 8) % 8 * 16 + (y + ay + 4) % 4 * 4 + (z + az + 4) % 4
        return jnp.where(spot == target, 1.0, 0.0).astype(BF16)

    def spread_rows(which, value):
        rows[which] = jnp.concatenate([value] * 4, axis=0).T

    def halves(ref, order, which):
        cells = ref[...]
        parts = jnp.concatenate([cells // 256, cells % 256], axis=0).astype(F32).astype(BF16)
        moved = jnp.dot(parts, order, preferred_element_type=F32)
        spread_rows(which, moved[0:32])
        spread_rows(which + 1, moved[32:64])

    halves(fs_ref, order_of(1), 0)
    source_order = order_of(-1)
    halves(fr_ref, source_order, 2)
    high, low = split(ft_ref[...])
    lowest = (ft_ref[...] - high.astype(F32) - low.astype(F32)).astype(BF16)
    moved = jnp.dot(
        jnp.concatenate([high, low, lowest], axis=0), source_order, preferred_element_type=F32
    )
    spread_rows(4, moved[0:32] + moved[32:64] + moved[64:96])

    def flat(which, half):
        lane = lanes((16, 128))
        pieces = [rows[which, pl.ds(half * 4 + q, 16, stride=8), :] for q in range(4)]
        total = pieces[0]
        for q in range(1, 4):
            total = jnp.where(lane // 32 == q, pieces[q], total)
        return total

    def mask(hi, p):
        one = jnp.where(hi == float(p), 1.0, 0.0)
        return jnp.concatenate([one, one], axis=0).astype(BF16)

    column = lax.broadcasted_iota(jnp.int32, (256, 128), 0).astype(F32)

    def one_hot(low):
        return jnp.where(column == low, 1.0, 0.0).astype(BF16)

    for half in range(2):
        send_hi, send_lo, recv_hi, recv_lo, recv_weight = (flat(i, half) for i in range(5))
        part = slice(half * 128, half * 128 + 128)
        for j in range(16):
            this = slice(j, j + 1)
            quad = jnp.floor(send_hi[this] * 0.5)
            his[j, :, part] = jnp.broadcast_to(quad, (8, 128))
            low = send_lo[this] + (send_hi[this] - 2.0 * quad) * 256.0
            ohs[j, half, 0:256] = one_hot(low)
            ohs[j, half, 256:512] = one_hot(low - 256.0)
            place_in = slice((j % 4) * 256 + half * 128, (j % 4) * 256 + half * 128 + 128)
            hi = jnp.broadcast_to(recv_hi[this], (8, 128))
            hir[j // 4, :, place_in] = hi
            ohr[2 * j + half] = one_hot(recv_lo[this])
            edge[j // 4, :, place_in] = jnp.broadcast_to(recv_weight[this], (8, 128))
    lane = lanes((1, 128))
    line = lane % 64
    first = (line % 2) * 128
    near, far = jnp.where(lane < 64, 127, 0), jnp.where(lane < 64, 0, 127)
    hi = jnp.broadcast_to((line // 2).astype(F32), (8, 128))
    hiz[...] = hi
    ohr[32] = one_hot((first + far).astype(F32))
    his[16, :, 0:128] = jnp.broadcast_to((line // 4).astype(F32), (8, 128))
    low = ((line % 4) * 128 + near).astype(F32)
    ohs[16, 0, 0:256] = one_hot(low)
    ohs[16, 0, 256:512] = one_hot(low - 256.0)
    tsend[0:1, 0:64] = wells_ref[...].astype(F32)
    twice = tsend[0:1]
    well = jnp.where(lane < 64, twice, pltpu.roll(twice, 64, 1)).astype(jnp.int32)
    well_x, well_y, well_z = well // 32768, well // 512 % 64, well % 512
    owned = (well_x // 4 == ax) & (well_y // 16 == ay) & (well_z // 128 == az)
    cell = (well_x % 4 * 16 + well_y % 16) * 128 + well_z % 128
    hiw[...] = jnp.broadcast_to(jnp.where(owned, cell // 256, -1).astype(F32), (8, 128))
    ohw[...] = one_hot((cell % 256).astype(F32))

    def begin(i, carry):
        for u in range(4):
            p = 4 * i + u
            for parity in range(2):
                res[p, :, parity * 128 : parity * 128 + 128] = start_ref[
                    pl.ds(2 * p + parity, 16, stride=64), :
                ]
        return carry

    lax.fori_loop(0, 8, begin, 0)
    pair = lax.broadcasted_iota(jnp.int32, (32, 1024), 0).astype(F32)
    total = jnp.zeros((64, 256), F32)
    for j in range(4):
        weight = jnp.broadcast_to(edge[j, 0:1, :], (32, 1024))
        hit = pair == jnp.broadcast_to(hir[j, 0:1, :], (32, 1024))
        high, low = split(jnp.where(hit, weight, 0.0))
        total = total + dot_nt(
            jnp.concatenate([high, low], axis=0),
            jnp.concatenate([ohr[8 * j + h] for h in range(8)], axis=1),
        )
    fault = total[0:32] + total[32:64]
    acc[0:32, 0, :] = fault

    for x in range(4):
        tsend[x : x + 1] = ty_ref[x * 16 + 15 : x * 16 + 16]
    tsend[4:8] = jnp.zeros((4, 128), F32)
    pl.semaphore_wait(barrier, 127)
    faces = (
        copy(tx_ref.at[pl.ds(48, 16)], trecv.at[pl.ds(0, 16)], tssem.at[0], trsem.at[0], up_x),
        copy(tsend, trecv.at[pl.ds(16, 8)], tssem.at[1], trsem.at[1], up_y),
        copy(tz_ref, trecv.at[pl.ds(24, 64)], tssem.at[2], trsem.at[2], up_z),
    )
    for face in faces:
        face.start()
    shift = table_ref[0]
    for i in range(1, 16):
        shift = jnp.where(index_ref[0] == i, table_ref[i], shift)
    for face in faces:
        face.wait()
    lane = lanes((16, 128))
    row = lax.broadcasted_iota(jnp.int32, (16, 128), 0)
    inside = [jnp.where(p > 0, 1.0, 0.0) for p in place]
    outside = [jnp.where(p < n - 1, 1.0, 0.0) for p, n in zip(place, (8, 4, 4))]
    for x in range(4):
        these = slice(x * 16, x * 16 + 16)
        upper_x = tx_ref[these] * (outside[0] if x == 3 else 1.0)
        if x == 0:
            lower_x = trecv[0:16] * inside[0]
        else:
            lower_x = tx_ref[(x - 1) * 16 : x * 16]
        ty = ty_ref[these]
        upper_y = jnp.where(row == 15, ty * outside[1], ty)
        lower_y = jnp.where(
            row == 0, trecv[16 + x : 17 + x] * inside[1], pltpu.roll(ty, 1, 0)
        )
        tz = tz_ref[these]
        upper_z = jnp.where(lane == 127, tz * outside[2], tz)
        lower_z = jnp.where(
            lane == 0,
            pltpu.roll(trecv[24 + x * 16 : 40 + x * 16], 1, 1) * inside[2],
            pltpu.roll(tz, 1, 1),
        )
        coef[0, these] = upper_x
        coef[1, these] = lower_x
        coef[2, these] = upper_y
        coef[3, these] = lower_y
        coef[4, these] = upper_z
        coef[5, these] = lower_z
        coef[6, these] = (
            upper_x + lower_x + upper_y + lower_y + upper_z + lower_z + shift * pv_ref[these]
        )
    for p in range(32):
        for parity in range(2):
            r = 2 * p + parity
            coef[6, r : r + 1] += acc[p, 0:1, parity * 128 : parity * 128 + 128]
    coef[7] = 1.0 / coef[6]
    both = jnp.concatenate([coef[5], coef[4]], axis=0).T
    lane = lanes((1, 128))
    edge[4, :, 0:128] = jnp.broadcast_to(
        jnp.where(lane < 64, both[0:1], both[127:128]), (8, 128)
    )
    lane = lanes((64, 128))
    coef[4] = jnp.where(lane == 127, 0.0, coef[4])
    coef[5] = jnp.where(lane == 0, 0.0, coef[5])

    def initial(i, carry):
        for u in range(4):
            p = 4 * i + u
            for parity in range(2):
                part = slice(parity * 128, parity * 128 + 128)
                inverse = jnp.broadcast_to(coef[7, pl.ds(2 * p + parity, 1)], (16, 128))
                d = res[p, :, part] * inverse
                dpad[0, 1 + i // 2, 1 + (i % 2) * 8 + 2 * u + parity] = d
                dbf[u % 2 * 2 + parity, pl.ds(pl.multiple_of((2 * i + u // 2) * 16, 16), 16)] = d.astype(BF16)
                xacc[p, :, part] = jnp.zeros_like(d)
        return carry

    lax.fori_loop(0, 8, initial, 0)

    def pick(source, one_hot, hi_of, width, count):
        product = jnp.dot(source, one_hot, preferred_element_type=F32)
        tiles = []
        for h in range(width // 128):
            part = slice(h * 128, h * 128 + 128)
            hi = hi_of(part)
            first = jnp.zeros((8, 128), F32)
            second = jnp.zeros((8, 128), F32)
            for p in range(count):
                hit = hi == float(p)
                first = jnp.where(hit, product[p * 16 : p * 16 + 8, part], first)
                second = jnp.where(hit, product[p * 16 + 8 : p * 16 + 16, part], second)
            tiles.append((first, second))
        return tiles

    def gather(j, width):
        picks = [ohs[j, h] for h in range(width // 128)]
        return pick(
            jnp.concatenate([dbf[q] for q in range(4)], axis=1),
            picks[0] if len(picks) == 1 else jnp.concatenate(picks, axis=1),
            lambda part: his[j, :, part], width, 16,
        )

    def scatter(j, tiles):
        values = []
        for h, (first, second) in enumerate(tiles):
            weight = edge[j, :, h * 128 : h * 128 + 128]
            values.append(jnp.concatenate([first * weight, second * weight], axis=0).astype(BF16))
        picks = [ohr[8 * j + h] for h in range(len(values))]
        picks = picks[0] if len(picks) == 1 else jnp.concatenate(picks, axis=1)
        sums = []
        for side in range(2):
            placed = [
                jnp.concatenate([mk[8 * j + h, side * 16 + p] * value for p in range(16)], axis=0)
                for h, value in enumerate(values)
            ]
            placed = placed[0] if len(placed) == 1 else jnp.concatenate(placed, axis=1)
            sums.append(dot_nt(placed, picks).reshape(16, 16, 256))
        return sums

    exchange = copy(gsend.at[pl.ds(0, 127)], grecv.at[pl.ds(0, 127)], gs1, gr1, place)
    spread = copy(gsend.at[pl.ds(0, 127)], gall.at[pl.ds(0, 127)], gs2, gr2, place)

    def permute(t):
        a = lax.broadcasted_iota(jnp.int32, (256, 256), 0)
        b = lax.broadcasted_iota(jnp.int32, (256, 256), 1)
        order = jnp.where(b == a % 16 * 16 + a // 16, 1.0, 0.0).astype(BF16)

        def block(i, carry):
            k = jnp.where(t == 0, 0, t * 6 - 2) + i
            for q in range(2):
                sides = []
                for side in range(2):
                    base = k * 1024 + (2 * q + side) * 16
                    sides.append(
                        jnp.concatenate(
                            [bas[pl.ds(pl.multiple_of(base + 64 * kk, 16), 16), :] for kk in range(16)],
                            axis=0,
                        )
                    )
                turned = jnp.dot(
                    order, jnp.concatenate(sides, axis=1), preferred_element_type=F32
                ).astype(BF16)
                for side in range(2):
                    for xx in range(16):
                        r = (2 * q + side) * 16 + xx
                        bt[r // 2, pl.ds(pl.multiple_of(k * 16, 16), 16), r % 2 * 128 : r % 2 * 128 + 128] = (
                            turned[xx * 16 : xx * 16 + 16, side * 128 : side * 128 + 128]
                        )
            return carry

        lax.fori_loop(0, jnp.where(t == 0, 4, 6), block, 0)

    def iterate(t, carry):
        now, gain = carry
        par = t % 2
        here = dpad.at[par]
        halos = [
            copy(here.at[4, pl.ds(1, 16)], here.at[0, pl.ds(1, 16)], hssem.at[0], hrsem.at[par, 0], up_x),
            copy(here.at[1, pl.ds(1, 16)], here.at[5, pl.ds(1, 16)], hssem.at[1], hrsem.at[par, 1], down_x),
            copy(here.at[pl.ds(1, 4), 16], here.at[pl.ds(1, 4), 0], hssem.at[2], hrsem.at[par, 2], up_y),
            copy(here.at[pl.ds(1, 4), 1], here.at[pl.ds(1, 4), 17], hssem.at[3], hrsem.at[par, 3], down_y),
        ]
        def stencil(r):
            x, y = 1 + r // 16, 1 + r % 16
            p, part = r // 2, slice(r % 2 * 128, r % 2 * 128 + 128)
            d = here[x, y]
            xacc[p, :, part] += d

            def times(which, value):
                return jnp.broadcast_to(coef[which, r : r + 1], (16, 128)) * value

            total = times(4, pltpu.roll(d, 127, 1)) + times(5, pltpu.roll(d, 1, 1))
            for which, inside_too, near in (
                (0, x < 4, (x + 1, y)), (1, x > 1, (x - 1, y)), (2, y < 16, (x, y + 1)), (3, y > 1, (x, y - 1))
            ):
                if inside_too:
                    total = total + times(which, here[near])
            res[p, :, part] = res[p, :, part] - (times(6, d) - total)

        halos_z = [
            copy(zsend.at[0], zrecv.at[par, 0], hssem.at[4], hrsem.at[par, 4], up_z),
            copy(zsend.at[1], zrecv.at[par, 1], hssem.at[5], hrsem.at[par, 5], down_z),
        ]
        for group in (range(0, 2), range(2, 8), range(8, 16)):
            for j in group:
                for h, (first, second) in enumerate(gather(j, 256)):
                    first, second = half_swap(first, second)
                    first, second = quarter_swap(first), quarter_swap(second)
                    base = j * 8 + h * 4
                    send[base] = first[0:4]
                    send[base + 1] = first[4:8]
                    send[base + 2] = second[0:4]
                    send[base + 3] = second[4:8]
            if group[0] == 8:
                ((first, second),) = gather(16, 128)
                first, second = half_swap(first, second)
                zsend[0] = first
                zsend[1] = second
                for halo in halos_z:
                    halo.start()
            for slot in range(group[0] * 8, min(group[-1] * 8 + 8, 127)):
                copy(
                    send.at[slot], recv.at[par, slot], ssem, rsem.at[par, slot // 32], peer(SLOTS[slot])
                ).start()
            if group[0] == 2:
                for halo in halos:
                    halo.start()
        recv[par, 127] = send[127]
        for r in range(64):
            stencil(r)
        @pl.when(t == 0)
        def _():
            fetch.wait()

            def build(c, carry):
                for h in range(8):
                    hi = hir[c, :, h * 128 : h * 128 + 128]
                    for p in range(32):
                        mk[8 * c + h, p] = mask(hi, p)
                return carry

            lax.fori_loop(0, 4, build, 0)
            hi = hiz[...]
            for p in range(32):
                mk[32, p] = mask(hi, p)

        @pl.when(t < 3)
        def _():
            permute(t)

        @pl.when(t == 3)
        def _():
            gfull[...] = jnp.zeros_like(gfull)

            def add(i, carry):
                total = gfull[...]
                for u in range(4):
                    total = total + dot_nt(bt[4 * i + u], bt[4 * i + u])
                gfull[...] = total
                return carry

            lax.fori_loop(0, 8, add, 0)
            gmat[0] = gfull[0:128, 0:128]
            gmat[1] = gfull[0:128, 128:256]
            gmat[2] = gfull[128:256, 128:256]

        @pl.when(t == 4)
        def _():
            gfull[:, 0:128] = jnp.zeros((256, 128), F32)

            def at_wells(i, carry):
                total = gfull[:, 0:128]
                for u in range(4):
                    p = 4 * i + u
                    hit = hiw[0:1] == lax.convert_element_type(p, F32)
                    found = jnp.dot(bt[p], ohw[...], preferred_element_type=F32)
                    total = total + jnp.where(hit, found, 0.0)
                gfull[:, 0:128] = total
                return carry

            lax.fori_loop(0, 8, at_wells, 0)
            gmat[3] = jnp.where(
                lanes((128, 128)) < 64, gfull[0:128, 0:128], gfull[128:256, 0:128]
            )

        @pl.when(t == 5)
        def _():
            for c in range(128):
                gsend[c] = gmat[c // 32, c % 32 * 4 : c % 32 * 4 + 4]
            for offset in SLOTS[:127]:
                copy(gsend.at[number(offset)], grecv.at[me], gs1, gr1, peer(offset)).start()
            grecv[me] = gsend[me]

        @pl.when(t == 6)
        def _():
            exchange.wait_recv()
            gsum[...] = jnp.sum(grecv[...], axis=0)
            for offset in SLOTS[:127]:
                copy(gsum, gall.at[me], gs2, gr2, peer(offset)).start()
            gall[me] = gsum[...]

        for halo in halos:
            halo.wait_recv()

        for y in range(16):
            for x, which, beyond in ((0, 1, 0), (3, 0, 5)):
                r = x * 16 + y
                p, part = r // 2, slice(r % 2 * 128, r % 2 * 128 + 128)
                res[p, :, part] += jnp.broadcast_to(coef[which, r : r + 1], (16, 128)) * here[beyond, 1 + y]
        for x in range(4):
            for y, which, beyond in ((0, 3, 0), (15, 2, 17)):
                r = x * 16 + y
                p, part = r // 2, slice(r % 2 * 128, r % 2 * 128 + 128)
                res[p, :, part] += jnp.broadcast_to(coef[which, r : r + 1], (16, 128)) * here[1 + x, beyond]
        for halo in halos_z:
            halo.wait_recv()
        for side, value in enumerate(scatter(4, [half_swap(zrecv[par, 0], zrecv[par, 1])])):
            acc[side * 16 : side * 16 + 16] = value
        for j in (3, 2, 1, 0):
            count = 32 if j < 3 else 31
            copy(
                send.at[pl.ds(0, count)], recv.at[par, pl.ds(0, count)], ssem, rsem.at[par, j], place
            ).wait_recv()
            tiles = []
            for h in range(8):
                base = j * 32 + h * 4
                first = jnp.concatenate([recv[par, base], recv[par, base + 1]], axis=0)
                second = jnp.concatenate([recv[par, base + 2], recv[par, base + 3]], axis=0)
                tiles.append(half_swap(quarter_swap(first), quarter_swap(second)))
            sums = scatter(j, tiles)
            if j:
                for side, value in enumerate(sums):
                    acc[side * 16 : side * 16 + 16] += value
        for r in range(64):
            p, part = r // 2, slice(r % 2 * 128, r % 2 * 128 + 128)
            residual = res[p, :, part] + acc[p, :, part] + sums[p // 16][p % 16, :, part]
            res[p, :, part] = residual
            inverse = jnp.broadcast_to(coef[7, r : r + 1], (16, 128))
            x, y = 1 + r // 16, 1 + r % 16
            d = now * here[x, y] + gain * (residual * inverse)
            dpad[1 - par, x, y] = d
            dbf[r % 4, r // 4 * 16 : r // 4 * 16 + 16] = d.astype(BF16)
        for halo in halos + halos_z:
            halo.wait_send()
        copy(send.at[pl.ds(0, 127)], recv.at[par, pl.ds(0, 127)], ssem, rsem.at[par, 0], place).wait_send()
        nxt_now, nxt_gain = carry
        for step in range(TERMS - 2):
            nxt_now = jnp.where(t == step, weights()[step + 1][0], nxt_now)
            nxt_gain = jnp.where(t == step, weights()[step + 1][1], nxt_gain)
        return nxt_now, nxt_gain

    lax.fori_loop(
        0, TERMS - 1, iterate, (jnp.float32(weights()[0][0]), jnp.float32(weights()[0][1]))
    )

    def project(i, total):
        for u in range(8):
            p = 8 * i + u
            d = jnp.concatenate([dpad[1, 1 + i, 1 + 2 * u], dpad[1, 1 + i, 2 + 2 * u]], axis=1)
            x = xacc[p] + d
            xacc[p] = x
            high, low = split(x)
            parts = jnp.concatenate([high, low], axis=0)
            rest[p] = parts
            total = total + dot_nt(parts, bt[p])
        return total

    total = lax.fori_loop(0, 4, project, jnp.zeros((32, 256), F32))
    for c in range(32):
        csend[c] = total[c % 16 * 2 : c % 16 * 2 + 2, c // 16 * 128 : c // 16 * 128 + 128]
    mine = ax * 4 + ay
    for offset in [o for o in SLOTS if o[2] == 0]:
        x, y = xs[offset[0]], ys[offset[1]]
        to = copy(csend.at[x * 4 + y], crecv.at[me], cs1, cr1, (x, y, y))
        if offset[:2] != (0, 0):
            to.start()
        else:

            @pl.when(az != ay)
            def _(to=to):
                to.start()

    ((first_w, second_w),) = pick(
        rest[:, 0:16].reshape(512, 256), ohw[...], lambda part: hiw[...], 128, 32
    )
    ((low_first, low_second),) = pick(
        rest[:, 16:32].reshape(512, 256), ohw[...], lambda part: hiw[...], 128, 32
    )
    packed, _ = half_swap(first_w + low_first, second_w + low_second)
    for c in range(4):
        wsend[c] = packed[2 * c : 2 * c + 2]
    for c in range(4):

        @pl.when(~((ax == 2 * c) & (ay == c) & (az == (c + 1) % 4)))
        def _(c=c):
            copy(wsend.at[c], wrecv.at[me], ws1, wr1, (2 * c, c, (c + 1) % 4)).start()

    owner = (ax == 2 * ay) & (az == (ay + 1) % 4)

    @pl.when(owner)
    def _():
        wrecv[me] = wsend[ay]
        copy(wrecv.at[pl.ds(0, 127)], wrecv.at[pl.ds(0, 127)], ws1, wr1, place).wait_recv()
        wsum[...] = jnp.sum(wrecv[...], axis=0)
        for offset in SLOTS[:127]:
            copy(wsum, wall.at[ay], ws2, wr2, peer(offset)).start()
        wall[ay] = wsum[...]

    spread.wait_recv()
    for c in range(128):
        gmat[c // 32, c % 32 * 4 : c % 32 * 4 + 4] = gall[c]

    @pl.when(az == ay)
    def _():
        crecv[me] = csend[mine]
        copy(crecv.at[pl.ds(0, 127)], crecv.at[pl.ds(0, 127)], cs1, cr1, place).wait_recv()
        csum[...] = jnp.sum(crecv[...], axis=0)
        for offset in SLOTS[:127]:
            copy(csum, call.at[mine], cs2, cr2, peer(offset)).start()
        call[mine] = csum[...]
        copy(call.at[pl.ds(0, 31)], call.at[pl.ds(0, 31)], cs2, cr2, place).wait_recv()

    @pl.when(az != ay)
    def _():
        copy(call, call, cs2, cr2, place).wait_recv()

    for c in range(32):
        cmat[c % 16 * 2 : c % 16 * 2 + 2, c // 16 * 128 : c // 16 * 128 + 128] = call[c]
    leading = cmat[0:16]
    first = leading.astype(BF16)
    exact = dict(precision=lax.Precision.HIGHEST)
    wide = first.astype(F32)
    near, far = wide[:, 0:128], wide[:, 128:256]
    taken = jnp.concatenate(
        [
            jnp.dot(near, gmat[0], preferred_element_type=F32, **exact) + dot_nt(far, gmat[1], **exact),
            jnp.dot(near, gmat[1], preferred_element_type=F32, **exact)
            + jnp.dot(far, gmat[2], preferred_element_type=F32, **exact),
        ],
        axis=1,
    )
    second_sum = leading + cmat[16:32] - taken
    both = jnp.concatenate([first, second_sum.astype(BF16)], axis=0)
    first_ref[...] = leading
    coeffs_ref[...] = leading + second_sum

    def subtract(i, total):
        for u in range(8):
            p = 8 * i + u
            taken = jnp.dot(both, bt[p], preferred_element_type=F32)
            left = xacc[p] - taken[0:16] - taken[16:32]
            high, low = split(left)
            parts = jnp.concatenate([high, low], axis=0)
            rest[p] = parts
            total = total + dot_nt(parts, parts)
        return total

    total = lax.fori_loop(0, 4, subtract, jnp.zeros((32, 32), F32))
    gram = total[0:16, 0:16] + total[0:16, 16:32] + total[16:32, 0:16]
    lane = lanes((8, 128))
    wide = jnp.concatenate([gram, jnp.zeros((16, 112), F32)], axis=1)
    row = lax.broadcasted_iota(jnp.int32, (8, 128), 0)
    for half in range(2):
        value = wide[half * 8 : half * 8 + 8]
        line = jnp.zeros((1, 128), F32)
        for i in range(8):
            line = line + pltpu.roll(value[i : i + 1], 16 * i, 1)
        qsend[half : half + 1] = line
    for offset in SLOTS[:127]:
        copy(qsend, qrecv.at[me], qs, qr, peer(offset)).start()
    qrecv[me] = qsend[...]

    copy(qrecv.at[pl.ds(0, 127)], qrecv.at[pl.ds(0, 127)], qs, qr, place).wait_recv()
    sums = jnp.sum(qrecv[...], axis=0)
    pieces = []
    for half in range(2):
        for i in range(8):
            pieces.append(pltpu.roll(sums[half : half + 1], (128 - 16 * i) % 128, 1))
    gram = jnp.concatenate(pieces, axis=0)
    lane = lanes((16, 128))
    row = lax.broadcasted_iota(jnp.int32, (16, 128), 0)
    table = jnp.where(lane < 16, gram, jnp.where(lane == row + 16, 1.0, 0.0))
    for j in range(15):
        column = jnp.broadcast_to(table[:, j : j + 1], (16, 128))
        factor = jnp.where(row > j, column / column[j : j + 1], 0.0)
        table = table - factor * table[j : j + 1]
    pivot = jnp.sum(jnp.where(lane == row, table, 0.0), axis=1, keepdims=True)
    scale = 1024.0 / jnp.sqrt(pivot)
    inverse = table[:, 16:32] * scale
    high, low = split(inverse)
    factors_ref[...] = jnp.concatenate([high, low, high], axis=1)

    @pl.when(owner)
    def _():
        copy(wall.at[pl.ds(0, 3)], wall.at[pl.ds(0, 3)], ws2, wr2, place).wait_recv()

    @pl.when(jnp.logical_not(owner))
    def _():
        copy(wall, wall, ws2, wr2, place).wait_recv()

    packed = jnp.concatenate([wall[c] for c in range(4)], axis=0)
    at_wells = jnp.where(lanes((16, 128)) < 64, jnp.concatenate([packed, pltpu.roll(packed, 64, 1)], axis=0), 0.0)
    at_basis = gmat[3].astype(BF16)
    taken = jnp.dot(both[:, 0:128], at_basis, preferred_element_type=F32) + pltpu.roll(
        jnp.dot(both[:, 128:256], at_basis, preferred_element_type=F32), 64, 1
    )
    at_wells = jnp.where(lanes((16, 128)) < 64, at_wells - taken[0:16] - taken[16:32], 0.0)
    answer = jnp.dot(inverse, at_wells, precision=lax.Precision.HIGHEST, preferred_element_type=F32)
    resp_ref[...] = answer[:, 0:64]
    exchange.wait_send()
    copy(gall.at[pl.ds(0, 127)], gall.at[pl.ds(0, 127)], gs2, gr2, place).wait_send()
    copy(qrecv.at[pl.ds(0, 127)], qrecv.at[pl.ds(0, 127)], qs, qr, place).wait_send()

    @pl.when(az == ay)
    def _():
        copy(call.at[pl.ds(0, 31)], call.at[pl.ds(0, 31)], cs1, cr1, place).wait_send()
        copy(crecv.at[pl.ds(0, 127)], crecv.at[pl.ds(0, 127)], cs2, cr2, place).wait_send()

    @pl.when(az != ay)
    def _():
        copy(call, call, cs1, cr1, place).wait_send()

    @pl.when(owner)
    def _():
        copy(wall.at[pl.ds(0, 3)], wall.at[pl.ds(0, 3)], ws1, wr1, place).wait_send()
        copy(wrecv.at[pl.ds(0, 127)], wrecv.at[pl.ds(0, 127)], ws2, wr2, place).wait_send()

    @pl.when(jnp.logical_not(owner))
    def _():
        copy(wall, wall, ws1, wr1, place).wait_send()


def solve(*args):
    vmem = pl.BlockSpec(memory_space=pltpu.VMEM)
    smem = pl.BlockSpec(memory_space=pltpu.SMEM)
    dma = pltpu.SemaphoreType.DMA
    return pl.pallas_call(
        solve_kernel,
        out_shape=(
            jax.ShapeDtypeStruct((32, 32, 256), BF16),
            jax.ShapeDtypeStruct((16, 48), BF16),
            jax.ShapeDtypeStruct((16, 256), F32),
            jax.ShapeDtypeStruct((16, 256), F32),
            jax.ShapeDtypeStruct((16, 64), F32),
        ),
        in_specs=[vmem, pl.BlockSpec(memory_space=pl.ANY)] + [vmem] * 4 + [smem] * 2 + [vmem] * 5,
        out_specs=(vmem,) * 5,
        scratch_shapes=[
            pltpu.VMEM((2, 6, 18, 16, 128), F32),
            pltpu.VMEM((4, 256, 128), BF16),
            pltpu.VMEM((32, 16, 256), F32),
            pltpu.VMEM((32, 16, 256), F32),
            pltpu.VMEM((32, 16, 256), F32),
            pltpu.VMEM((17, 2, 512, 128), BF16),
            pltpu.VMEM((33, 256, 128), BF16),
            pltpu.VMEM((17, 8, 256), F32),
            pltpu.VMEM((4, 8, 1024), F32),
            pltpu.VMEM((8, 128), F32),
            pltpu.VMEM((33, 32, 16, 128), BF16),
            pltpu.VMEM((128, 4, 128), F32),
            pltpu.VMEM((2, 128, 4, 128), F32),
            pltpu.VMEM((2, 8, 128), F32),
            pltpu.VMEM((2, 2, 8, 128), F32),
            pltpu.VMEM((8, 64, 128), F32),
            pltpu.VMEM((5, 8, 1024), F32),
            pltpu.VMEM((5, 128, 128), F32),
            pltpu.VMEM((8, 128), F32),
            pltpu.VMEM((88, 128), F32),
            pltpu.VMEM((16384, 128), BF16),
            pltpu.VMEM((32, 256, 256), BF16),
            pltpu.VMEM((4, 128, 128), F32),
            pltpu.VMEM((256, 256), F32),
            pltpu.VMEM((128, 4, 128), F32),
            pltpu.VMEM((128, 4, 128), F32),
            pltpu.VMEM((128, 4, 128), F32),
            pltpu.VMEM((4, 128), F32),
            pltpu.VMEM((32, 2, 128), F32),
            pltpu.VMEM((128, 2, 128), F32),
            pltpu.VMEM((32, 2, 128), F32),
            pltpu.VMEM((2, 128), F32),
            pltpu.VMEM((2, 128), F32),
            pltpu.VMEM((128, 2, 128), F32),
            pltpu.VMEM((4, 2, 128), F32),
            pltpu.VMEM((128, 2, 128), F32),
            pltpu.VMEM((4, 2, 128), F32),
            pltpu.VMEM((2, 128), F32),
            pltpu.VMEM((256, 128), BF16),
            pltpu.VMEM((8, 128), F32),
            pltpu.VMEM((32, 256), F32),
            dma,
            dma((2, 4)),
            dma((6,)),
            dma((2, 6)),
            dma((3,)),
            dma((3,)),
        ]
        + [dma] * 15,
        compiler_params=pltpu.CompilerParams(
            collective_id=0, has_side_effects=True, vmem_limit_bytes=60 * 1024 * 1024
        ),
    )(*args)


def finish_kernel(
    rest_ref, factors_ref, first_in, coeffs_in, resp_in, out_ref, first_ref, coeffs_ref, resp_ref
):
    first_ref[...] = first_in[...]
    coeffs_ref[...] = coeffs_in[...]
    resp_ref[...] = resp_in[...]
    factors = factors_ref[...]

    def finish(i, carry):
        for u in range(4):
            p = 4 * i + u
            parts = rest_ref[p]
            block = jnp.dot(
                factors, jnp.concatenate([parts[0:16], parts[0:16], parts[16:32]], axis=0),
                preferred_element_type=F32,
            )
            for parity in range(2):
                out_ref[pl.ds(2 * p + parity, 16, stride=64), :] = block[
                    :, parity * 128 : parity * 128 + 128
                ]
        return carry

    lax.fori_loop(0, 8, finish, 0)


def finish(*args):
    vmem = pl.BlockSpec(memory_space=pltpu.VMEM)
    return pl.pallas_call(
        finish_kernel,
        out_shape=(
            jax.ShapeDtypeStruct((1024, 128), F32),
            jax.ShapeDtypeStruct((16, 256), F32),
            jax.ShapeDtypeStruct((16, 256), F32),
            jax.ShapeDtypeStruct((16, 64), F32),
        ),
        in_specs=[vmem] * 5,
        out_specs=(vmem,) * 4,
    )(*args)


def local(
    start_block, basis, trans_x, trans_y, trans_z, pore_volume, shift_table, shift_index,
    fault_send, fault_recv, fault_trans, well_cells,
):
    wells = well_cells.reshape(1, 64)
    offsets = np.zeros((8, 128), np.int32)
    offsets[0:3] = np.array(SLOTS, np.int32).T
    parts = solve(
        start_block.reshape(1024, 128),
        basis.reshape(16384, 128),
        trans_x.reshape(64, 128),
        trans_y.reshape(64, 128),
        trans_z.reshape(64, 128),
        pore_volume.reshape(64, 128),
        shift_table,
        shift_index,
        fault_send[0].T,
        fault_recv[0].T,
        fault_trans[0].T,
        wells,
        jnp.asarray(offsets),
    )
    new_block, first_coeffs, coeffs, well_resp = finish(*parts)
    return new_block.reshape(start_block.shape), first_coeffs.T, coeffs.T, well_resp.T


def solution(mesh):
    in_specs = (
        P(None, "gx", "gy", "gz"),
        P(None, "gx", "gy", "gz"),
        P("gx", "gy", "gz"),
        P("gx", "gy", "gz"),
        P("gx", "gy", "gz"),
        P("gx", "gy", "gz"),
        P(),
        P(),
        P(("gx", "gy", "gz"), None, None),
        P(("gx", "gy", "gz"), None, None),
        P(("gx", "gy", "gz"), None, None),
        P(),
    )
    out_specs = (P(None, "gx", "gy", "gz"), P(), P(), P())
    return jax.shard_map(local, mesh=mesh, in_specs=in_specs, out_specs=out_specs, check_vma=False)
```

```python
import functools
import math

import jax
import jax.numpy as jnp
import numpy as np
from jax import lax
from jax.experimental import pallas as pl
from jax.experimental.pallas import tpu as pltpu
from jax.sharding import PartitionSpec as P

TERMS = 8
MESH = pl.DeviceIdType.MESH
F32 = jnp.float32
BF16 = jnp.bfloat16
SIGMA = 1.0 / 0.9


def weights():
    now = 1.0 / SIGMA
    table = []
    for _ in range(TERMS - 1):
        new = 1.0 / (2.0 * SIGMA - now)
        table.append((new * now, 2.0 * new / 0.9))
        now = new
    return table


def far_first():
    along = {8: (0.0, 0.5, 1.0, 1.5, 2.0, 1.5, 1.0, 0.5), 4: (0.0, 1.0, 2.0, 1.0)}
    every = [(x, y, z) for x in range(8) for y in range(4) for z in range(4)]
    return sorted(every, key=lambda o: -(along[8][o[0]] + along[4][o[1]] + along[4][o[2]]))


SLOTS = far_first()


def lanes(shape):
    return lax.broadcasted_iota(jnp.int32, shape, len(shape) - 1)


def half_swap(first, second):
    low = lanes(first.shape) < 64
    return (
        jnp.where(low, first, pltpu.roll(second, 64, 1)),
        jnp.where(low, pltpu.roll(first, 64, 1), second),
    )


def quarter_swap(value):
    upper = lax.broadcasted_iota(jnp.int32, value.shape, 0) // 4
    odd = lanes(value.shape) // 32 % 2
    moved = jnp.where(upper == 0, pltpu.roll(value, 96, 1), pltpu.roll(value, 32, 1))
    return jnp.where(upper == odd, value, pltpu.roll(moved, 4, 0))


def split(value):
    high = value.astype(BF16)
    return high, (value - high.astype(F32)).astype(BF16)


def dot_nt(a, b, **kw):
    return lax.dot_general(a, b, (((1,), (1,)), ((), ())), preferred_element_type=F32, **kw)


def solve_kernel(
    start_ref, basis_ref, tx_ref, ty_ref, tz_ref, pv_ref, table_ref, index_ref, fs_ref, fr_ref, ft_ref, wells_ref, offs_ref,
    rest_ref, factors_ref, first_ref, coeffs_ref, resp_ref,
    dpad, dbf, res, xacc, acc, ohs, ohr, his, hir, hiz, mk, send, recv, zsend, zrecv, coef, edge,
    rows, tsend, trecv, bas, bt, rest, gmat, gfull, gsend, grecv, gall, gsum, csend, crecv, call, csum,
    qsend, qrecv, wsend, wrecv, wall, wsum, ohw, hiw, cmat,
    ssem, rsem, hssem, hrsem, tssem, trsem, bsem, gs1, gr1, gs2, gr2, cs1, cr1, cs2, cr2,
    qs, qr, ws1, wr1, ws2, wr2, ksem,
):
    ax, ay, az = lax.axis_index("gx"), lax.axis_index("gy"), lax.axis_index("gz")
    place = (ax, ay, az)
    me = ax * 16 + ay * 4 + az
    xs = [(ax + i) % 8 for i in range(8)]
    ys = [(ay + i) % 4 for i in range(4)]
    zs = [(az + i) % 4 for i in range(4)]

    def peer(offset):
        return (xs[offset[0] % 8], ys[offset[1] % 4], zs[offset[2] % 4])

    def number(offset):
        x, y, z = peer(offset)
        return x * 16 + y * 4 + z

    up_x, down_x = peer((1, 0, 0)), peer((7, 0, 0))
    up_y, down_y = peer((0, 1, 0)), peer((0, 3, 0))
    up_z, down_z = peer((0, 0, 1)), peer((0, 0, 3))

    def copy(src, dst, ss, rs, where):
        return pltpu.make_async_remote_copy(
            src_ref=src, dst_ref=dst, send_sem=ss, recv_sem=rs, device_id=where, device_id_type=MESH
        )

    barrier = pltpu.get_barrier_semaphore()
    for offset in SLOTS[:127]:
        pl.semaphore_signal(barrier, inc=1, device_id=peer(offset), device_id_type=MESH)
    fetch = pltpu.make_async_copy(basis_ref, bas, bsem)
    fetch.start()

    offs = offs_ref[...]
    spot = lax.broadcasted_iota(jnp.int32, (128, 128), 0)

    def order_of(sign):
        x, y, z = (offs[i : i + 1] * sign for i in range(3))
        target = (x + ax + 8) % 8 * 16 + (y + ay + 4) % 4 * 4 + (z + az + 4) % 4
        return jnp.where(spot == target, 1.0, 0.0).astype(BF16)

    def spread_rows(which, value):
        rows[which] = jnp.concatenate([value] * 4, axis=0).T

    def halves(ref, order, which):
        cells = ref[...]
        parts = jnp.concatenate([cells // 256, cells % 256], axis=0).astype(F32).astype(BF16)
        moved = jnp.dot(parts, order, preferred_element_type=F32)
        spread_rows(which, moved[0:32])
        spread_rows(which + 1, moved[32:64])

    halves(fs_ref, order_of(1), 0)
    source_order = order_of(-1)
    halves(fr_ref, source_order, 2)
    high, low = split(ft_ref[...])
    lowest = (ft_ref[...] - high.astype(F32) - low.astype(F32)).astype(BF16)
    moved = jnp.dot(
        jnp.concatenate([high, low, lowest], axis=0), source_order, preferred_element_type=F32
    )
    spread_rows(4, moved[0:32] + moved[32:64] + moved[64:96])

    def flat(which, half):
        lane = lanes((16, 128))
        pieces = [rows[which, pl.ds(half * 4 + q, 16, stride=8), :] for q in range(4)]
        total = pieces[0]
        for q in range(1, 4):
            total = jnp.where(lane // 32 == q, pieces[q], total)
        return total

    def mask(hi, p):
        one = jnp.where(hi == float(p), 1.0, 0.0)
        return jnp.concatenate([one, one], axis=0).astype(BF16)

    column = lax.broadcasted_iota(jnp.int32, (256, 128), 0).astype(F32)

    def one_hot(low):
        return jnp.where(column == low, 1.0, 0.0).astype(BF16)

    for half in range(2):
        send_hi, send_lo, recv_hi, recv_lo, recv_weight = (flat(i, half) for i in range(5))
        part = slice(half * 128, half * 128 + 128)
        for j in range(16):
            this = slice(j, j + 1)
            quad = jnp.floor(send_hi[this] * 0.5)
            his[j, :, part] = jnp.broadcast_to(quad, (8, 128))
            low = send_lo[this] + (send_hi[this] - 2.0 * quad) * 256.0
            ohs[j, half, 0:256] = one_hot(low)
            ohs[j, half, 256:512] = one_hot(low - 256.0)
            place_in = slice((j % 4) * 256 + half * 128, (j % 4) * 256 + half * 128 + 128)
            hi = jnp.broadcast_to(recv_hi[this], (8, 128))
            hir[j // 4, :, place_in] = hi
            ohr[2 * j + half] = one_hot(recv_lo[this])
            edge[j // 4, :, place_in] = jnp.broadcast_to(recv_weight[this], (8, 128))
    lane = lanes((1, 128))
    line = lane % 64
    first = (line % 2) * 128
    near, far = jnp.where(lane < 64, 127, 0), jnp.where(lane < 64, 0, 127)
    hi = jnp.broadcast_to((line // 2).astype(F32), (8, 128))
    hiz[...] = hi
    ohr[32] = one_hot((first + far).astype(F32))
    his[16, :, 0:128] = jnp.broadcast_to((line // 4).astype(F32), (8, 128))
    low = ((line % 4) * 128 + near).astype(F32)
    ohs[16, 0, 0:256] = one_hot(low)
    ohs[16, 0, 256:512] = one_hot(low - 256.0)
    tsend[0:1, 0:64] = wells_ref[...].astype(F32)
    twice = tsend[0:1]
    well = jnp.where(lane < 64, twice, pltpu.roll(twice, 64, 1)).astype(jnp.int32)
    well_x, well_y, well_z = well // 32768, well // 512 % 64, well % 512
    owned = (well_x // 4 == ax) & (well_y // 16 == ay) & (well_z // 128 == az)
    cell = (well_x % 4 * 16 + well_y % 16) * 128 + well_z % 128
    hiw[...] = jnp.broadcast_to(jnp.where(owned, cell // 256, -1).astype(F32), (8, 128))
    ohw[...] = one_hot((cell % 256).astype(F32))

    def begin(i, carry):
        for u in range(4):
            p = 4 * i + u
            for parity in range(2):
                res[p, :, parity * 128 : parity * 128 + 128] = start_ref[
                    pl.ds(2 * p + parity, 16, stride=64), :
                ]
        return carry

    lax.fori_loop(0, 8, begin, 0)
    pair = lax.broadcasted_iota(jnp.int32, (32, 1024), 0).astype(F32)
    total = jnp.zeros((64, 256), F32)
    for j in range(4):
        weight = jnp.broadcast_to(edge[j, 0:1, :], (32, 1024))
        hit = pair == jnp.broadcast_to(hir[j, 0:1, :], (32, 1024))
        high, low = split(jnp.where(hit, weight, 0.0))
        total = total + dot_nt(
            jnp.concatenate([high, low], axis=0),
            jnp.concatenate([ohr[8 * j + h] for h in range(8)], axis=1),
        )
    fault = total[0:32] + total[32:64]
    acc[0:32, 0, :] = fault

    for x in range(4):
        tsend[x : x + 1] = ty_ref[x * 16 + 15 : x * 16 + 16]
    tsend[4:8] = jnp.zeros((4, 128), F32)
    pl.semaphore_wait(barrier, 127)
    faces = (
        copy(tx_ref.at[pl.ds(48, 16)], trecv.at[pl.ds(0, 16)], tssem.at[0], trsem.at[0], up_x),
        copy(tsend, trecv.at[pl.ds(16, 8)], tssem.at[1], trsem.at[1], up_y),
        copy(tz_ref, trecv.at[pl.ds(24, 64)], tssem.at[2], trsem.at[2], up_z),
    )
    for face in faces:
        face.start()
    shift = table_ref[0]
    for i in range(1, 16):
        shift = jnp.where(index_ref[0] == i, table_ref[i], shift)
    for face in faces:
        face.wait()
    lane = lanes((16, 128))
    row = lax.broadcasted_iota(jnp.int32, (16, 128), 0)
    inside = [jnp.where(p > 0, 1.0, 0.0) for p in place]
    outside = [jnp.where(p < n - 1, 1.0, 0.0) for p, n in zip(place, (8, 4, 4))]
    for x in range(4):
        these = slice(x * 16, x * 16 + 16)
        upper_x = tx_ref[these] * (outside[0] if x == 3 else 1.0)
        if x == 0:
            lower_x = trecv[0:16] * inside[0]
        else:
            lower_x = tx_ref[(x - 1) * 16 : x * 16]
        ty = ty_ref[these]
        upper_y = jnp.where(row == 15, ty * outside[1], ty)
        lower_y = jnp.where(
            row == 0, trecv[16 + x : 17 + x] * inside[1], pltpu.roll(ty, 1, 0)
        )
        tz = tz_ref[these]
        upper_z = jnp.where(lane == 127, tz * outside[2], tz)
        lower_z = jnp.where(
            lane == 0,
            pltpu.roll(trecv[24 + x * 16 : 40 + x * 16], 1, 1) * inside[2],
            pltpu.roll(tz, 1, 1),
        )
        coef[0, these] = upper_x
        coef[1, these] = lower_x
        coef[2, these] = upper_y
        coef[3, these] = lower_y
        coef[4, these] = upper_z
        coef[5, these] = lower_z
        coef[6, these] = (
            upper_x + lower_x + upper_y + lower_y + upper_z + lower_z + shift * pv_ref[these]
        )
    for p in range(32):
        for parity in range(2):
            r = 2 * p + parity
            coef[6, r : r + 1] += acc[p, 0:1, parity * 128 : parity * 128 + 128]
    coef[7] = 1.0 / coef[6]
    both = jnp.concatenate([coef[5], coef[4]], axis=0).T
    lane = lanes((1, 128))
    edge[4, :, 0:128] = jnp.broadcast_to(
        jnp.where(lane < 64, both[0:1], both[127:128]), (8, 128)
    )
    lane = lanes((64, 128))
    coef[4] = jnp.where(lane == 127, 0.0, coef[4])
    coef[5] = jnp.where(lane == 0, 0.0, coef[5])

    def initial(i, carry):
        for u in range(4):
            p = 4 * i + u
            for parity in range(2):
                part = slice(parity * 128, parity * 128 + 128)
                inverse = jnp.broadcast_to(coef[7, pl.ds(2 * p + parity, 1)], (16, 128))
                d = res[p, :, part] * inverse
                dpad[0, 1 + i // 2, 1 + (i % 2) * 8 + 2 * u + parity] = d
                dbf[u % 2 * 2 + parity, pl.ds(pl.multiple_of((2 * i + u // 2) * 16, 16), 16)] = d.astype(BF16)
                xacc[p, :, part] = jnp.zeros_like(d)
        return carry

    lax.fori_loop(0, 8, initial, 0)

    def pick(source, one_hot, hi_of, width, count):
        product = jnp.dot(source, one_hot, preferred_element_type=F32)
        tiles = []
        for h in range(width // 128):
            part = slice(h * 128, h * 128 + 128)
            hi = hi_of(part)
            first = jnp.zeros((8, 128), F32)
            second = jnp.zeros((8, 128), F32)
            for p in range(count):
                hit = hi == float(p)
                first = jnp.where(hit, product[p * 16 : p * 16 + 8, part], first)
                second = jnp.where(hit, product[p * 16 + 8 : p * 16 + 16, part], second)
            tiles.append((first, second))
        return tiles

    def gather(j, width):
        picks = [ohs[j, h] for h in range(width // 128)]
        return pick(
            jnp.concatenate([dbf[q] for q in range(4)], axis=1),
            picks[0] if len(picks) == 1 else jnp.concatenate(picks, axis=1),
            lambda part: his[j, :, part], width, 16,
        )

    def scatter(j, tiles):
        values = []
        for h, (first, second) in enumerate(tiles):
            weight = edge[j, :, h * 128 : h * 128 + 128]
            values.append(jnp.concatenate([first * weight, second * weight], axis=0).astype(BF16))
        picks = [ohr[8 * j + h] for h in range(len(values))]
        picks = picks[0] if len(picks) == 1 else jnp.concatenate(picks, axis=1)
        sums = []
        for side in range(2):
            placed = [
                jnp.concatenate([mk[8 * j + h, side * 16 + p] * value for p in range(16)], axis=0)
                for h, value in enumerate(values)
            ]
            placed = placed[0] if len(placed) == 1 else jnp.concatenate(placed, axis=1)
            sums.append(dot_nt(placed, picks).reshape(16, 16, 256))
        return sums

    exchange = copy(gsend.at[pl.ds(0, 127)], grecv.at[pl.ds(0, 127)], gs1, gr1, place)
    spread = copy(gsend.at[pl.ds(0, 127)], gall.at[pl.ds(0, 127)], gs2, gr2, place)

    def permute(t):
        a = lax.broadcasted_iota(jnp.int32, (256, 256), 0)
        b = lax.broadcasted_iota(jnp.int32, (256, 256), 1)
        order = jnp.where(b == a % 16 * 16 + a // 16, 1.0, 0.0).astype(BF16)

        def block(i, carry):
            k = jnp.where(t == 0, 0, t * 6 - 2) + i
            for q in range(2):
                sides = []
                for side in range(2):
                    base = k * 1024 + (2 * q + side) * 16
                    sides.append(
                        jnp.concatenate(
                            [bas[pl.ds(pl.multiple_of(base + 64 * kk, 16), 16), :] for kk in range(16)],
                            axis=0,
                        )
                    )
                turned = jnp.dot(
                    order, jnp.concatenate(sides, axis=1), preferred_element_type=F32
                ).astype(BF16)
                for side in range(2):
                    for xx in range(16):
                        r = (2 * q + side) * 16 + xx
                        bt[r // 2, pl.ds(pl.multiple_of(k * 16, 16), 16), r % 2 * 128 : r % 2 * 128 + 128] = (
                            turned[xx * 16 : xx * 16 + 16, side * 128 : side * 128 + 128]
                        )
            return carry

        lax.fori_loop(0, jnp.where(t == 0, 4, 6), block, 0)

    def iterate(t, carry):
        now, gain = carry
        par = t % 2
        here = dpad.at[par]
        halos = [
            copy(here.at[4, pl.ds(1, 16)], here.at[0, pl.ds(1, 16)], hssem.at[0], hrsem.at[par, 0], up_x),
            copy(here.at[1, pl.ds(1, 16)], here.at[5, pl.ds(1, 16)], hssem.at[1], hrsem.at[par, 1], down_x),
            copy(here.at[pl.ds(1, 4), 16], here.at[pl.ds(1, 4), 0], hssem.at[2], hrsem.at[par, 2], up_y),
            copy(here.at[pl.ds(1, 4), 1], here.at[pl.ds(1, 4), 17], hssem.at[3], hrsem.at[par, 3], down_y),
        ]
        for halo in halos:
            halo.start()

        def stencil(r):
            x, y = 1 + r // 16, 1 + r % 16
            p, part = r // 2, slice(r % 2 * 128, r % 2 * 128 + 128)
            d = here[x, y]
            xacc[p, :, part] += d

            def times(which, value):
                return jnp.broadcast_to(coef[which, r : r + 1], (16, 128)) * value

            total = times(4, pltpu.roll(d, 127, 1)) + times(5, pltpu.roll(d, 1, 1))
            for which, inside_too, near in (
                (0, x < 4, (x + 1, y)), (1, x > 1, (x - 1, y)), (2, y < 16, (x, y + 1)), (3, y > 1, (x, y - 1))
            ):
                if inside_too:
                    total = total + times(which, here[near])
            res[p, :, part] = res[p, :, part] - (times(6, d) - total)

        halos_z = [
            copy(zsend.at[0], zrecv.at[par, 0], hssem.at[4], hrsem.at[par, 4], up_z),
            copy(zsend.at[1], zrecv.at[par, 1], hssem.at[5], hrsem.at[par, 5], down_z),
        ]
        for group in (range(0, 2), range(2, 8), range(8, 16)):
            for j in group:
                for h, (first, second) in enumerate(gather(j, 256)):
                    first, second = half_swap(first, second)
                    first, second = quarter_swap(first), quarter_swap(second)
                    base = j * 8 + h * 4
                    send[base] = first[0:4]
                    send[base + 1] = first[4:8]
                    send[base + 2] = second[0:4]
                    send[base + 3] = second[4:8]
            if group[0] == 8:
                ((first, second),) = gather(16, 128)
                first, second = half_swap(first, second)
                zsend[0] = first
                zsend[1] = second
                for halo in halos_z:
                    halo.start()
            for slot in range(group[0] * 8, min(group[-1] * 8 + 8, 127)):
                copy(
                    send.at[slot], recv.at[par, slot], ssem, rsem.at[par, slot // 32], peer(SLOTS[slot])
                ).start()
        recv[par, 127] = send[127]
        for r in range(64):
            stencil(r)
        @pl.when(t == 0)
        def _():
            fetch.wait()

            def build(c, carry):
                for h in range(8):
                    hi = hir[c, :, h * 128 : h * 128 + 128]
                    for p in range(32):
                        mk[8 * c + h, p] = mask(hi, p)
                return carry

            lax.fori_loop(0, 4, build, 0)
            hi = hiz[...]
            for p in range(32):
                mk[32, p] = mask(hi, p)

        @pl.when(t < 3)
        def _():
            permute(t)

        @pl.when(t == 3)
        def _():
            gfull[...] = jnp.zeros_like(gfull)

            def add(i, carry):
                total = gfull[...]
                for u in range(4):
                    total = total + dot_nt(bt[4 * i + u], bt[4 * i + u])
                gfull[...] = total
                return carry

            lax.fori_loop(0, 8, add, 0)
            gmat[0] = gfull[0:128, 0:128]
            gmat[1] = gfull[0:128, 128:256]
            gmat[2] = gfull[128:256, 128:256]

        @pl.when(t == 4)
        def _():
            gfull[:, 0:128] = jnp.zeros((256, 128), F32)

            def at_wells(i, carry):
                total = gfull[:, 0:128]
                for u in range(4):
                    p = 4 * i + u
                    hit = hiw[0:1] == lax.convert_element_type(p, F32)
                    found = jnp.dot(bt[p], ohw[...], preferred_element_type=F32)
                    total = total + jnp.where(hit, found, 0.0)
                gfull[:, 0:128] = total
                return carry

            lax.fori_loop(0, 8, at_wells, 0)
            gmat[3] = jnp.where(
                lanes((128, 128)) < 64, gfull[0:128, 0:128], gfull[128:256, 0:128]
            )

        @pl.when(t == 5)
        def _():
            for c in range(128):
                gsend[c] = gmat[c // 32, c % 32 * 4 : c % 32 * 4 + 4]
            for offset in SLOTS[:127]:
                copy(gsend.at[number(offset)], grecv.at[me], gs1, gr1, peer(offset)).start()
            grecv[me] = gsend[me]

        @pl.when(t == 6)
        def _():
            exchange.wait_recv()
            gsum[...] = jnp.sum(grecv[...], axis=0)
            for offset in SLOTS[:127]:
                copy(gsum, gall.at[me], gs2, gr2, peer(offset)).start()
            gall[me] = gsum[...]

        for halo in halos_z:
            halo.wait_recv()
        for side, value in enumerate(scatter(4, [half_swap(zrecv[par, 0], zrecv[par, 1])])):
            acc[side * 16 : side * 16 + 16] = value
        for j in (3, 2, 1, 0):
            if j == 0:
                for halo in halos:
                    halo.wait_recv()

                for y in range(16):
                    for x, which, beyond in ((0, 1, 0), (3, 0, 5)):
                        r = x * 16 + y
                        p, part = r // 2, slice(r % 2 * 128, r % 2 * 128 + 128)
                        res[p, :, part] += jnp.broadcast_to(coef[which, r : r + 1], (16, 128)) * here[beyond, 1 + y]
                for x in range(4):
                    for y, which, beyond in ((0, 3, 0), (15, 2, 17)):
                        r = x * 16 + y
                        p, part = r // 2, slice(r % 2 * 128, r % 2 * 128 + 128)
                        res[p, :, part] += jnp.broadcast_to(coef[which, r : r + 1], (16, 128)) * here[1 + x, beyond]
            count = 32 if j < 3 else 31
            copy(
                send.at[pl.ds(0, count)], recv.at[par, pl.ds(0, count)], ssem, rsem.at[par, j], place
            ).wait_recv()
            tiles = []
            for h in range(8):
                base = j * 32 + h * 4
                first = jnp.concatenate([recv[par, base], recv[par, base + 1]], axis=0)
                second = jnp.concatenate([recv[par, base + 2], recv[par, base + 3]], axis=0)
                tiles.append(half_swap(quarter_swap(first), quarter_swap(second)))
            sums = scatter(j, tiles)
            if j:
                for side, value in enumerate(sums):
                    acc[side * 16 : side * 16 + 16] += value
        for r in range(64):
            p, part = r // 2, slice(r % 2 * 128, r % 2 * 128 + 128)
            residual = res[p, :, part] + acc[p, :, part] + sums[p // 16][p % 16, :, part]
            res[p, :, part] = residual
            inverse = jnp.broadcast_to(coef[7, r : r + 1], (16, 128))
            x, y = 1 + r // 16, 1 + r % 16
            d = now * here[x, y] + gain * (residual * inverse)
            dpad[1 - par, x, y] = d
            dbf[r % 4, r // 4 * 16 : r // 4 * 16 + 16] = d.astype(BF16)
        for halo in halos + halos_z:
            halo.wait_send()
        copy(send.at[pl.ds(0, 127)], recv.at[par, pl.ds(0, 127)], ssem, rsem.at[par, 0], place).wait_send()
        nxt_now, nxt_gain = carry
        for step in range(TERMS - 2):
            nxt_now = jnp.where(t == step, weights()[step + 1][0], nxt_now)
            nxt_gain = jnp.where(t == step, weights()[step + 1][1], nxt_gain)
        return nxt_now, nxt_gain

    lax.fori_loop(
        0, TERMS - 1, iterate, (jnp.float32(weights()[0][0]), jnp.float32(weights()[0][1]))
    )

    def project(i, total):
        for u in range(8):
            p = 8 * i + u
            d = jnp.concatenate([dpad[1, 1 + i, 1 + 2 * u], dpad[1, 1 + i, 2 + 2 * u]], axis=1)
            x = xacc[p] + d
            xacc[p] = x
            high, low = split(x)
            parts = jnp.concatenate([high, low], axis=0)
            rest[p] = parts
            total = total + dot_nt(parts, bt[p])
        return total

    total = lax.fori_loop(0, 4, project, jnp.zeros((32, 256), F32))
    for c in range(32):
        csend[c] = total[c % 16 * 2 : c % 16 * 2 + 2, c // 16 * 128 : c // 16 * 128 + 128]
    mine = ax * 4 + ay
    for offset in [o for o in SLOTS if o[2] == 0]:
        x, y = xs[offset[0]], ys[offset[1]]
        to = copy(csend.at[x * 4 + y], crecv.at[me], cs1, cr1, (x, y, y))
        if offset[:2] != (0, 0):
            to.start()
        else:

            @pl.when(az != ay)
            def _(to=to):
                to.start()

    ((first_w, second_w),) = pick(
        rest[:, 0:16].reshape(512, 256), ohw[...], lambda part: hiw[...], 128, 32
    )
    ((low_first, low_second),) = pick(
        rest[:, 16:32].reshape(512, 256), ohw[...], lambda part: hiw[...], 128, 32
    )
    packed, _ = half_swap(first_w + low_first, second_w + low_second)
    for c in range(4):
        wsend[c] = packed[2 * c : 2 * c + 2]
    for c in range(4):

        @pl.when(~((ax == 2 * c) & (ay == c) & (az == (c + 1) % 4)))
        def _(c=c):
            copy(wsend.at[c], wrecv.at[me], ws1, wr1, (2 * c, c, (c + 1) % 4)).start()

    owner = (ax == 2 * ay) & (az == (ay + 1) % 4)

    @pl.when(owner)
    def _():
        wrecv[me] = wsend[ay]
        copy(wrecv.at[pl.ds(0, 127)], wrecv.at[pl.ds(0, 127)], ws1, wr1, place).wait_recv()
        wsum[...] = jnp.sum(wrecv[...], axis=0)
        for offset in SLOTS[:127]:
            copy(wsum, wall.at[ay], ws2, wr2, peer(offset)).start()
        wall[ay] = wsum[...]

    spread.wait_recv()
    for c in range(128):
        gmat[c // 32, c % 32 * 4 : c % 32 * 4 + 4] = gall[c]

    @pl.when(az == ay)
    def _():
        crecv[me] = csend[mine]
        copy(crecv.at[pl.ds(0, 127)], crecv.at[pl.ds(0, 127)], cs1, cr1, place).wait_recv()
        csum[...] = jnp.sum(crecv[...], axis=0)
        for offset in SLOTS[:127]:
            copy(csum, call.at[mine], cs2, cr2, peer(offset)).start()
        call[mine] = csum[...]
        copy(call.at[pl.ds(0, 31)], call.at[pl.ds(0, 31)], cs2, cr2, place).wait_recv()

    @pl.when(az != ay)
    def _():
        copy(call, call, cs2, cr2, place).wait_recv()

    for c in range(32):
        cmat[c % 16 * 2 : c % 16 * 2 + 2, c // 16 * 128 : c // 16 * 128 + 128] = call[c]
    leading = cmat[0:16]
    first = leading.astype(BF16)
    exact = dict(precision=lax.Precision.HIGHEST)
    wide = first.astype(F32)
    near, far = wide[:, 0:128], wide[:, 128:256]
    taken = jnp.concatenate(
        [
            jnp.dot(near, gmat[0], preferred_element_type=F32, **exact) + dot_nt(far, gmat[1], **exact),
            jnp.dot(near, gmat[1], preferred_element_type=F32, **exact)
            + jnp.dot(far, gmat[2], preferred_element_type=F32, **exact),
        ],
        axis=1,
    )
    second_sum = leading + cmat[16:32] - taken
    both = jnp.concatenate([first, second_sum.astype(BF16)], axis=0)
    first_ref[...] = leading
    coeffs_ref[...] = leading + second_sum

    def subtract(i, total):
        for u in range(8):
            p = 8 * i + u
            taken = jnp.dot(both, bt[p], preferred_element_type=F32)
            left = xacc[p] - taken[0:16] - taken[16:32]
            high, low = split(left)
            parts = jnp.concatenate([high, low], axis=0)
            rest[p] = parts
            total = total + dot_nt(parts, parts)
        return total

    total = lax.fori_loop(0, 4, subtract, jnp.zeros((32, 32), F32))
    keep = pltpu.make_async_copy(rest, rest_ref, ksem)
    keep.start()
    gram = total[0:16, 0:16] + total[0:16, 16:32] + total[16:32, 0:16]
    lane = lanes((8, 128))
    wide = jnp.concatenate([gram, jnp.zeros((16, 112), F32)], axis=1)
    row = lax.broadcasted_iota(jnp.int32, (8, 128), 0)
    for half in range(2):
        value = wide[half * 8 : half * 8 + 8]
        line = jnp.zeros((1, 128), F32)
        for i in range(8):
            line = line + pltpu.roll(value[i : i + 1], 16 * i, 1)
        qsend[half : half + 1] = line
    for offset in SLOTS[:127]:
        copy(qsend, qrecv.at[me], qs, qr, peer(offset)).start()
    qrecv[me] = qsend[...]

    copy(qrecv.at[pl.ds(0, 127)], qrecv.at[pl.ds(0, 127)], qs, qr, place).wait_recv()
    sums = jnp.sum(qrecv[...], axis=0)
    pieces = []
    for half in range(2):
        for i in range(8):
            pieces.append(pltpu.roll(sums[half : half + 1], (128 - 16 * i) % 128, 1))
    gram = jnp.concatenate(pieces, axis=0)
    lane = lanes((16, 128))
    row = lax.broadcasted_iota(jnp.int32, (16, 128), 0)
    table = jnp.where(lane < 16, gram, jnp.where(lane == row + 16, 1.0, 0.0))
    for j in range(15):
        column = jnp.broadcast_to(table[:, j : j + 1], (16, 128))
        factor = jnp.where(row > j, column / column[j : j + 1], 0.0)
        table = table - factor * table[j : j + 1]
    pivot = jnp.sum(jnp.where(lane == row, table, 0.0), axis=1, keepdims=True)
    scale = 1024.0 / jnp.sqrt(pivot)
    inverse = table[:, 16:32] * scale
    high, low = split(inverse)
    factors_ref[...] = jnp.concatenate([high, low, high], axis=1)

    @pl.when(owner)
    def _():
        copy(wall.at[pl.ds(0, 3)], wall.at[pl.ds(0, 3)], ws2, wr2, place).wait_recv()

    @pl.when(jnp.logical_not(owner))
    def _():
        copy(wall, wall, ws2, wr2, place).wait_recv()

    packed = jnp.concatenate([wall[c] for c in range(4)], axis=0)
    at_wells = jnp.where(lanes((16, 128)) < 64, jnp.concatenate([packed, pltpu.roll(packed, 64, 1)], axis=0), 0.0)
    at_basis = gmat[3].astype(BF16)
    taken = jnp.dot(both[:, 0:128], at_basis, preferred_element_type=F32) + pltpu.roll(
        jnp.dot(both[:, 128:256], at_basis, preferred_element_type=F32), 64, 1
    )
    at_wells = jnp.where(lanes((16, 128)) < 64, at_wells - taken[0:16] - taken[16:32], 0.0)
    answer = jnp.dot(inverse, at_wells, precision=lax.Precision.HIGHEST, preferred_element_type=F32)
    resp_ref[...] = answer[:, 0:64]
    keep.wait()
    exchange.wait_send()
    copy(gall.at[pl.ds(0, 127)], gall.at[pl.ds(0, 127)], gs2, gr2, place).wait_send()
    copy(qrecv.at[pl.ds(0, 127)], qrecv.at[pl.ds(0, 127)], qs, qr, place).wait_send()

    @pl.when(az == ay)
    def _():
        copy(call.at[pl.ds(0, 31)], call.at[pl.ds(0, 31)], cs1, cr1, place).wait_send()
        copy(crecv.at[pl.ds(0, 127)], crecv.at[pl.ds(0, 127)], cs2, cr2, place).wait_send()

    @pl.when(az != ay)
    def _():
        copy(call, call, cs1, cr1, place).wait_send()

    @pl.when(owner)
    def _():
        copy(wall.at[pl.ds(0, 3)], wall.at[pl.ds(0, 3)], ws1, wr1, place).wait_send()
        copy(wrecv.at[pl.ds(0, 127)], wrecv.at[pl.ds(0, 127)], ws2, wr2, place).wait_send()

    @pl.when(jnp.logical_not(owner))
    def _():
        copy(wall, wall, ws1, wr1, place).wait_send()


def solve(*args):
    vmem = pl.BlockSpec(memory_space=pltpu.VMEM)
    smem = pl.BlockSpec(memory_space=pltpu.SMEM)
    dma = pltpu.SemaphoreType.DMA
    return pl.pallas_call(
        solve_kernel,
        out_shape=(
            jax.ShapeDtypeStruct((32, 32, 256), BF16),
            jax.ShapeDtypeStruct((16, 48), BF16),
            jax.ShapeDtypeStruct((16, 256), F32),
            jax.ShapeDtypeStruct((16, 256), F32),
            jax.ShapeDtypeStruct((16, 64), F32),
        ),
        in_specs=[vmem, pl.BlockSpec(memory_space=pl.ANY)] + [vmem] * 4 + [smem] * 2 + [vmem] * 5,
        out_specs=(pl.BlockSpec(memory_space=pl.ANY),) + (vmem,) * 4,
        scratch_shapes=[
            pltpu.VMEM((2, 6, 18, 16, 128), F32),
            pltpu.VMEM((4, 256, 128), BF16),
            pltpu.VMEM((32, 16, 256), F32),
            pltpu.VMEM((32, 16, 256), F32),
            pltpu.VMEM((32, 16, 256), F32),
            pltpu.VMEM((17, 2, 512, 128), BF16),
            pltpu.VMEM((33, 256, 128), BF16),
            pltpu.VMEM((17, 8, 256), F32),
            pltpu.VMEM((4, 8, 1024), F32),
            pltpu.VMEM((8, 128), F32),
            pltpu.VMEM((33, 32, 16, 128), BF16),
            pltpu.VMEM((128, 4, 128), F32),
            pltpu.VMEM((2, 128, 4, 128), F32),
            pltpu.VMEM((2, 8, 128), F32),
            pltpu.VMEM((2, 2, 8, 128), F32),
            pltpu.VMEM((8, 64, 128), F32),
            pltpu.VMEM((5, 8, 1024), F32),
            pltpu.VMEM((5, 128, 128), F32),
            pltpu.VMEM((8, 128), F32),
            pltpu.VMEM((88, 128), F32),
            pltpu.VMEM((16384, 128), BF16),
            pltpu.VMEM((32, 256, 256), BF16),
            pltpu.VMEM((32, 32, 256), BF16),
            pltpu.VMEM((4, 128, 128), F32),
            pltpu.VMEM((256, 256), F32),
            pltpu.VMEM((128, 4, 128), F32),
            pltpu.VMEM((128, 4, 128), F32),
            pltpu.VMEM((128, 4, 128), F32),
            pltpu.VMEM((4, 128), F32),
            pltpu.VMEM((32, 2, 128), F32),
            pltpu.VMEM((128, 2, 128), F32),
            pltpu.VMEM((32, 2, 128), F32),
            pltpu.VMEM((2, 128), F32),
            pltpu.VMEM((2, 128), F32),
            pltpu.VMEM((128, 2, 128), F32),
            pltpu.VMEM((4, 2, 128), F32),
            pltpu.VMEM((128, 2, 128), F32),
            pltpu.VMEM((4, 2, 128), F32),
            pltpu.VMEM((2, 128), F32),
            pltpu.VMEM((256, 128), BF16),
            pltpu.VMEM((8, 128), F32),
            pltpu.VMEM((32, 256), F32),
            dma,
            dma((2, 4)),
            dma((6,)),
            dma((2, 6)),
            dma((3,)),
            dma((3,)),
        ]
        + [dma] * 16,
        compiler_params=pltpu.CompilerParams(
            collective_id=0, has_side_effects=True, vmem_limit_bytes=60 * 1024 * 1024
        ),
    )(*args)


def finish_kernel(
    rest_ref, factors_ref, first_in, coeffs_in, resp_in, out_ref, first_ref, coeffs_ref, resp_ref
):
    first_ref[...] = first_in[...]
    coeffs_ref[...] = coeffs_in[...]
    resp_ref[...] = resp_in[...]
    factors = factors_ref[...]

    def finish(i, carry):
        for u in range(4):
            p = 4 * i + u
            parts = rest_ref[p]
            block = jnp.dot(
                factors, jnp.concatenate([parts[0:16], parts[0:16], parts[16:32]], axis=0),
                preferred_element_type=F32,
            )
            for parity in range(2):
                out_ref[pl.ds(2 * p + parity, 16, stride=64), :] = block[
                    :, parity * 128 : parity * 128 + 128
                ]
        return carry

    lax.fori_loop(0, 8, finish, 0)


def finish(*args):
    vmem = pl.BlockSpec(memory_space=pltpu.VMEM)
    return pl.pallas_call(
        finish_kernel,
        out_shape=(
            jax.ShapeDtypeStruct((1024, 128), F32),
            jax.ShapeDtypeStruct((16, 256), F32),
            jax.ShapeDtypeStruct((16, 256), F32),
            jax.ShapeDtypeStruct((16, 64), F32),
        ),
        in_specs=[vmem] * 5,
        out_specs=(vmem,) * 4,
    )(*args)


def local(
    start_block, basis, trans_x, trans_y, trans_z, pore_volume, shift_table, shift_index,
    fault_send, fault_recv, fault_trans, well_cells,
):
    wells = well_cells.reshape(1, 64)
    offsets = np.zeros((8, 128), np.int32)
    offsets[0:3] = np.array(SLOTS, np.int32).T
    parts = solve(
        start_block.reshape(1024, 128),
        basis.reshape(16384, 128),
        trans_x.reshape(64, 128),
        trans_y.reshape(64, 128),
        trans_z.reshape(64, 128),
        pore_volume.reshape(64, 128),
        shift_table,
        shift_index,
        fault_send[0].T,
        fault_recv[0].T,
        fault_trans[0].T,
        wells,
        jnp.asarray(offsets),
    )
    new_block, first_coeffs, coeffs, well_resp = finish(*parts)
    return new_block.reshape(start_block.shape), first_coeffs.T, coeffs.T, well_resp.T


def solution(mesh):
    in_specs = (
        P(None, "gx", "gy", "gz"),
        P(None, "gx", "gy", "gz"),
        P("gx", "gy", "gz"),
        P("gx", "gy", "gz"),
        P("gx", "gy", "gz"),
        P("gx", "gy", "gz"),
        P(),
        P(),
        P(("gx", "gy", "gz"), None, None),
        P(("gx", "gy", "gz"), None, None),
        P(("gx", "gy", "gz"), None, None),
        P(),
    )
    out_specs = (P(None, "gx", "gy", "gz"), P(), P(), P())
    return jax.shard_map(local, mesh=mesh, in_specs=in_specs, out_specs=out_specs, check_vma=False)
```
